32 devices in a mesh: src: 16 (over z, y, x), ccd: 2 (over core).
Axes of the slice: x: 2, y: 2, z: 4, core: 2. Of those that a mesh axis runs over, the one named last changes fastest.
Arguments:
- design: float32 [5, 262144], P(None, ('src', 'ccd')), may hold values from -6 to 6
- observed: float32 [262144], P(('src', 'ccd')), may hold values from -12 to 12
- weight: float32 [262144], P(('src', 'ccd')), may hold values from 0.25 to 4
- phase_frac: float32 [262144], P(('src', 'ccd')), may hold values from 0 to 1
- axis_factors: float32 [3, 262144], P(None, ('src', 'ccd')), may hold values from -6 to 6
- source_index: int32 [262144], P(('src', 'ccd')), may hold values from 0 to 1023
- knot_index: int32 [262144], P(('src', 'ccd')), may hold values from 0 to 127
- counts: int32 [16, 2, 16], P('src', 'ccd'), may hold values from 1 to 512, as said below
Outputs:
- source_params: float32 [5, 16384], P(None, 'src')
- attitude: float32 [3, 2048], P(None, 'src')
- residual: float32 [262144], P(('src', 'ccd'))
The draws below stay inside these ranges and needn't reach their ends.
Inputs may be any that keep to these rules, and one draw needn't show every extreme that they name: Slot l of device (p, c) is live when l % 512 < counts[p, c, l // 512]; every device has one full block of 512 live slots, and one time shard receives full blocks from every device.
All inputs are finite; a program needn't handle non-finite values.
Results may differ from the reference program's by a relative error of at most 0.0003.
Values sent between devices are 32-bit elements; how exact they have to be, the bound alone decides.
No kernel may reach another device: no remote copies, remote signals or barrier semaphores. Data moves between devices by JAX's collectives and lax.ppermute only.
A program may use at most 64 MiB of HBM per device.

```python
import math
import jax
import jax.numpy as jnp
from jax import lax

ROWS_DEV = 8192
SRC_DEV = 1024
KNOT_DEV = 128
ITERS = 3
SHARDS = 16
CCDS = 2
CAP = 512
KNOTS = 2048
ROWS = 262144
N_SRC = 16
N_CCD = 2


def draw_counts(key, part):
    subkeys = jax.random.split(jax.random.fold_in(key, 7), 5)
    shape_all = (SHARDS, CCDS, SHARDS)
    heavy_dest = jax.random.randint(subkeys[0], (SHARDS,), 0, 4) == 0
    light_load = jax.random.randint(subkeys[1], shape_all, 1, CAP // 4 + 2)
    heavy_load = jax.random.randint(subkeys[2], shape_all, max(CAP // 2, 1), CAP + 1)
    block_loads = jnp.where(heavy_dest[None, None, :], heavy_load, light_load)
    full_dest = jax.random.randint(subkeys[3], (), 0, SHARDS)
    offset = jax.random.randint(subkeys[4], (), 1, SHARDS)
    sender = lax.broadcasted_iota(jnp.int32, shape_all, 0)
    target = lax.broadcasted_iota(jnp.int32, shape_all, 2)
    full_block = (target == full_dest) | (target == (sender + offset) % SHARDS)
    return jnp.minimum(jnp.where(full_block, CAP, block_loads), CAP).astype(jnp.int32)


def set_ends(drawn, rng, smallest, top_value):
    spot = [jax.random.randint(jax.random.fold_in(rng, axis), (), 0, length) for axis, length in enumerate(drawn.shape)]
    widest = drawn.shape.index(max(drawn.shape))
    beside = spot[:widest] + [(spot[widest] + 1) % drawn.shape[widest]] + spot[widest + 1:]
    return drawn.at[tuple(spot)].set(smallest).at[tuple(beside)].set(top_value)


def block_levels(key, shape, cuts, smallest, top_value):
    def one(dim, blocks):
        steps = jax.random.uniform(jax.random.fold_in(jax.random.fold_in(key, 6), dim), (blocks,), jnp.float32, smallest / len(cuts), top_value / len(cuts))
        return jnp.repeat(jnp.exp(steps), shape[dim] // blocks).reshape((-1,) + (1,) * (len(shape) - dim - 1))

    factor_of = one(*cuts[0])
    for cut in cuts[1:]:
        factor_of = factor_of * one(*cut)
    return factor_of


def noise(rng, shape, deviation, limit, pieces=(), kind=jnp.bfloat16):
    drawn = deviation * jax.random.normal(rng, shape, jnp.float32)
    if pieces:
        drawn = drawn * block_levels(rng, shape, pieces, -0.22, 0.18)
    return jnp.clip(drawn, -limit, limit).astype(kind)


def setup_inputs(seed: int = 0) -> dict:
    seeds = jax.random.split(jax.random.key(seed), 9)
    design = noise(seeds[0], (5, ROWS), 1.0, 6.0, ((1, 32),), jnp.float32)
    observed = noise(seeds[1], (ROWS,), 2.0, 12.0, ((0, 32),), jnp.float32)
    weight = jnp.clip(jnp.exp(math.log(4.0) - 2.7725887 * jax.random.uniform(seeds[2], (ROWS,), jnp.float32) ** block_levels(seeds[2], (ROWS,), ((0, 32),), -0.2, 0.2)), 0.25, 4.0)
    phase_frac = jnp.clip(1.0 * jax.random.uniform(seeds[3], (ROWS,), jnp.float32) ** block_levels(seeds[3], (ROWS,), ((0, 32),), -0.2, 0.2), 0.0, 1.0)
    axis_factors = noise(seeds[4], (3, ROWS), 1.0, 6.0, ((1, 32),), jnp.float32)
    source_index = set_ends(jax.random.randint(seeds[5], (ROWS,), 0, SRC_DEV), jax.random.fold_in(seeds[5], 1), 0, SRC_DEV - 1).astype(jnp.int32)
    knot_index = set_ends(jax.random.randint(seeds[6], (ROWS,), 0, KNOT_DEV), jax.random.fold_in(seeds[6], 1), 0, KNOT_DEV - 1).astype(jnp.int32)
    counts = draw_counts(jax.random.fold_in(seeds[8], 71), 0)
    return dict(design=design, observed=observed, weight=weight, phase_frac=phase_frac, axis_factors=axis_factors, source_index=source_index, knot_index=knot_index, counts=counts)


src_ridge = 1.0
att_ridge = 1.0
relax_step = 0.15

def row_moments(design_rows, observed_rows, weight_rows):
    products = []
    for m in range(5):
        for n in range(m, 5):
            products.append(design_rows[m] * design_rows[n] * weight_rows)
    for m in range(5):
        products.append(design_rows[m] * weight_rows * observed_rows)
    return jnp.stack(products)

def solve_small(moments):
    matrix = {}
    position = 0
    for m in range(5):
        for n in range(m, 5):
            matrix[m, n] = moments[position] + (src_ridge if m == n else 0.0)
            position += 1
    factor = {}
    for j in range(5):
        for i in range(j, 5):
            running = matrix[j, i]
            for k in range(j):
                running = running - factor[i, k] * factor[j, k]
            if i == j:
                factor[j, j] = jnp.sqrt(running)
            else:
                factor[i, j] = running / factor[j, j]
    forward = []
    for i in range(5):
        running = moments[15 + i]
        for k in range(i):
            running = running - factor[i, k] * forward[k]
        forward.append(running / factor[i, i])
    solution = [None] * 5
    for i in reversed(range(5)):
        running = forward[i]
        for k in range(i + 1, 5):
            running = running - factor[k, i] * solution[k]
        solution[i] = running / factor[i, i]
    return jnp.stack(solution)

def spline_basis(phase_rows):
    remain = 1.0 - phase_rows
    square = phase_rows * phase_rows
    cube_term = square * phase_rows
    return [remain * remain * remain / 6.0, (3.0 * cube_term - 6.0 * square + 4.0) / 6.0, (-3.0 * cube_term + 3.0 * square + 3.0 * phase_rows + 1.0) / 6.0, cube_term / 6.0]

def spread_ref(row_values, spline_terms, knot_rows):
    running = jnp.zeros((3, KNOTS + 3), jnp.float32)
    for j in range(4):
        running = running + jax.ops.segment_sum((row_values * spline_terms[j]).T, knot_rows + j, num_segments=KNOTS + 3).T
    return running

def predict_ref(padded, spline_terms, axis_rows, knot_rows):
    running = jnp.zeros_like(spline_terms[0])
    for j in range(4):
        running = running + spline_terms[j] * lax.optimization_barrier(jnp.sum(axis_rows * jnp.take(padded, knot_rows + j, axis=1), 0))
    return running

def reference(design, observed, weight, phase_frac, axis_factors, source_index, knot_index, counts):
    shard_rows = N_CCD * ROWS_DEV
    local_row = jnp.arange(ROWS_DEV, dtype=jnp.int32)
    bucket = local_row // CAP
    slot_pos = local_row % CAP
    live_mask = (slot_pos[None, None, :] < counts[:, :, bucket]).astype(jnp.float32).reshape(N_SRC, shard_rows)
    design_sh = design.reshape(5, N_SRC, shard_rows).transpose(1, 0, 2)
    factor_sh = axis_factors.reshape(3, N_SRC, shard_rows).transpose(1, 0, 2)
    observed_sh = observed.reshape(N_SRC, shard_rows)
    weight_sh = weight.reshape(N_SRC, shard_rows) * live_mask
    phase_sh = phase_frac.reshape(N_SRC, shard_rows)
    source_sh = source_index.reshape(N_SRC, shard_rows)
    knot_sh = knot_index.reshape(N_SRC, shard_rows) + jnp.tile(bucket * KNOT_DEV, N_CCD)[None, :]

    def source_step(scan_items):
        design_rows, observed_rows, weight_rows, source_rows, live_rows = scan_items
        moments = jax.ops.segment_sum(row_moments(design_rows, observed_rows, weight_rows).T, source_rows, num_segments=SRC_DEV).T
        params = solve_small(moments)
        fitted = lax.optimization_barrier(jnp.sum(design_rows * jnp.take(params, source_rows, axis=1), 0))
        return (params, live_rows * (observed_rows - fitted))
    params_sh, resid_sh = lax.map(source_step, (design_sh, observed_sh, weight_sh, source_sh, live_mask))
    source_params = params_sh.transpose(1, 0, 2).reshape(5, N_SRC * SRC_DEV)
    zero_knots = jnp.zeros((3, KNOTS + 3), jnp.float32)

    def assemble_step(carried, scan_items):
        factor_rows, weight_rows, phase_rows, knot_rows, resid_rows = scan_items
        spline_terms = spline_basis(phase_rows)
        rhs_part = spread_ref(weight_rows * factor_rows * resid_rows, spline_terms, knot_rows)
        diag_part = spread_ref(weight_rows * factor_rows * factor_rows, [t * t for t in spline_terms], knot_rows)
        return ((carried[0] + rhs_part, carried[1] + diag_part), None)
    (rhs_full, diag_full), _ = lax.scan(assemble_step, (zero_knots, zero_knots), (factor_sh, weight_sh, phase_sh, knot_sh, resid_sh))
    rhs_knots = rhs_full[:, :KNOTS]
    diag_knots = att_ridge + diag_full[:, :KNOTS]
    coefficients = relax_step * rhs_knots / diag_knots
    for iteration in range(1, ITERS):
        padded = jnp.pad(coefficients, ((0, 0), (0, 3)))

        def normal_step(carried, scan_items):
            factor_rows, weight_rows, phase_rows, knot_rows = scan_items
            spline_terms = spline_basis(phase_rows)
            predicted = predict_ref(padded, spline_terms, factor_rows, knot_rows)
            return (carried + spread_ref(weight_rows * factor_rows * predicted, spline_terms, knot_rows), None)
        back_full, _ = lax.scan(normal_step, zero_knots, (factor_sh, weight_sh, phase_sh, knot_sh))
        normal_prod = att_ridge * coefficients + back_full[:, :KNOTS]
        coefficients = coefficients + relax_step * (rhs_knots - normal_prod) / diag_knots
    padded = jnp.pad(coefficients, ((0, 0), (0, 3)))

    def final_step(scan_items):
        factor_rows, phase_rows, knot_rows, resid_rows, live_rows = scan_items
        predicted = predict_ref(padded, spline_basis(phase_rows), factor_rows, knot_rows)
        return live_rows * (resid_rows - predicted)
    residual = lax.map(final_step, (factor_sh, phase_sh, knot_sh, resid_sh, live_mask))
    return (source_params, coefficients, residual.reshape(ROWS))
```

```python
import jax
import jax.numpy as jnp
from jax import lax
from jax.experimental import pallas as pl
from jax.experimental.pallas import tpu as pltpu
from jax.sharding import PartitionSpec as P

SRC_DEV = 1024
KNOT_DEV = 128
ITERS = 3
LANES = 128
SUB = 8
LOW = 256
SIGNALS = 15 + 5
PAIRS = [(x, y) for x in range(3) for y in range(x, 3)]

src_ridge = 1.0
att_ridge = 1.0
relax_step = 0.15

f32 = jnp.float32
bf16 = jnp.bfloat16


def bernstein_products():
    parts = [(1.0, 0.0, 0.0, 0.0), (4.0, 12.0, 6.0, 1.0), (1.0, 6.0, 12.0, 4.0), (0.0, 0.0, 0.0, 1.0)]
    table = {}
    for i in range(4):
        for j in range(i, 4):
            coefs = [0.0] * 7
            for p in range(4):
                for q in range(4):
                    coefs[p + q] += parts[i][p] * parts[j][q] / 36.0
            table[i, j] = coefs
    return table


def split3(value):
    high = value.astype(bf16).astype(f32)
    rest = value - high
    middle = rest.astype(bf16).astype(f32)
    return [high, middle, rest - middle]


def spline_basis(phase_rows):
    remain = 1.0 - phase_rows
    square = phase_rows * phase_rows
    cube_term = square * phase_rows
    return [
        remain * remain * remain / 6.0,
        (3.0 * cube_term - 6.0 * square + 4.0) / 6.0,
        (-3.0 * cube_term + 3.0 * square + 3.0 * phase_rows + 1.0) / 6.0,
        cube_term / 6.0,
    ]


def solve_small(moments):
    matrix = {}
    position = 0
    for m in range(5):
        for n in range(m, 5):
            matrix[m, n] = moments[position] + (src_ridge if m == n else 0.0)
            position += 1
    factor = {}
    inverse = {}
    for j in range(5):
        for i in range(j, 5):
            running = matrix[j, i]
            for k in range(j):
                running = running - factor[i, k] * factor[j, k]
            if i == j:
                factor[j, j] = jnp.sqrt(running)
                inverse[j] = 1.0 / factor[j, j]
            else:
                factor[i, j] = running * inverse[j]
    forward = []
    for i in range(5):
        running = moments[15 + i]
        for k in range(i):
            running = running - factor[i, k] * forward[k]
        forward.append(running * inverse[i])
    solved = [None] * 5
    for i in reversed(range(5)):
        running = forward[i]
        for k in range(i + 1, 5):
            running = running - factor[k, i] * solved[k]
        solved[i] = running * inverse[i]
    return solved


def iota(shape, axis):
    return lax.broadcasted_iota(jnp.int32, shape, axis)


def fill_counts(counts_ref, limit_ref):
    shards = counts_ref.shape[2]
    rep = limit_ref.shape[0] // shards
    for d in range(shards):
        limit_ref[pl.ds(d * rep, rep), :] = jnp.full((rep, LANES), counts_ref[0, 0, d], jnp.int32)


def live_rows(limit_ref, start, rep):
    tile_row = start + iota((SUB, LANES), 0)
    slot = lax.rem(tile_row, rep) * LANES + iota((SUB, LANES), 1)
    return (slot < limit_ref[pl.ds(start, SUB), :]).astype(f32)


def by_tile(wide_ref, tiled_ref):
    rows = wide_ref.shape[0]
    for t in range(tiled_ref.shape[0]):
        tiled_ref[t, 0:rows, :] = wide_ref[:, t * LANES : (t + 1) * LANES]


def onehot(index_row, count):
    hit = iota((count, LANES), 0) == index_row
    return jnp.where(hit, 1.0, 0.0).astype(bf16)


def contract(left, right):
    return lax.dot_general(left, right, (((1,), (1,)), ((), ())), preferred_element_type=f32)


def shift_up(value, n):
    turned = pltpu.roll(value, n, 1)
    before = pltpu.roll(turned, 1, 0)
    before = jnp.where(iota(value.shape, 0) == 0, 0.0, before)
    return jnp.where(iota(value.shape, 1) < n, before, turned)


def shift_down(value, n):
    turned = pltpu.roll(value, LANES - n, 1)
    after = pltpu.roll(turned, value.shape[0] - 1, 0)
    after = jnp.where(iota(value.shape, 0) == value.shape[0] - 1, 0.0, after)
    return jnp.where(iota(value.shape, 1) >= LANES - n, after, turned)


def source_kernel(counts_ref, design_ref, obs_ref, weight_ref, index_ref, out_ref, tiled, limit, pieces, total):
    tiles = obs_ref.shape[0]
    rep = tiles // counts_ref.shape[2]
    fill_counts(counts_ref, limit)
    by_tile(design_ref, tiled)
    total[...] = jnp.zeros_like(total)
    highs = SRC_DEV // LOW

    def group(g, _):
        start = pl.multiple_of(g * SUB, SUB)
        rows = pl.ds(start, SUB)
        w = weight_ref[rows, :] * live_rows(limit, start, rep)
        cols = [tiled[rows, m, :] for m in range(5)]
        cols_w = [c * w for c in cols]
        values = [cols_w[m] * cols[n] for m in range(5) for n in range(m, 5)]
        values += [c * obs_ref[rows, :] for c in cols_w]
        for q, value in enumerate(values):
            for s, part in enumerate(split3(value)):
                pieces[:, s * SIGNALS + q, :] = part
        lefts, rights = [], []
        for i in range(SUB):
            block = pieces[i].astype(bf16)
            index = index_ref[pl.ds(start + i, 1), :]
            high = index // LOW
            masks = [jnp.where(jnp.broadcast_to(high, block.shape) == h, 1.0, 0.0).astype(bf16) for h in range(highs)]
            lefts.append(jnp.concatenate([block * mask for mask in masks], 0))
            rights.append(onehot(index - high * LOW, LOW))
        total[...] += contract(jnp.concatenate(lefts, 1), jnp.concatenate(rights, 1))
        return 0

    lax.fori_loop(0, tiles // SUB, group, 0)
    rows = pieces.shape[1]
    for h in range(highs):
        block = total[h * rows : h * rows + 3 * SIGNALS, :]
        summed = block[0:SIGNALS] + block[SIGNALS : 2 * SIGNALS] + block[2 * SIGNALS : 3 * SIGNALS]
        for half in range(LOW // LANES):
            out_ref[:, h * (LOW // LANES) + half, :] = summed[:, half * LANES : (half + 1) * LANES]


def band_kernel(counts_ref, phase_ref, axis_ref, weight_ref, knot_ref, out_ref, tiled, limit, pieces, moments):
    tiles = phase_ref.shape[0]
    shards = counts_ref.shape[2]
    rep = tiles // shards
    fill_counts(counts_ref, limit)
    by_tile(axis_ref, tiled)
    width = pieces.shape[1]

    def group(g, _):
        start = pl.multiple_of(g * SUB, SUB)
        rows = pl.ds(start, SUB)
        w = weight_ref[rows, :] * live_rows(limit, start, rep)
        u = phase_ref[rows, :]
        r = 1.0 - u
        u2, r2 = u * u, r * r
        u3, r3 = u2 * u, r2 * r
        powers = [r3 * r3, r3 * r2 * u, r2 * r2 * u2, r3 * u3, r2 * u2 * u2, r * u2 * u3, u3 * u3]
        axes = [tiled[rows, x, :] for x in range(3)]
        axes_w = [a * w for a in axes]
        pairs = [axes_w[x] * axes[y] for x, y in PAIRS]
        for p in range(7):
            for n in range(6):
                pieces[:, p * 6 + n, :] = powers[p] * pairs[n]
        per_block = min(rep, SUB)
        for b in range(SUB // per_block):
            lefts, rights = [], []
            for i in range(b * per_block, (b + 1) * per_block):
                lefts.append(jnp.concatenate(split3(pieces[i]), 0).astype(bf16))
                rights.append(onehot(knot_ref[pl.ds(start + i, 1), :], KNOT_DEV))
            got = contract(jnp.concatenate(lefts, 1), jnp.concatenate(rights, 1))
            summed = got[0:width] + got[width : 2 * width] + got[2 * width :]
            where_to = (start + b * per_block) // rep
            if rep <= SUB:
                moments[:, pl.ds(where_to, 1), :] = summed[:, None, :]
            else:
                moments[:, pl.ds(where_to, 1), :] += summed[:, None, :]
        return 0

    if rep > SUB:
        moments[...] = jnp.zeros_like(moments)
    lax.fori_loop(0, tiles // SUB, group, 0)
    table = bernstein_products()
    for n in range(6):
        parts = [moments[p * 6 + n] for p in range(7)]

        def product(i, j):
            return sum(c * part for c, part in zip(table[i, j], parts) if c)

        for delta in range(4):
            running = product(3 - delta, 3)
            for j in reversed(range(3 - delta)):
                running = product(j, j + delta) + shift_up(running, 1)
            out_ref[delta * 6 + n] = running


def resid_kernel(
    counts_ref, mine_ref, other_ref, design_ref, obs_ref, weight_ref, index_ref, phase_ref, axis_ref, knot_ref,
    params_ref, resid_ref, rhs_ref, tiled, tiled_axis, limit, pieces, moments, solved_ref,
):
    tiles = obs_ref.shape[0]
    shards = counts_ref.shape[2]
    rep = tiles // shards
    fill_counts(counts_ref, limit)
    by_tile(design_ref, tiled)
    by_tile(axis_ref, tiled_axis)
    solved = solve_small([mine_ref[q] + other_ref[q] for q in range(SIGNALS)])
    blocks = SRC_DEV // LANES
    for m in range(5):
        solved_ref[m] = solved[m]
        for b in range(blocks):
            params_ref[m : m + 1, b * LANES : (b + 1) * LANES] = solved[m][b : b + 1, :]
    width = pieces.shape[1]

    def group(g, _):
        start = pl.multiple_of(g * SUB, SUB)
        rows = pl.ds(start, SUB)
        live = live_rows(limit, start, rep)
        index = index_ref[rows, :]
        block_of = index // LANES
        lane_of = index - block_of * LANES
        hits = [block_of == b for b in range(blocks)]
        fitted = jnp.zeros((SUB, LANES), f32)
        for m in range(5):
            picked = jnp.zeros((SUB, LANES), f32)
            for b in range(blocks):
                table = jnp.broadcast_to(solved_ref[m, b : b + 1, :], (SUB, LANES))
                picked = jnp.where(hits[b], jnp.take_along_axis(table, lane_of, axis=1), picked)
            fitted = fitted + tiled[rows, m, :] * picked
        resid = live * (obs_ref[rows, :] - fitted)
        resid_ref[rows, :] = resid
        scaled = weight_ref[rows, :] * live * resid
        basis = spline_basis(phase_ref[rows, :])
        for x in range(3):
            along = scaled * tiled_axis[rows, x, :]
            for j in range(4):
                pieces[:, j * 3 + x, :] = along * basis[j]
        per_block = min(rep, SUB)
        for b in range(SUB // per_block):
            lefts, rights = [], []
            for i in range(b * per_block, (b + 1) * per_block):
                lefts.append(jnp.concatenate(split3(pieces[i]), 0).astype(bf16))
                rights.append(onehot(knot_ref[pl.ds(start + i, 1), :], KNOT_DEV))
            got = contract(jnp.concatenate(lefts, 1), jnp.concatenate(rights, 1))
            summed = got[0:width] + got[width : 2 * width] + got[2 * width :]
            where_to = (start + b * per_block) // rep
            if rep <= SUB:
                moments[:, pl.ds(where_to, 1), :] = summed[:, None, :]
            else:
                moments[:, pl.ds(where_to, 1), :] += summed[:, None, :]
        return 0

    if rep > SUB:
        moments[...] = jnp.zeros_like(moments)
    lax.fori_loop(0, tiles // SUB, group, 0)
    for x in range(3):
        running = moments[9 + x]
        for j in reversed(range(3)):
            running = moments[j * 3 + x] + shift_up(running, 1)
        rhs_ref[x] = running


def final_kernel(
    counts_ref, place_ref, sums_ref, resid_ref, phase_ref, axis_ref, knot_ref,
    att_ref, out_ref, tiled_axis, limit, tables, coef_ref,
):
    tiles = phase_ref.shape[0]
    shards = counts_ref.shape[2]
    rep = tiles // shards
    fill_counts(counts_ref, limit)
    by_tile(axis_ref, tiled_axis)
    order = {pair: n for n, pair in enumerate(PAIRS)}

    def band(delta, x, y):
        return sums_ref[3 + delta * 6 + order[min(x, y), max(x, y)]]

    rhs = [sums_ref[x] for x in range(3)]
    scale = [relax_step / (att_ridge + band(0, x, x)) for x in range(3)]
    coefs = [rhs[x] * scale[x] for x in range(3)]
    for _ in range(1, ITERS):
        ahead = {(y, delta): shift_down(coefs[y], delta) for y in range(3) for delta in range(1, 4)}
        fresh = []
        for x in range(3):
            normal = att_ridge * coefs[x]
            for y in range(3):
                normal = normal + band(0, x, y) * coefs[y]
            for delta in range(1, 4):
                for y in range(3):
                    normal = normal + band(delta, x, y) * ahead[y, delta]
                normal = normal + shift_up(sum(band(delta, x, y) * coefs[y] for y in range(3)), delta)
            fresh.append(coefs[x] + scale[x] * (rhs[x] - normal))
        coefs = fresh
    place = place_ref[0]
    for x in range(3):
        coef_ref[x] = coefs[x]
        att_ref[x : x + 1, :] = coef_ref[x, pl.ds(place, 1), :]
        for j in range(4):
            window = coefs[x] if j == 0 else shift_down(coefs[x], j)
            for d in range(shards):
                tables[x * 4 + j, pl.ds(d * rep, rep), :] = jnp.broadcast_to(window[d : d + 1], (rep, LANES))

    def group(g, _):
        start = pl.multiple_of(g * SUB, SUB)
        rows = pl.ds(start, SUB)
        knots = knot_ref[rows, :]
        basis = spline_basis(phase_ref[rows, :])
        predicted = jnp.zeros((SUB, LANES), f32)
        for j in range(4):
            inner = jnp.zeros((SUB, LANES), f32)
            for x in range(3):
                inner = inner + tiled_axis[rows, x, :] * jnp.take_along_axis(tables[x * 4 + j, rows, :], knots, axis=1)
            predicted = predicted + basis[j] * inner
        out_ref[rows, :] = live_rows(limit, start, rep) * (resid_ref[rows, :] - predicted)
        return 0

    lax.fori_loop(0, tiles // SUB, group, 0)


SMEM = pl.BlockSpec(memory_space=pltpu.SMEM)
VMEM = pl.BlockSpec(memory_space=pltpu.VMEM)


def call(kernel, name, scalars, arrays, outs, scratch):
    return pl.pallas_call(
        kernel,
        name=name,
        out_shape=outs,
        in_specs=[SMEM] * len(scalars) + [VMEM] * len(arrays),
        out_specs=jax.tree.map(lambda _: VMEM, outs),
        scratch_shapes=scratch,
    )(*scalars, *arrays)


def swapped(value, axis, bit):
    size = lax.axis_size(axis)
    return lax.ppermute(value, axis, [(i, i ^ bit) for i in range(size)])


def summed_over(value, axis):
    size = lax.axis_size(axis)
    if size & (size - 1):
        return lax.psum(value, axis)
    bit = 1
    while bit < size:
        value = value + swapped(value, axis, bit)
        bit *= 2
    return value


def on_device(design, observed, weight, phase_frac, axis_factors, source_index, knot_index, counts):
    row_count = observed.shape[0]
    tiles = row_count // LANES
    shards = lax.axis_size("src")
    obs, w, phase, index, knots = (
        a.reshape(tiles, LANES) for a in (observed, weight, phase_frac, source_index, knot_index)
    )
    tiled = pltpu.VMEM((tiles, SUB, LANES), f32)
    limit = pltpu.VMEM((tiles, LANES), jnp.int32)
    blocks = SRC_DEV // LANES
    highs = SRC_DEV // LOW
    moments = call(
        source_kernel, "source_sums", [counts], [design, obs, w, index],
        jax.ShapeDtypeStruct((SIGNALS, blocks, LANES), f32),
        [tiled, limit, pltpu.VMEM((SUB, 64, LANES), f32), pltpu.VMEM((highs * 64, LOW), f32)],
    )
    band = call(
        band_kernel, "band_sums", [counts], [phase, axis_factors, w, knots],
        jax.ShapeDtypeStruct((24, shards, KNOT_DEV), f32),
        [tiled, limit, pltpu.VMEM((SUB, 48, LANES), f32), pltpu.VMEM((48, shards, KNOT_DEV), f32)],
    )
    if lax.axis_size("ccd") == 2:
        other = swapped(moments, "ccd", 1)
    else:
        moments = summed_over(moments, "ccd")
        other = jnp.zeros_like(moments)
    params, resid, rhs = call(
        resid_kernel, "residuals", [counts], [moments, other, design, obs, w, index, phase, axis_factors, knots],
        (
            jax.ShapeDtypeStruct((5, SRC_DEV), f32),
            jax.ShapeDtypeStruct((tiles, LANES), f32),
            jax.ShapeDtypeStruct((3, shards, KNOT_DEV), f32),
        ),
        [
            tiled, tiled, limit, pltpu.VMEM((SUB, 16, LANES), f32), pltpu.VMEM((16, shards, KNOT_DEV), f32),
            pltpu.VMEM((5, blocks, LANES), f32),
        ],
    )
    sums = jnp.concatenate([rhs, band], 0)
    sums = summed_over(summed_over(sums, "ccd"), "src")
    place = lax.axis_index("src").reshape(1)
    attitude, residual = call(
        final_kernel, "attitude", [counts, place], [sums, resid, phase, axis_factors, knots],
        (jax.ShapeDtypeStruct((3, KNOT_DEV), f32), jax.ShapeDtypeStruct((tiles, LANES), f32)),
        [tiled, limit, pltpu.VMEM((12, tiles, LANES), f32), pltpu.VMEM((3, shards, KNOT_DEV), f32)],
    )
    return params, attitude, residual.reshape(row_count)


def solution(mesh):
    rows = P(("src", "ccd"))
    wide = P(None, ("src", "ccd"))
    in_specs = (wide, rows, rows, rows, wide, rows, rows, P("src", "ccd", None))
    out_specs = (P(None, "src"), P(None, "src"), rows)
    return jax.shard_map(on_device, mesh=mesh, in_specs=in_specs, out_specs=out_specs, check_vma=False)
```

```python
import jax
import jax.numpy as jnp
from jax import lax
from jax.experimental import pallas as pl
from jax.experimental.pallas import tpu as pltpu
from jax.sharding import PartitionSpec as P

SRC_DEV = 1024
KNOT_DEV = 128
ITERS = 3
LANES = 128
SUB = 8
LOW = 256
SIGNALS = 15 + 5
PAIRS = [(x, y) for x in range(3) for y in range(x, 3)]

src_ridge = 1.0
att_ridge = 1.0
relax_step = 0.15

f32 = jnp.float32
bf16 = jnp.bfloat16


def bernstein_products():
    parts = [(1.0, 0.0, 0.0, 0.0), (4.0, 12.0, 6.0, 1.0), (1.0, 6.0, 12.0, 4.0), (0.0, 0.0, 0.0, 1.0)]
    table = {}
    for i in range(4):
        for j in range(i, 4):
            coefs = [0.0] * 7
            for p in range(4):
                for q in range(4):
                    coefs[p + q] += parts[i][p] * parts[j][q] / 36.0
            table[i, j] = coefs
    return table


def split3(value):
    high = value.astype(bf16).astype(f32)
    rest = value - high
    middle = rest.astype(bf16).astype(f32)
    return [high, middle, rest - middle]


def spline_basis(phase_rows):
    remain = 1.0 - phase_rows
    square = phase_rows * phase_rows
    cube_term = square * phase_rows
    return [
        remain * remain * remain / 6.0,
        (3.0 * cube_term - 6.0 * square + 4.0) / 6.0,
        (-3.0 * cube_term + 3.0 * square + 3.0 * phase_rows + 1.0) / 6.0,
        cube_term / 6.0,
    ]


def solve_small(moments):
    matrix = {}
    position = 0
    for m in range(5):
        for n in range(m, 5):
            matrix[m, n] = moments[position] + (src_ridge if m == n else 0.0)
            position += 1
    factor = {}
    inverse = {}
    for j in range(5):
        for i in range(j, 5):
            running = matrix[j, i]
            for k in range(j):
                running = running - factor[i, k] * factor[j, k]
            if i == j:
                factor[j, j] = jnp.sqrt(running)
                inverse[j] = 1.0 / factor[j, j]
            else:
                factor[i, j] = running * inverse[j]
    forward = []
    for i in range(5):
        running = moments[15 + i]
        for k in range(i):
            running = running - factor[i, k] * forward[k]
        forward.append(running * inverse[i])
    solved = [None] * 5
    for i in reversed(range(5)):
        running = forward[i]
        for k in range(i + 1, 5):
            running = running - factor[k, i] * solved[k]
        solved[i] = running * inverse[i]
    return solved


def iota(shape, axis):
    return lax.broadcasted_iota(jnp.int32, shape, axis)


def fill_counts(counts_ref, limit_ref):
    shards = counts_ref.shape[2]
    rep = limit_ref.shape[0] // shards
    for d in range(shards):
        limit_ref[pl.ds(d * rep, rep), :] = jnp.full((rep, LANES), counts_ref[0, 0, d], jnp.int32)


def live_rows(limit_ref, start, rep):
    tile_row = start + iota((SUB, LANES), 0)
    slot = lax.rem(tile_row, rep) * LANES + iota((SUB, LANES), 1)
    return (slot < limit_ref[pl.ds(start, SUB), :]).astype(f32)


def by_tile(wide_ref, tiled_ref):
    rows = wide_ref.shape[0]
    for t in range(tiled_ref.shape[0]):
        tiled_ref[t, 0:rows, :] = wide_ref[:, t * LANES : (t + 1) * LANES]


def spread_row(index_row, count):
    packed = jnp.broadcast_to(index_row.astype(f32), (2 * SUB, LANES)).astype(bf16)
    return jnp.concatenate([packed] * (count // (2 * SUB)), 0)


def is_equal(left, right):
    return jnp.where(left == right, jnp.ones((), bf16), jnp.zeros((), bf16))


def onehot(index_row, count):
    return is_equal(iota((count, LANES), 0).astype(f32).astype(bf16), spread_row(index_row, count))


def contract(left, right):
    return lax.dot_general(left, right, (((1,), (1,)), ((), ())), preferred_element_type=f32)


def shift_up(value, n):
    turned = pltpu.roll(value, n, 1)
    before = pltpu.roll(turned, 1, 0)
    before = jnp.where(iota(value.shape, 0) == 0, 0.0, before)
    return jnp.where(iota(value.shape, 1) < n, before, turned)


def shift_down(value, n):
    turned = pltpu.roll(value, LANES - n, 1)
    after = pltpu.roll(turned, value.shape[0] - 1, 0)
    after = jnp.where(iota(value.shape, 0) == value.shape[0] - 1, 0.0, after)
    return jnp.where(iota(value.shape, 1) >= LANES - n, after, turned)


def source_kernel(counts_ref, design_ref, obs_ref, weight_ref, index_ref, out_ref, tiled, limit, pieces, total):
    tiles = obs_ref.shape[0]
    rep = tiles // counts_ref.shape[2]
    fill_counts(counts_ref, limit)
    by_tile(design_ref, tiled)
    total[...] = jnp.zeros_like(total)
    highs = SRC_DEV // LOW

    def group(g, _):
        start = pl.multiple_of(g * SUB, SUB)
        rows = pl.ds(start, SUB)
        w = weight_ref[rows, :] * live_rows(limit, start, rep)
        cols = [tiled[rows, m, :] for m in range(5)]
        cols_w = [c * w for c in cols]
        values = [cols_w[m] * cols[n] for m in range(5) for n in range(m, 5)]
        values += [c * obs_ref[rows, :] for c in cols_w]
        for q, value in enumerate(values):
            for s, part in enumerate(split3(value)):
                pieces[:, s * SIGNALS + q, :] = part
        lefts, rights = [], []
        for i in range(SUB):
            block = pieces[i].astype(bf16)
            index = index_ref[pl.ds(start + i, 1), :]
            high = index // LOW
            packed = spread_row(high, 2 * SUB)
            masks = [is_equal(packed, jnp.full((), h, bf16)) for h in range(highs)]
            copies = block.shape[0] // (2 * SUB)
            lefts.append(jnp.concatenate([block * jnp.concatenate([mask] * copies, 0) for mask in masks], 0))
            rights.append(onehot(index - high * LOW, LOW))
        total[...] += contract(jnp.concatenate(lefts, 1), jnp.concatenate(rights, 1))
        return 0

    lax.fori_loop(0, tiles // SUB, group, 0)
    rows = pieces.shape[1]
    for h in range(highs):
        block = total[h * rows : h * rows + 3 * SIGNALS, :]
        summed = block[0:SIGNALS] + block[SIGNALS : 2 * SIGNALS] + block[2 * SIGNALS : 3 * SIGNALS]
        for half in range(LOW // LANES):
            out_ref[:, h * (LOW // LANES) + half, :] = summed[:, half * LANES : (half + 1) * LANES]


def band_kernel(counts_ref, phase_ref, axis_ref, weight_ref, knot_ref, out_ref, tiled, limit, pieces, moments):
    tiles = phase_ref.shape[0]
    shards = counts_ref.shape[2]
    rep = tiles // shards
    fill_counts(counts_ref, limit)
    by_tile(axis_ref, tiled)
    width = pieces.shape[1]

    def group(g, _):
        start = pl.multiple_of(g * SUB, SUB)
        rows = pl.ds(start, SUB)
        w = weight_ref[rows, :] * live_rows(limit, start, rep)
        u = phase_ref[rows, :]
        r = 1.0 - u
        u2, r2 = u * u, r * r
        u3, r3 = u2 * u, r2 * r
        powers = [r3 * r3, r3 * r2 * u, r2 * r2 * u2, r3 * u3, r2 * u2 * u2, r * u2 * u3, u3 * u3]
        axes = [tiled[rows, x, :] for x in range(3)]
        axes_w = [a * w for a in axes]
        pairs = [axes_w[x] * axes[y] for x, y in PAIRS]
        for p in range(7):
            for n in range(6):
                pieces[:, p * 6 + n, :] = powers[p] * pairs[n]
        per_block = min(rep, SUB)
        for b in range(SUB // per_block):
            lefts, rights = [], []
            for i in range(b * per_block, (b + 1) * per_block):
                lefts.append(jnp.concatenate(split3(pieces[i]), 0).astype(bf16))
                rights.append(onehot(knot_ref[pl.ds(start + i, 1), :], KNOT_DEV))
            got = contract(jnp.concatenate(lefts, 1), jnp.concatenate(rights, 1))
            summed = got[0:width] + got[width : 2 * width] + got[2 * width :]
            where_to = (start + b * per_block) // rep
            if rep <= SUB:
                moments[:, pl.ds(where_to, 1), :] = summed[:, None, :]
            else:
                moments[:, pl.ds(where_to, 1), :] += summed[:, None, :]
        return 0

    if rep > SUB:
        moments[...] = jnp.zeros_like(moments)
    lax.fori_loop(0, tiles // SUB, group, 0)
    table = bernstein_products()
    for n in range(6):
        parts = [moments[p * 6 + n] for p in range(7)]

        def product(i, j):
            return sum(c * part for c, part in zip(table[i, j], parts) if c)

        for delta in range(4):
            running = product(3 - delta, 3)
            for j in reversed(range(3 - delta)):
                running = product(j, j + delta) + shift_up(running, 1)
            out_ref[delta * 6 + n] = running


def pack(value, q, message_ref):
    quantities = len(PAIRS) * 4 + 3
    parts = message_ref.shape[0]
    shards = value.shape[0]
    owned = shards // parts
    zero = jnp.zeros((1, LANES), f32)
    for p in range(parts):
        for r in range(owned):
            d = p * owned + r
            message_ref[p, r * quantities + q : r * quantities + q + 1, :] = value[d : d + 1]
        start, stop = p * owned, (p + 1) * owned
        after = value[stop : stop + 1] if stop < shards else zero
        before = value[start - 1 : start] if start else zero
        edge = jnp.where(iota((1, LANES), 1) < LANES // 2, after, before)
        message_ref[p, owned * quantities + q : owned * quantities + q + 1, :] = edge


def resid_kernel(
    counts_ref, mine_ref, other_ref, band_ref, design_ref, obs_ref, weight_ref, index_ref, phase_ref, axis_ref, knot_ref,
    params_ref, resid_ref, message_ref, tiled, tiled_axis, limit, pieces, moments, solved_ref,
):
    tiles = obs_ref.shape[0]
    shards = counts_ref.shape[2]
    rep = tiles // shards
    fill_counts(counts_ref, limit)
    by_tile(design_ref, tiled)
    by_tile(axis_ref, tiled_axis)
    solved = solve_small([mine_ref[q] + other_ref[q] for q in range(SIGNALS)])
    blocks = SRC_DEV // LANES
    for m in range(5):
        solved_ref[m] = solved[m]
        for b in range(blocks):
            params_ref[m : m + 1, b * LANES : (b + 1) * LANES] = solved[m][b : b + 1, :]
    width = pieces.shape[1]

    def group(g, _):
        start = pl.multiple_of(g * SUB, SUB)
        rows = pl.ds(start, SUB)
        live = live_rows(limit, start, rep)
        index = index_ref[rows, :]
        block_of = index // LANES
        lane_of = index - block_of * LANES
        hits = [block_of == b for b in range(blocks)]
        fitted = jnp.zeros((SUB, LANES), f32)
        for m in range(5):
            picked = jnp.zeros((SUB, LANES), f32)
            for b in range(blocks):
                table = jnp.broadcast_to(solved_ref[m, b : b + 1, :], (SUB, LANES))
                picked = jnp.where(hits[b], jnp.take_along_axis(table, lane_of, axis=1), picked)
            fitted = fitted + tiled[rows, m, :] * picked
        resid = live * (obs_ref[rows, :] - fitted)
        resid_ref[rows, :] = resid
        scaled = weight_ref[rows, :] * live * resid
        basis = spline_basis(phase_ref[rows, :])
        for x in range(3):
            along = scaled * tiled_axis[rows, x, :]
            for j in range(4):
                pieces[:, j * 3 + x, :] = along * basis[j]
        per_block = min(rep, SUB)
        for b in range(SUB // per_block):
            lefts, rights = [], []
            for i in range(b * per_block, (b + 1) * per_block):
                lefts.append(jnp.concatenate(split3(pieces[i]), 0).astype(bf16))
                rights.append(onehot(knot_ref[pl.ds(start + i, 1), :], KNOT_DEV))
            got = contract(jnp.concatenate(lefts, 1), jnp.concatenate(rights, 1))
            summed = got[0:width] + got[width : 2 * width] + got[2 * width :]
            where_to = (start + b * per_block) // rep
            if rep <= SUB:
                moments[:, pl.ds(where_to, 1), :] = summed[:, None, :]
            else:
                moments[:, pl.ds(where_to, 1), :] += summed[:, None, :]
        return 0

    if rep > SUB:
        moments[...] = jnp.zeros_like(moments)
    lax.fori_loop(0, tiles // SUB, group, 0)
    for x in range(3):
        running = moments[9 + x]
        for j in reversed(range(3)):
            running = moments[j * 3 + x] + shift_up(running, 1)
        pack(running, x, message_ref)
    for q in range(band_ref.shape[0]):
        pack(band_ref[q], 3 + q, message_ref)


def solve_kernel(place_ref, sums_ref, out_ref):
    quantities = len(PAIRS) * 4 + 3
    owned = out_ref.shape[0] // 4
    ring = -(-(owned + 2) // SUB) * SUB
    order = {pair: n for n, pair in enumerate(PAIRS)}
    row, lane = iota((ring, LANES), 0), iota((ring, LANES), 1)
    inside = row < owned
    after = (row == owned) & (lane < LANES // 2)
    before = (row == ring - 1) & (lane >= LANES // 2)
    edge = (place_ref[0] == place_ref[1] - 1).astype(jnp.int32)
    known = jnp.where(after & (jnp.full((ring, LANES), edge, jnp.int32) == 1), 0.0, 1.0)

    def load(q):
        rows = jnp.concatenate([sums_ref[pl.ds(r * quantities + q, 1), :] for r in range(owned)], 0)
        rest = jnp.broadcast_to(sums_ref[pl.ds(owned * quantities + q, 1), :], (ring - owned, LANES))
        return jnp.where(inside | after | before, jnp.concatenate([rows, rest], 0), 0.0)

    def turn(value, n):
        turned = pltpu.roll(value, n % LANES, 1)
        if n > 0:
            return jnp.where(lane < n, pltpu.roll(turned, 1, 0), turned)
        return jnp.where(lane >= LANES + n, pltpu.roll(turned, ring - 1, 0), turned)

    loaded = [load(q) for q in range(quantities)]

    def band(delta, x, y):
        return loaded[3 + delta * 6 + order[min(x, y), max(x, y)]]

    rhs = loaded[:3]
    scale = [relax_step / (att_ridge + band(0, x, x)) * known for x in range(3)]
    coefs = [rhs[x] * scale[x] for x in range(3)]
    for _ in range(1, ITERS):
        ahead = {(y, delta): turn(coefs[y], -delta) for y in range(3) for delta in range(1, 4)}
        fresh = []
        for x in range(3):
            normal = att_ridge * coefs[x]
            for y in range(3):
                normal = normal + band(0, x, y) * coefs[y]
            for delta in range(1, 4):
                for y in range(3):
                    normal = normal + band(delta, x, y) * ahead[y, delta]
                normal = normal + turn(sum(band(delta, x, y) * coefs[y] for y in range(3)), delta)
            fresh.append(coefs[x] + scale[x] * (rhs[x] - normal))
        coefs = fresh
    for x in range(3):
        for r in range(owned):
            out_ref[pl.ds(r * 4 + x, 1), :] = coefs[x][r : r + 1]


def predict_kernel(
    counts_ref, place_ref, coef_ref, resid_ref, phase_ref, axis_ref, knot_ref,
    att_ref, out_ref, tiled_axis, limit, tables, own,
):
    tiles = phase_ref.shape[0]
    shards = counts_ref.shape[2]
    rep = tiles // shards
    fill_counts(counts_ref, limit)
    by_tile(axis_ref, tiled_axis)
    place = place_ref[0]
    for x in range(3):
        coefs = coef_ref[:, x, :]
        own[x] = coefs
        att_ref[x : x + 1, :] = own[x, pl.ds(place, 1), :]
        for j in range(4):
            window = coefs if j == 0 else shift_down(coefs, j)
            for d in range(shards):
                tables[x * 4 + j, pl.ds(d * rep, rep), :] = jnp.broadcast_to(window[d : d + 1], (rep, LANES))

    def group(g, _):
        start = pl.multiple_of(g * SUB, SUB)
        rows = pl.ds(start, SUB)
        knots = knot_ref[rows, :]
        basis = spline_basis(phase_ref[rows, :])
        predicted = jnp.zeros((SUB, LANES), f32)
        for j in range(4):
            inner = jnp.zeros((SUB, LANES), f32)
            for x in range(3):
                inner = inner + tiled_axis[rows, x, :] * jnp.take_along_axis(tables[x * 4 + j, rows, :], knots, axis=1)
            predicted = predicted + basis[j] * inner
        out_ref[rows, :] = live_rows(limit, start, rep) * (resid_ref[rows, :] - predicted)
        return 0

    lax.fori_loop(0, tiles // SUB, group, 0)


BOTH = ("src", "ccd")
SMEM = pl.BlockSpec(memory_space=pltpu.SMEM)
VMEM = pl.BlockSpec(memory_space=pltpu.VMEM)


def call(kernel, name, scalars, arrays, outs, scratch):
    return pl.pallas_call(
        kernel,
        name=name,
        out_shape=outs,
        in_specs=[SMEM] * len(scalars) + [VMEM] * len(arrays),
        out_specs=jax.tree.map(lambda _: VMEM, outs),
        scratch_shapes=scratch,
        compiler_params=pltpu.CompilerParams(vmem_limit_bytes=8 << 20),
    )(*scalars, *arrays)


def swapped(value, axis, bit):
    size = lax.axis_size(axis)
    return lax.ppermute(value, axis, [(i, i ^ bit) for i in range(size)])


def summed_over(value, axis):
    size = lax.axis_size(axis)
    if size & (size - 1):
        return lax.psum(value, axis)
    bit = 1
    while bit < size:
        value = value + swapped(value, axis, bit)
        bit *= 2
    return value


def halved(value, mask, keep):
    pair = value.reshape((2, value.shape[0] // 2) + value.shape[1:])
    kept = lax.dynamic_index_in_dim(pair, keep, 0, False)
    sent = lax.dynamic_index_in_dim(pair, 1 - keep, 0, False)
    return kept + swapped(sent, BOTH, mask)


def doubled(value, mask, keep):
    other = swapped(value, BOTH, mask)
    first = jnp.where(keep == 0, value, other)
    second = jnp.where(keep == 0, other, value)
    return jnp.concatenate([first, second], 0)


def on_device(design, observed, weight, phase_frac, axis_factors, source_index, knot_index, counts):
    row_count = observed.shape[0]
    tiles = row_count // LANES
    shards = lax.axis_size("src")
    obs, w, phase, index, knots = (
        a.reshape(tiles, LANES) for a in (observed, weight, phase_frac, source_index, knot_index)
    )
    tiled = pltpu.VMEM((tiles, SUB, LANES), f32)
    limit = pltpu.VMEM((tiles, LANES), jnp.int32)
    blocks = SRC_DEV // LANES
    highs = SRC_DEV // LOW
    moments = call(
        source_kernel, "source_sums", [counts], [design, obs, w, index],
        jax.ShapeDtypeStruct((SIGNALS, blocks, LANES), f32),
        [tiled, limit, pltpu.VMEM((SUB, 64, LANES), f32), pltpu.VMEM((highs * 64, LOW), f32)],
    )
    band = call(
        band_kernel, "band_sums", [counts], [phase, axis_factors, w, knots],
        jax.ShapeDtypeStruct((24, shards, KNOT_DEV), f32),
        [tiled, limit, pltpu.VMEM((SUB, 48, LANES), f32), pltpu.VMEM((48, shards, KNOT_DEV), f32)],
    )
    if lax.axis_size("ccd") == 2:
        other = swapped(moments, "ccd", 1)
    else:
        moments = summed_over(moments, "ccd")
        other = jnp.zeros_like(moments)
    fast = lax.axis_size("ccd") == 2 and shards >= 4 and shards & (shards - 1) == 0
    parts = 4 if fast else 1
    owned = shards // parts
    message_rows = -(-(owned + 1) * 27 // SUB) * SUB
    params, resid, message = call(
        resid_kernel, "residuals", [counts],
        [moments, other, band, design, obs, w, index, phase, axis_factors, knots],
        (
            jax.ShapeDtypeStruct((5, SRC_DEV), f32),
            jax.ShapeDtypeStruct((tiles, LANES), f32),
            jax.ShapeDtypeStruct((parts, message_rows, LANES), f32),
        ),
        [
            tiled, tiled, limit, pltpu.VMEM((SUB, 16, LANES), f32), pltpu.VMEM((16, shards, KNOT_DEV), f32),
            pltpu.VMEM((5, blocks, LANES), f32),
        ],
    )
    place = lax.axis_index("src")
    if fast:
        upper = lax.axis_index("ccd")
        for shift in range(shards.bit_length() - 1):
            upper = upper ^ ((place >> shift) & 1)
        lower = place & 1
        sums = halved(halved(message, 1, upper), 3, lower)[0]
        bit = 2
        while bit < shards:
            sums = sums + swapped(sums, BOTH, 2 * bit + 1)
            bit *= 2
        part = 2 * upper + lower
    else:
        sums = summed_over(summed_over(message[0], "ccd"), "src")
        part = jnp.zeros_like(place)
    coefs = call(
        solve_kernel, "attitude", [jnp.stack([part, jnp.full_like(part, parts)])], [sums],
        jax.ShapeDtypeStruct((owned * 4, LANES), f32), [],
    )
    if fast:
        coefs = doubled(doubled(coefs, 3, lower), 1, upper)
    attitude, residual = call(
        predict_kernel, "predict", [counts, place.reshape(1)],
        [coefs.reshape(shards, 4, LANES), resid, phase, axis_factors, knots],
        (jax.ShapeDtypeStruct((3, KNOT_DEV), f32), jax.ShapeDtypeStruct((tiles, LANES), f32)),
        [tiled, limit, pltpu.VMEM((12, tiles, LANES), f32), pltpu.VMEM((3, shards, KNOT_DEV), f32)],
    )
    return params, attitude, residual.reshape(row_count)


def solution(mesh):
    rows = P(("src", "ccd"))
    wide = P(None, ("src", "ccd"))
    in_specs = (wide, rows, rows, rows, wide, rows, rows, P("src", "ccd", None))
    out_specs = (P(None, "src"), P(None, "src"), rows)
    return jax.shard_map(on_device, mesh=mesh, in_specs=in_specs, out_specs=out_specs, check_vma=False)
```

```python
import jax
import jax.numpy as jnp
from jax import lax
from jax.experimental import pallas as pl
from jax.experimental.pallas import tpu as pltpu
from jax.sharding import PartitionSpec as P

SRC_DEV = 1024
KNOT_DEV = 128
ITERS = 3
LANES = 128
SUB = 8
LOW = 256
STEPS = 16
CUBICS = [(1.0, 0.0, 0.0, 0.0), (4.0, 12.0, 6.0, 1.0), (1.0, 6.0, 12.0, 4.0), (0.0, 0.0, 0.0, 1.0)]
SIGNALS = 15 + 5
PAIRS = [(x, y) for x in range(3) for y in range(x, 3)]

src_ridge = 1.0
att_ridge = 1.0
relax_step = 0.15

f32 = jnp.float32
bf16 = jnp.bfloat16


def bernstein_products():
    table = {}
    for i in range(4):
        for j in range(i, 4):
            coefs = [0.0] * 7
            for p in range(4):
                for q in range(4):
                    coefs[p + q] += CUBICS[i][p] * CUBICS[j][q] / 36.0
            table[i, j] = coefs
    return table


def split3(value):
    high = value.astype(bf16).astype(f32)
    rest = value - high
    middle = rest.astype(bf16).astype(f32)
    return [high, middle, rest - middle]


def spline_basis(phase_rows):
    remain = 1.0 - phase_rows
    square = phase_rows * phase_rows
    cube_term = square * phase_rows
    return [
        remain * remain * remain / 6.0,
        (3.0 * cube_term - 6.0 * square + 4.0) / 6.0,
        (-3.0 * cube_term + 3.0 * square + 3.0 * phase_rows + 1.0) / 6.0,
        cube_term / 6.0,
    ]


def solve_small(moments):
    matrix = {}
    position = 0
    for m in range(5):
        for n in range(m, 5):
            matrix[m, n] = moments[position] + (src_ridge if m == n else 0.0)
            position += 1
    factor = {}
    inverse = {}
    for j in range(5):
        for i in range(j, 5):
            running = matrix[j, i]
            for k in range(j):
                running = running - factor[i, k] * factor[j, k]
            if i == j:
                factor[j, j] = jnp.sqrt(running)
                inverse[j] = 1.0 / factor[j, j]
            else:
                factor[i, j] = running * inverse[j]
    forward = []
    for i in range(5):
        running = moments[15 + i]
        for k in range(i):
            running = running - factor[i, k] * forward[k]
        forward.append(running * inverse[i])
    solved = [None] * 5
    for i in reversed(range(5)):
        running = forward[i]
        for k in range(i + 1, 5):
            running = running - factor[k, i] * solved[k]
        solved[i] = running * inverse[i]
    return solved


def iota(shape, axis):
    return lax.broadcasted_iota(jnp.int32, shape, axis)


def spread_row(index_row, count):
    packed = jnp.broadcast_to(index_row, (2 * SUB, LANES)).astype(bf16)
    return jnp.concatenate([packed] * (count // (2 * SUB)), 0)


def is_equal(left, right):
    return jnp.where(left == right, jnp.ones((), bf16), jnp.zeros((), bf16))


def onehot(index_row, count):
    return is_equal(iota((count, LANES), 0).astype(f32).astype(bf16), spread_row(index_row, count))


def by_tile(wide_ref, tiled_ref):
    rows = wide_ref.shape[0]
    for t in range(tiled_ref.shape[0]):
        tiled_ref[t, 0:rows, :] = wide_ref[:, t * LANES : (t + 1) * LANES]


def tile_of(wide_ref, t):
    block = wide_ref[:, pl.ds(pl.multiple_of(t * LANES, LANES), LANES)]
    return jnp.concatenate([block, jnp.zeros((SUB - block.shape[0], LANES), f32)], 0)


def row_of(ref, t):
    return jnp.broadcast_to(ref[pl.ds(t, 1), :], (SUB, LANES))


def per_sublane(values, kind):
    row = iota((SUB, LANES), 0)
    out = jnp.full((SUB, LANES), values[0], kind)
    for s in range(1, SUB):
        if values[s] != values[0]:
            out = jnp.where(row == s, jnp.full((SUB, LANES), values[s], kind), out)
    return out


def pick_rows(value, pattern):
    return jnp.take_along_axis(value, pattern, axis=0)


def patterns(values):
    values = list(values) + [0] * (-len(values) % SUB)
    return [per_sublane(values[i : i + SUB], jnp.int32) for i in range(0, len(values), SUB)]


def stacked_parts(values):
    value = jnp.concatenate(values, 0)
    rows = 3 * value.shape[0]
    parts = split3(value)
    if rows % (2 * SUB):
        parts.append(jnp.zeros((SUB, LANES), f32))
    return jnp.concatenate(parts, 0).astype(bf16)


def sum_parts(value, rows):
    return value[0:rows] + value[rows : 2 * rows] + value[2 * rows : 3 * rows]


def add_blocks(moments_ref, start, steps, rep, rows, left_of, knot_ref):
    per_block = min(rep, steps)
    for b in range(steps // per_block):
        lefts, rights = [], []
        for i in range(b * per_block, (b + 1) * per_block):
            lefts.append(left_of(start + i))
            rights.append(onehot(knot_ref[pl.ds(start + i, 1), :].astype(f32), KNOT_DEV))
        got = contract(jnp.concatenate(lefts, 1), jnp.concatenate(rights, 1))
        summed = sum_parts(got, rows)[:, None, :]
        where_to = pl.ds((start + b * per_block) // rep, 1)
        if rep <= steps:
            moments_ref[:, where_to, :] = summed
        else:
            moments_ref[:, where_to, :] += summed


def contract(left, right):
    return lax.dot_general(left, right, (((1,), (1,)), ((), ())), preferred_element_type=f32)


def shift_up(value, n):
    turned = pltpu.roll(value, n, 1)
    before = pltpu.roll(turned, 1, 0)
    before = jnp.where(iota(value.shape, 0) == 0, 0.0, before)
    return jnp.where(iota(value.shape, 1) < n, before, turned)


def shift_down(value, n):
    turned = pltpu.roll(value, LANES - n, 1)
    after = pltpu.roll(turned, value.shape[0] - 1, 0)
    after = jnp.where(iota(value.shape, 0) == value.shape[0] - 1, 0.0, after)
    return jnp.where(iota(value.shape, 1) >= LANES - n, after, turned)


def source_kernel(
    counts_hbm, design_hbm, obs_hbm, weight_hbm, index_hbm, out_ref, live_ref,
    counts_ref, design_ref, obs_ref, weight_ref, index_ref, sems, low_ref, high_ref, total,
):
    tiles = obs_ref.shape[0]
    shards = counts_ref.shape[2]
    rep = tiles // shards
    copies = [
        pltpu.make_async_copy(src, dst, sems.at[i])
        for i, (src, dst) in enumerate(
            [(counts_hbm, counts_ref), (weight_hbm, weight_ref), (index_hbm, index_ref), (obs_hbm, obs_ref),
             (design_hbm, design_ref)]
        )
    ]
    for copy in copies:
        copy.start()
    total[...] = jnp.zeros_like(total)
    highs = SRC_DEV // LOW
    pairs = [(m, n) for m in range(5) for n in range(m, 5)] + [(m, 5) for m in range(5)]
    lefts_of = patterns([m for m, _ in pairs])
    rights_of = patterns([n for _, n in pairs])
    rows = SUB * len(lefts_of)
    is_observed = iota((SUB, LANES), 0) == 5
    copies[0].wait()
    slots = iota((rep, LANES), 0) * LANES + iota((rep, LANES), 1)
    for d in range(shards):
        live_ref[pl.ds(d * rep, rep), :] = (slots < counts_ref[0, 0, d]).astype(f32)
    copies[1].wait()
    copies[2].wait()
    for g in range(tiles // SUB):
        at = pl.ds(g * SUB, SUB)
        weight_ref[at, :] = weight_ref[at, :] * live_ref[at, :]
        high = index_ref[at, :] // LOW
        high_ref[at, :] = high.astype(f32)
        low_ref[at, :] = (index_ref[at, :] - high * LOW).astype(f32)
    copies[3].wait()
    copies[4].wait()

    def group(g, _):
        start = g * STEPS
        lefts, rights = [], []
        for i in range(STEPS):
            t = start + i
            values = jnp.where(is_observed, row_of(obs_ref, t), tile_of(design_ref, t))
            scaled = values * row_of(weight_ref, t)
            block = stacked_parts([pick_rows(scaled, m) * pick_rows(values, n) for m, n in zip(lefts_of, rights_of)])
            packed = spread_row(high_ref[pl.ds(t, 1), :], 2 * SUB)
            masks = [is_equal(packed, jnp.full((), h, bf16)) for h in range(highs)]
            repeats = block.shape[0] // (2 * SUB)
            lefts.append(jnp.concatenate([block * jnp.concatenate([mask] * repeats, 0) for mask in masks], 0))
            rights.append(onehot(low_ref[pl.ds(t, 1), :], LOW))
        total[...] += contract(jnp.concatenate(lefts, 1), jnp.concatenate(rights, 1))
        return 0

    lax.fori_loop(0, tiles // STEPS, group, 0)
    height = total.shape[0] // highs
    for h in range(highs):
        summed = sum_parts(total[h * height : (h + 1) * height, :], rows)
        for half in range(LOW // LANES):
            out_ref[:, h * (LOW // LANES) + half, :] = summed[0:SIGNALS, half * LANES : (half + 1) * LANES]


def band_kernel(live_ref, phase_ref, axis_ref, weight_ref, knot_ref, out_ref, scaled_ref, moments):
    tiles, shards = phase_ref.shape[0], moments.shape[1]
    rep = tiles // shards
    scaled_ref[...] = weight_ref[...] * live_ref[...]
    rows = moments.shape[0]
    power = iota((SUB, LANES), 0)
    other = jnp.maximum(6 - power, 0)
    lefts_of = patterns([PAIRS[q % 6][0] for q in range(24)])
    rights_of = patterns([PAIRS[q % 6][1] for q in range(24)])
    powers_of = patterns([q // 6 for q in range(rows)])

    def left_of(t):
        u = row_of(phase_ref, t)
        r = 1.0 - u
        powers = jnp.ones((SUB, LANES), f32)
        for base, exponent in ((u, power), (r, other)):
            squared = base * base
            for bit, factor in ((1, base), (2, squared), (4, squared * squared)):
                powers = powers * jnp.where((exponent & bit) != 0, factor, 1.0)
        axes = tile_of(axis_ref, t)
        scaled = axes * row_of(scaled_ref, t)
        products = [pick_rows(scaled, x) * pick_rows(axes, y) for x, y in zip(lefts_of, rights_of)]
        return stacked_parts([products[i % 3] * pick_rows(powers, p) for i, p in enumerate(powers_of)])

    def group(g, _):
        add_blocks(moments, g * STEPS, STEPS, rep, rows, left_of, knot_ref)
        return 0

    if rep > STEPS:
        moments[...] = jnp.zeros_like(moments)
    lax.fori_loop(0, tiles // STEPS, group, 0)
    table = bernstein_products()
    for n in range(6):
        parts = [moments[p * 6 + n] for p in range(7)]

        def product(i, j):
            return sum(c * part for c, part in zip(table[i, j], parts) if c)

        for delta in range(4):
            running = product(3 - delta, 3)
            for j in reversed(range(3 - delta)):
                running = product(j, j + delta) + shift_up(running, 1)
            out_ref[delta * 6 + n] = running


def pack(value, q, message_ref):
    quantities = len(PAIRS) * 4 + 3
    parts = message_ref.shape[0]
    shards = value.shape[0]
    owned = shards // parts
    zero = jnp.zeros((1, LANES), f32)
    for p in range(parts):
        for r in range(owned):
            d = p * owned + r
            message_ref[p, r * quantities + q : r * quantities + q + 1, :] = value[d : d + 1]
        start, stop = p * owned, (p + 1) * owned
        after = value[stop : stop + 1] if stop < shards else zero
        before = value[start - 1 : start] if start else zero
        edge = jnp.where(iota((1, LANES), 1) < LANES // 2, after, before)
        message_ref[p, owned * quantities + q : owned * quantities + q + 1, :] = edge


def resid_kernel(
    mine_ref, other_ref, band_ref, live_ref, design_ref, obs_ref, weight_ref, index_ref, phase_ref, axis_ref, knot_ref,
    params_ref, resid_ref, message_ref, tiled, scaled_ref, moments, solved_ref,
):
    tiles, shards = obs_ref.shape[0], moments.shape[1]
    rep = tiles // shards
    by_tile(design_ref, tiled)
    solved = solve_small([mine_ref[q] + other_ref[q] for q in range(SIGNALS)])
    blocks = SRC_DEV // LANES
    for m in range(5):
        solved_ref[m] = solved[m]
        for b in range(blocks):
            params_ref[m : m + 1, b * LANES : (b + 1) * LANES] = solved[m][b : b + 1, :]
    rows = moments.shape[0]
    axes_of = patterns([q % 3 for q in range(rows)])
    weights_of = [
        [per_sublane([CUBICS[min(q // 3, 3)][c] / 6.0 for q in range(i, i + SUB)], f32) for c in range(4)]
        for i in range(0, rows, SUB)
    ]

    def left_of(t):
        u = row_of(phase_ref, t)
        r = 1.0 - u
        u2, r2 = u * u, r * r
        cubes = [r2 * r, r2 * u, r * u2, u2 * u]
        axes = tile_of(axis_ref, t)
        scaled = axes * row_of(scaled_ref, t)
        return stacked_parts(
            [pick_rows(scaled, x) * sum(c * m for c, m in zip(w, cubes)) for x, w in zip(axes_of, weights_of)]
        )

    def group(g, _):
        for part in range(STEPS // SUB):
            at = pl.ds(pl.multiple_of(g * STEPS + part * SUB, SUB), SUB)
            live = live_ref[at, :]
            index = index_ref[at, :]
            block_of = index // LANES
            lane_of = index - block_of * LANES
            hits = [block_of == b for b in range(blocks)]
            fitted = jnp.zeros((SUB, LANES), f32)
            for m in range(5):
                picked = jnp.zeros((SUB, LANES), f32)
                for b in range(blocks):
                    table = jnp.broadcast_to(solved_ref[m, b : b + 1, :], (SUB, LANES))
                    picked = jnp.where(hits[b], jnp.take_along_axis(table, lane_of, axis=1), picked)
                fitted = fitted + tiled[at, m, :] * picked
            resid = live * (obs_ref[at, :] - fitted)
            resid_ref[at, :] = resid
            scaled_ref[at, :] = weight_ref[at, :] * live * resid
        add_blocks(moments, g * STEPS, STEPS, rep, rows, left_of, knot_ref)
        return 0

    if rep > STEPS:
        moments[...] = jnp.zeros_like(moments)
    lax.fori_loop(0, tiles // STEPS, group, 0)
    for x in range(3):
        running = moments[9 + x]
        for j in reversed(range(3)):
            running = moments[j * 3 + x] + shift_up(running, 1)
        pack(running, x, message_ref)
    for q in range(band_ref.shape[0]):
        pack(band_ref[q], 3 + q, message_ref)


def solve_kernel(place_ref, sums_ref, out_ref):
    quantities = len(PAIRS) * 4 + 3
    owned = out_ref.shape[0] // 4
    ring = -(-(owned + 2) // SUB) * SUB
    order = {pair: n for n, pair in enumerate(PAIRS)}
    row, lane = iota((ring, LANES), 0), iota((ring, LANES), 1)
    inside = row < owned
    after = (row == owned) & (lane < LANES // 2)
    before = (row == ring - 1) & (lane >= LANES // 2)
    edge = (place_ref[0] == place_ref[1] - 1).astype(jnp.int32)
    known = jnp.where(after & (jnp.full((ring, LANES), edge, jnp.int32) == 1), 0.0, 1.0)

    def load(q):
        rows = jnp.concatenate([sums_ref[pl.ds(r * quantities + q, 1), :] for r in range(owned)], 0)
        rest = jnp.broadcast_to(sums_ref[pl.ds(owned * quantities + q, 1), :], (ring - owned, LANES))
        return jnp.where(inside | after | before, jnp.concatenate([rows, rest], 0), 0.0)

    def turn(value, n):
        turned = pltpu.roll(value, n % LANES, 1)
        if n > 0:
            return jnp.where(lane < n, pltpu.roll(turned, 1, 0), turned)
        return jnp.where(lane >= LANES + n, pltpu.roll(turned, ring - 1, 0), turned)

    loaded = [load(q) for q in range(quantities)]

    def band(delta, x, y):
        return loaded[3 + delta * 6 + order[min(x, y), max(x, y)]]

    rhs = loaded[:3]
    scale = [relax_step / (att_ridge + band(0, x, x)) * known for x in range(3)]
    coefs = [rhs[x] * scale[x] for x in range(3)]
    for _ in range(1, ITERS):
        ahead = {(y, delta): turn(coefs[y], -delta) for y in range(3) for delta in range(1, 4)}
        fresh = []
        for x in range(3):
            normal = att_ridge * coefs[x]
            for y in range(3):
                normal = normal + band(0, x, y) * coefs[y]
            for delta in range(1, 4):
                for y in range(3):
                    normal = normal + band(delta, x, y) * ahead[y, delta]
                normal = normal + turn(sum(band(delta, x, y) * coefs[y] for y in range(3)), delta)
            fresh.append(coefs[x] + scale[x] * (rhs[x] - normal))
        coefs = fresh
    for x in range(3):
        for r in range(owned):
            out_ref[pl.ds(r * 4 + x, 1), :] = coefs[x][r : r + 1]


def predict_kernel(
    place_ref, coef_ref, live_ref, resid_ref, phase_ref, axis_ref, knot_ref, att_ref, out_ref, tiled, windows,
):
    tiles, shards = phase_ref.shape[0], coef_ref.shape[0]
    rep = tiles // shards
    by_tile(axis_ref, tiled)
    for x in range(3):
        coefs = coef_ref[:, x, :]
        for j in range(4):
            windows[x * 4 + j] = coefs if j == 0 else shift_down(coefs, j)
        att_ref[x : x + 1, :] = windows[x * 4, pl.ds(place_ref[0], 1), :]
    row = iota((SUB, LANES), 0)

    def group(g, _):
        start = pl.multiple_of(g * SUB, SUB)
        at = pl.ds(start, SUB)
        knots = knot_ref[at, :]
        basis = spline_basis(phase_ref[at, :])
        first = start // rep
        predicted = jnp.zeros((SUB, LANES), f32)
        for j in range(4):
            inner = jnp.zeros((SUB, LANES), f32)
            for x in range(3):
                table = jnp.broadcast_to(windows[x * 4 + j, pl.ds(first, 1), :], (SUB, LANES))
                for k in range(1, SUB // rep):
                    later = jnp.broadcast_to(windows[x * 4 + j, pl.ds(first + k, 1), :], (SUB, LANES))
                    table = jnp.where(row >= k * rep, later, table)
                inner = inner + tiled[at, x, :] * jnp.take_along_axis(table, knots, axis=1)
            predicted = predicted + basis[j] * inner
        out_ref[at, :] = live_ref[at, :] * (resid_ref[at, :] - predicted)
        return 0

    lax.fori_loop(0, tiles // SUB, group, 0)


BOTH = ("src", "ccd")
SMEM = pl.BlockSpec(memory_space=pltpu.SMEM)
VMEM = pl.BlockSpec(memory_space=pltpu.VMEM)
HBM = pl.BlockSpec(memory_space=pltpu.HBM)


def call(kernel, name, scalars, arrays, outs, scratch, space=VMEM):
    return pl.pallas_call(
        kernel,
        name=name,
        out_shape=outs,
        in_specs=[SMEM] * len(scalars) + [space] * len(arrays),
        out_specs=jax.tree.map(lambda _: VMEM, outs),
        scratch_shapes=scratch,
        compiler_params=pltpu.CompilerParams(vmem_limit_bytes=8 << 20),
    )(*scalars, *arrays)


def swapped(value, axis, bit):
    size = lax.axis_size(axis)
    return lax.ppermute(value, axis, [(i, i ^ bit) for i in range(size)])


def summed_over(value, axis):
    size = lax.axis_size(axis)
    if size & (size - 1):
        return lax.psum(value, axis)
    bit = 1
    while bit < size:
        value = value + swapped(value, axis, bit)
        bit *= 2
    return value


def halved(value, mask, keep):
    pair = value.reshape((2, value.shape[0] // 2) + value.shape[1:])
    kept = lax.dynamic_index_in_dim(pair, keep, 0, False)
    sent = lax.dynamic_index_in_dim(pair, 1 - keep, 0, False)
    return kept + swapped(sent, BOTH, mask)


def doubled(value, mask, keep):
    other = swapped(value, BOTH, mask)
    first = jnp.where(keep == 0, value, other)
    second = jnp.where(keep == 0, other, value)
    return jnp.concatenate([first, second], 0)


def on_device(design, observed, weight, phase_frac, axis_factors, source_index, knot_index, counts):
    row_count = observed.shape[0]
    tiles = row_count // LANES
    shards = lax.axis_size("src")
    obs, w, phase, index, knots = (
        a.reshape(tiles, LANES) for a in (observed, weight, phase_frac, source_index, knot_index)
    )
    tiled = pltpu.VMEM((tiles, SUB, LANES), f32)
    dense = pltpu.VMEM((tiles, LANES), f32)
    blocks = SRC_DEV // LANES
    moments, live = call(
        source_kernel, "source_sums", [], [counts, design, obs, w, index],
        (jax.ShapeDtypeStruct((SIGNALS, blocks, LANES), f32), jax.ShapeDtypeStruct((tiles, LANES), f32)),
        [
            pltpu.SMEM(counts.shape, jnp.int32), pltpu.VMEM(design.shape, f32), dense, dense,
            pltpu.VMEM((tiles, LANES), jnp.int32), pltpu.SemaphoreType.DMA((5,)), dense, dense,
            pltpu.VMEM((SRC_DEV // LOW * 80, LOW), f32),
        ],
        HBM,
    )
    band = call(
        band_kernel, "band_sums", [], [live, phase, axis_factors, w, knots],
        jax.ShapeDtypeStruct((24, shards, KNOT_DEV), f32),
        [dense, pltpu.VMEM((48, shards, KNOT_DEV), f32)],
    )
    if lax.axis_size("ccd") == 2:
        other = swapped(moments, "ccd", 1)
    else:
        moments = summed_over(moments, "ccd")
        other = jnp.zeros_like(moments)
    fast = lax.axis_size("ccd") == 2 and shards >= 4 and shards & (shards - 1) == 0
    parts = 4 if fast else 1
    owned = shards // parts
    message_rows = -(-(owned + 1) * 27 // SUB) * SUB
    params, resid, message = call(
        resid_kernel, "residuals", [],
        [moments, other, band, live, design, obs, w, index, phase, axis_factors, knots],
        (
            jax.ShapeDtypeStruct((5, SRC_DEV), f32),
            jax.ShapeDtypeStruct((tiles, LANES), f32),
            jax.ShapeDtypeStruct((parts, message_rows, LANES), f32),
        ),
        [tiled, dense, pltpu.VMEM((16, shards, KNOT_DEV), f32), pltpu.VMEM((5, blocks, LANES), f32)],
    )
    place = lax.axis_index("src")
    if fast:
        upper = lax.axis_index("ccd")
        for shift in range(shards.bit_length() - 1):
            upper = upper ^ ((place >> shift) & 1)
        lower = place & 1
        sums = halved(halved(message, 1, upper), 3, lower)[0]
        bit = 2
        while bit < shards:
            sums = sums + swapped(sums, BOTH, 2 * bit + 1)
            bit *= 2
        part = 2 * upper + lower
    else:
        sums = summed_over(summed_over(message[0], "ccd"), "src")
        part = jnp.zeros_like(place)
    coefs = call(
        solve_kernel, "attitude", [jnp.stack([part, jnp.full_like(part, parts)])], [sums],
        jax.ShapeDtypeStruct((owned * 4, LANES), f32), [],
    )
    if fast:
        coefs = doubled(doubled(coefs, 3, lower), 1, upper)
    attitude, residual = call(
        predict_kernel, "predict", [place.reshape(1)],
        [coefs.reshape(shards, 4, LANES), live, resid, phase, axis_factors, knots],
        (jax.ShapeDtypeStruct((3, KNOT_DEV), f32), jax.ShapeDtypeStruct((tiles, LANES), f32)),
        [tiled, pltpu.VMEM((12, shards, KNOT_DEV), f32)],
    )
    return params, attitude, residual.reshape(row_count)


def solution(mesh):
    rows = P(("src", "ccd"))
    wide = P(None, ("src", "ccd"))
    in_specs = (wide, rows, rows, rows, wide, rows, rows, P("src", "ccd", None))
    out_specs = (P(None, "src"), P(None, "src"), rows)
    return jax.shard_map(on_device, mesh=mesh, in_specs=in_specs, out_specs=out_specs, check_vma=False)
```

```python
import math

import jax
import jax.numpy as jnp
from jax import lax
from jax.experimental import pallas as pl
from jax.experimental.pallas import tpu as pltpu
from jax.sharding import PartitionSpec as P

SRC_DEV = 1024
KNOT_DEV = 128
ITERS = 3
LANES = 128
SUB = 8
LOW = 256
QUANTITIES = 3 + 4 * 6
REACH = 3 * (ITERS - 1)
PER_ROW = LANES // (2 * REACH)
CUBICS = [(1.0, 0.0, 0.0, 0.0), (4.0, 12.0, 6.0, 1.0), (1.0, 6.0, 12.0, 4.0), (0.0, 0.0, 0.0, 1.0)]
SIGNALS = 15 + 5
PAIRS = [(x, y) for x in range(3) for y in range(x, 3)]

src_ridge = 1.0
att_ridge = 1.0
relax_step = 0.15

f32 = jnp.float32
bf16 = jnp.bfloat16


def bernstein_products():
    table = {}
    for i in range(4):
        for j in range(i, 4):
            coefs = [0.0] * 7
            for p in range(4):
                for q in range(4):
                    coefs[p + q] += CUBICS[i][p] * CUBICS[j][q] / 36.0
            table[i, j] = coefs
    return table


def split3(value):
    high = value.astype(bf16).astype(f32)
    rest = value - high
    middle = rest.astype(bf16).astype(f32)
    return [high, middle, rest - middle]


def spline_basis(phase_rows):
    remain = 1.0 - phase_rows
    square = phase_rows * phase_rows
    cube_term = square * phase_rows
    return [
        remain * remain * remain / 6.0,
        (3.0 * cube_term - 6.0 * square + 4.0) / 6.0,
        (-3.0 * cube_term + 3.0 * square + 3.0 * phase_rows + 1.0) / 6.0,
        cube_term / 6.0,
    ]


def solve_small(moments):
    matrix = {}
    position = 0
    for m in range(5):
        for n in range(m, 5):
            matrix[m, n] = moments[position] + (src_ridge if m == n else 0.0)
            position += 1
    factor = {}
    inverse = {}
    for j in range(5):
        for i in range(j, 5):
            running = matrix[j, i]
            for k in range(j):
                running = running - factor[i, k] * factor[j, k]
            if i == j:
                factor[j, j] = jnp.sqrt(running)
                inverse[j] = 1.0 / factor[j, j]
            else:
                factor[i, j] = running * inverse[j]
    forward = []
    for i in range(5):
        running = moments[15 + i]
        for k in range(i):
            running = running - factor[i, k] * forward[k]
        forward.append(running * inverse[i])
    solved = [None] * 5
    for i in reversed(range(5)):
        running = forward[i]
        for k in range(i + 1, 5):
            running = running - factor[k, i] * solved[k]
        solved[i] = running * inverse[i]
    return solved


def iota(shape, axis):
    return lax.broadcasted_iota(jnp.int32, shape, axis)


def over_steps(tiles, body):
    steps = math.gcd(tiles, 64)
    if steps == tiles:
        body(0, steps)
        return

    def one(g, _):
        body(pl.multiple_of(g * steps, steps), steps)
        return 0

    lax.fori_loop(0, tiles // steps, one, 0)


def spread_row(index_row, count):
    packed = jnp.broadcast_to(index_row, (2 * SUB, LANES)).astype(bf16)
    return jnp.concatenate([packed] * (count // (2 * SUB)), 0)


def is_equal(left, right):
    return jnp.where(left == right, jnp.ones((), bf16), jnp.zeros((), bf16))


def onehot(index_row, count):
    return is_equal(iota((count, LANES), 0).astype(f32).astype(bf16), spread_row(index_row, count))


def by_tile(wide_ref, tiled_ref):
    rows = wide_ref.shape[0]
    for t in range(tiled_ref.shape[0]):
        tiled_ref[t, 0:rows, :] = wide_ref[:, t * LANES : (t + 1) * LANES]


def tile_of(wide_ref, t):
    start = t * LANES if isinstance(t, int) else pl.multiple_of(t * LANES, LANES)
    block = wide_ref[:, pl.ds(start, LANES)]
    return jnp.concatenate([block, jnp.zeros((SUB - block.shape[0], LANES), f32)], 0)


def row_of(ref, t):
    return jnp.broadcast_to(ref[pl.ds(t, 1), :], (SUB, LANES))


def per_sublane(values, kind):
    row = iota((SUB, LANES), 0)
    out = jnp.full((SUB, LANES), values[0], kind)
    for s in range(1, SUB):
        if values[s] != values[0]:
            out = jnp.where(row == s, jnp.full((SUB, LANES), values[s], kind), out)
    return out


def pick_rows(value, pattern):
    return jnp.take_along_axis(value, pattern, axis=0)


def patterns(values):
    values = list(values) + [0] * (-len(values) % SUB)
    return [per_sublane(values[i : i + SUB], jnp.int32) for i in range(0, len(values), SUB)]


def stacked_parts(values):
    value = jnp.concatenate(values, 0)
    rows = 3 * value.shape[0]
    parts = split3(value)
    if rows % (2 * SUB):
        parts.append(jnp.zeros((SUB, LANES), f32))
    return jnp.concatenate(parts, 0).astype(bf16)


def sum_parts(value, rows):
    return value[0:rows] + value[rows : 2 * rows] + value[2 * rows : 3 * rows]


def add_blocks(moments_ref, start, steps, rep, rows, left_of, knot_ref):
    per_block = min(rep, steps)
    for b in range(steps // per_block):
        lefts, rights = [], []
        for i in range(b * per_block, (b + 1) * per_block):
            lefts.append(left_of(start + i))
            rights.append(onehot(knot_ref[pl.ds(start + i, 1), :].astype(f32), KNOT_DEV))
        got = contract(jnp.concatenate(lefts, 1), jnp.concatenate(rights, 1))
        summed = sum_parts(got, rows)[:, None, :]
        where_to = pl.ds((start + b * per_block) // rep, 1)
        if rep <= steps:
            moments_ref[:, where_to, :] = summed
        else:
            moments_ref[:, where_to, :] += summed


def contract(left, right):
    return lax.dot_general(left, right, (((1,), (1,)), ((), ())), preferred_element_type=f32)


def shift_up(value, n):
    turned = pltpu.roll(value, n, 1)
    before = pltpu.roll(turned, 1, 0)
    before = jnp.where(iota(value.shape, 0) == 0, 0.0, before)
    return jnp.where(iota(value.shape, 1) < n, before, turned)


def shift_down(value, n):
    turned = pltpu.roll(value, LANES - n, 1)
    after = pltpu.roll(turned, value.shape[0] - 1, 0)
    after = jnp.where(iota(value.shape, 0) == value.shape[0] - 1, 0.0, after)
    return jnp.where(iota(value.shape, 1) >= LANES - n, after, turned)


def source_kernel(
    counts_hbm, design_hbm, obs_hbm, weight_hbm, index_hbm, out_ref, live_ref,
    counts_ref, design_ref, obs_ref, weight_ref, index_ref, sems, low_ref, high_ref, total,
):
    tiles = obs_ref.shape[0]
    shards = counts_ref.shape[2]
    rep = tiles // shards
    copies = [
        pltpu.make_async_copy(src, dst, sems.at[i])
        for i, (src, dst) in enumerate(
            [(counts_hbm, counts_ref), (weight_hbm, weight_ref), (index_hbm, index_ref), (obs_hbm, obs_ref),
             (design_hbm, design_ref)]
        )
    ]
    for copy in copies:
        copy.start()
    if math.gcd(tiles, 64) != tiles:
        total[...] = jnp.zeros_like(total)
    highs = SRC_DEV // LOW
    pairs = [(m, n) for m in range(5) for n in range(m, 5)] + [(m, 5) for m in range(5)]
    pairs += pairs[2 * SUB :]
    lefts_of = patterns([m for m, _ in pairs])
    rights_of = patterns([n for _, n in pairs])
    first_half = iota((SUB, LANES), 0) < SUB // 2
    is_observed = iota((SUB, LANES), 0) == 5
    copies[0].wait()
    slots = iota((rep, LANES), 0) * LANES + iota((rep, LANES), 1)
    for d in range(shards):
        live_ref[pl.ds(d * rep, rep), :] = (slots < counts_ref[0, 0, d]).astype(f32)
    copies[1].wait()
    copies[2].wait()
    for g in range(tiles // SUB):
        at = pl.ds(g * SUB, SUB)
        weight_ref[at, :] = weight_ref[at, :] * live_ref[at, :]
        high = index_ref[at, :] // LOW
        high_ref[at, :] = high.astype(f32)
        low_ref[at, :] = (index_ref[at, :] - high * LOW).astype(f32)
    copies[3].wait()
    copies[4].wait()

    def group(start, steps):
        lefts, rights = [], []
        for i in range(steps):
            t = start + i
            values = jnp.where(is_observed, row_of(obs_ref, t), tile_of(design_ref, t))
            scaled = values * row_of(weight_ref, t)
            products = [pick_rows(scaled, m) * pick_rows(values, n) for m, n in zip(lefts_of, rights_of)]
            high, middle, low = split3(products[2])
            parts = split3(jnp.concatenate(products[:2], 0)) + [jnp.where(first_half, high, middle), low]
            block = jnp.concatenate(parts, 0).astype(bf16)
            packed = spread_row(high_ref[pl.ds(t, 1), :], 2 * SUB)
            masks = [is_equal(packed, jnp.full((), h, bf16)) for h in range(highs)]
            repeats = block.shape[0] // (2 * SUB)
            lefts.append(jnp.concatenate([block * jnp.concatenate([mask] * repeats, 0) for mask in masks], 0))
            rights.append(onehot(low_ref[pl.ds(t, 1), :], LOW))
        got = contract(jnp.concatenate(lefts, 1), jnp.concatenate(rights, 1))
        if steps == tiles:
            total[...] = got
        else:
            total[...] += got

    over_steps(tiles, group)
    height = total.shape[0] // highs
    wide, half_tile = 2 * SUB, SUB // 2
    for h in range(highs):
        block = total[h * height : (h + 1) * height, :]
        tail = block[3 * wide :]
        summed = sum_parts(block, wide)
        rest = tail[0:half_tile] + tail[half_tile : 2 * half_tile] + tail[2 * half_tile : 3 * half_tile]
        for half in range(LOW // LANES):
            cols = slice(half * LANES, (half + 1) * LANES)
            out_ref[0:wide, h * (LOW // LANES) + half, :] = summed[:, cols]
            out_ref[wide:SIGNALS, h * (LOW // LANES) + half, :] = rest[:, cols]


def band_kernel(live_ref, phase_ref, axis_ref, weight_ref, knot_ref, out_ref, scaled_ref, moments):
    tiles, shards = phase_ref.shape[0], moments.shape[1]
    rep = tiles // shards
    scaled_ref[...] = weight_ref[...] * live_ref[...]
    rows = moments.shape[0]
    power = iota((SUB, LANES), 0)
    other = jnp.maximum(6 - power, 0)
    lefts_of = patterns([PAIRS[q % 6][0] for q in range(24)])
    rights_of = patterns([PAIRS[q % 6][1] for q in range(24)])
    powers_of = patterns([q // 6 for q in range(rows)])

    def left_of(t):
        u = row_of(phase_ref, t)
        r = 1.0 - u
        powers = jnp.ones((SUB, LANES), f32)
        for base, exponent in ((u, power), (r, other)):
            squared = base * base
            for bit, factor in ((1, base), (2, squared), (4, squared * squared)):
                powers = powers * jnp.where((exponent & bit) != 0, factor, 1.0)
        axes = tile_of(axis_ref, t)
        scaled = axes * row_of(scaled_ref, t)
        products = [pick_rows(scaled, x) * pick_rows(axes, y) for x, y in zip(lefts_of, rights_of)]
        return stacked_parts([products[i % 3] * pick_rows(powers, p) for i, p in enumerate(powers_of)])

    def group(start, steps):
        add_blocks(moments, start, steps, rep, rows, left_of, knot_ref)

    if rep > math.gcd(tiles, 64):
        moments[...] = jnp.zeros_like(moments)
    over_steps(tiles, group)
    table = bernstein_products()
    for n in range(6):
        parts = [moments[p * 6 + n] for p in range(7)]

        def product(i, j):
            return sum(c * part for c, part in zip(table[i, j], parts) if c)

        for delta in range(4):
            running = product(3 - delta, 3)
            for j in reversed(range(3 - delta)):
                running = product(j, j + delta) + shift_up(running, 1)
            out_ref[delta * 6 + n] = running


def halo_rows():
    return -(-QUANTITIES // PER_ROW)


def pack(source_ref, index, q, message_ref, packed):
    parts = message_ref.shape[0]
    owned = source_ref.shape[1] // parts
    for p in range(parts):
        message_ref[p, q * owned : (q + 1) * owned, :] = source_ref[index, p * owned : (p + 1) * owned, :]
    if parts == 1:
        return packed
    row, lane = iota((SUB, LANES), 0), iota((SUB, LANES), 1)
    blank = jnp.zeros((SUB - parts + 1, LANES), f32)
    after = jnp.concatenate([source_ref[index, pl.ds(owned, parts - 1, stride=owned), :], blank], 0)
    before = jnp.concatenate([source_ref[index, pl.ds(owned - 1, parts - 1, stride=owned), :], blank], 0)
    before = pltpu.roll(before, 1, 0)
    edge = jnp.where(lane < LANES // 2, after, jnp.where(row == 0, 0.0, before))
    place, slot = q // PER_ROW, q % PER_ROW
    width = 2 * REACH
    edge = pltpu.roll(edge, (REACH + width * slot) % LANES, 1)
    mine = (lane >= width * slot) & (lane < width * (slot + 1))
    return [jnp.where(mine, edge, row_) if i == place else row_ for i, row_ in enumerate(packed)]


def resid_kernel(
    mine_ref, other_ref, band_ref, live_ref, design_ref, obs_ref, weight_ref, index_ref, phase_ref, axis_ref, knot_ref,
    params_ref, resid_ref, message_ref, tiled, scaled_ref, moments, solved_ref, rhs_ref,
):
    tiles, shards = obs_ref.shape[0], moments.shape[1]
    rep = tiles // shards
    by_tile(design_ref, tiled)
    solved = solve_small([mine_ref[q] + other_ref[q] for q in range(SIGNALS)])
    blocks = SRC_DEV // LANES
    for m in range(5):
        solved_ref[m] = solved[m]
        for b in range(blocks):
            params_ref[m : m + 1, b * LANES : (b + 1) * LANES] = solved[m][b : b + 1, :]
    rows = moments.shape[0]
    axes_of = patterns([q % 3 for q in range(rows)])
    weights_of = [
        [per_sublane([CUBICS[min(q // 3, 3)][c] / 6.0 for q in range(i, i + SUB)], f32) for c in range(4)]
        for i in range(0, rows, SUB)
    ]

    def left_of(t):
        u = row_of(phase_ref, t)
        r = 1.0 - u
        u2, r2 = u * u, r * r
        cubes = [r2 * r, r2 * u, r * u2, u2 * u]
        axes = tile_of(axis_ref, t)
        scaled = axes * row_of(scaled_ref, t)
        return stacked_parts(
            [pick_rows(scaled, x) * sum(c * m for c, m in zip(w, cubes)) for x, w in zip(axes_of, weights_of)]
        )

    def group(start, steps):
        for part in range(steps // SUB):
            at = pl.ds(start + part * SUB, SUB)
            live = live_ref[at, :]
            index = index_ref[at, :]
            block_of = index // LANES
            lane_of = index - block_of * LANES
            hits = [block_of == b for b in range(blocks)]
            fitted = jnp.zeros((SUB, LANES), f32)
            for m in range(5):
                picked = jnp.zeros((SUB, LANES), f32)
                for b in range(blocks):
                    table = jnp.broadcast_to(solved_ref[m, b : b + 1, :], (SUB, LANES))
                    picked = jnp.where(hits[b], jnp.take_along_axis(table, lane_of, axis=1), picked)
                fitted = fitted + tiled[at, m, :] * picked
            resid = live * (obs_ref[at, :] - fitted)
            resid_ref[at, :] = resid
            scaled_ref[at, :] = weight_ref[at, :] * live * resid
        add_blocks(moments, start, steps, rep, rows, left_of, knot_ref)

    if rep > math.gcd(tiles, 64):
        moments[...] = jnp.zeros_like(moments)
    over_steps(tiles, group)
    parts = message_ref.shape[0]
    packed = [jnp.zeros((SUB, LANES), f32)] * halo_rows()
    for x in range(3):
        running = moments[9 + x]
        for j in reversed(range(3)):
            running = moments[j * 3 + x] + shift_up(running, 1)
        rhs_ref[x] = running
        packed = pack(rhs_ref, x, x, message_ref, packed)
    for q in range(band_ref.shape[0]):
        packed = pack(band_ref, q, 3 + q, message_ref, packed)
    first = QUANTITIES * (shards // parts)
    for p in range(parts):
        for i, row in enumerate(packed):
            message_ref[p, first + i : first + i + 1, :] = row[p : p + 1]


def solve_kernel(place_ref, sums_ref, out_ref):
    owned = out_ref.shape[0] // 4
    ring = -(-(owned + 2) // SUB) * SUB
    order = {pair: n for n, pair in enumerate(PAIRS)}
    row, lane = iota((ring, LANES), 0), iota((ring, LANES), 1)
    inside = row < owned
    after = (row == owned) & (lane < REACH)
    before = (row == ring - 1) & (lane >= LANES - REACH)
    edge = (place_ref[0] == place_ref[1] - 1).astype(jnp.int32)
    known = jnp.where(after & (jnp.full((ring, LANES), edge, jnp.int32) == 1), 0.0, 1.0)

    def load(q):
        rows = sums_ref[q * owned : (q + 1) * owned, :]
        rest = sums_ref[pl.ds(QUANTITIES * owned + q // PER_ROW, 1), :]
        rest = jnp.broadcast_to(rest, (ring - owned, LANES))
        rest = pltpu.roll(rest, (-(REACH + 2 * REACH * (q % PER_ROW))) % LANES, 1)
        return jnp.where(inside | after | before, jnp.concatenate([rows, rest], 0), 0.0)

    def turn(value, n):
        turned = pltpu.roll(value, n % LANES, 1)
        if n > 0:
            return jnp.where(lane < n, pltpu.roll(turned, 1, 0), turned)
        return jnp.where(lane >= LANES + n, pltpu.roll(turned, ring - 1, 0), turned)

    loaded = [load(q) for q in range(QUANTITIES)]

    def band(delta, x, y):
        return loaded[3 + delta * 6 + order[min(x, y), max(x, y)]]

    rhs = loaded[:3]
    scale = [relax_step / (att_ridge + band(0, x, x)) * known for x in range(3)]
    coefs = [rhs[x] * scale[x] for x in range(3)]
    for _ in range(1, ITERS):
        ahead = {(y, delta): turn(coefs[y], -delta) for y in range(3) for delta in range(1, 4)}
        fresh = []
        for x in range(3):
            normal = att_ridge * coefs[x]
            for y in range(3):
                normal = normal + band(0, x, y) * coefs[y]
            for delta in range(1, 4):
                for y in range(3):
                    normal = normal + band(delta, x, y) * ahead[y, delta]
                normal = normal + turn(sum(band(delta, x, y) * coefs[y] for y in range(3)), delta)
            fresh.append(coefs[x] + scale[x] * (rhs[x] - normal))
        coefs = fresh
    for x in range(3):
        for r in range(owned):
            out_ref[pl.ds(r * 4 + x, 1), :] = coefs[x][r : r + 1]


def prepare_kernel(_, live_ref, phase_ref, axis_ref, out_ref, tiled):
    by_tile(axis_ref, tiled)

    def group(start, steps):
        for part in range(steps // SUB):
            at = pl.ds(start + part * SUB, SUB)
            basis = [b * live_ref[at, :] for b in spline_basis(phase_ref[at, :])]
            for x in range(3):
                along = tiled[at, x, :]
                for j in range(4):
                    out_ref[x * 4 + j, at, :] = along * basis[j]

    over_steps(phase_ref.shape[0], group)


def predict_kernel(place_ref, coef_ref, factor_ref, resid_ref, knot_ref, att_ref, out_ref, windows):
    tiles, shards = resid_ref.shape[0], coef_ref.shape[0]
    rep = tiles // shards
    for x in range(3):
        coefs = coef_ref[:, x, :]
        for j in range(4):
            windows[x * 4 + j] = coefs if j == 0 else shift_down(coefs, j)
        att_ref[x : x + 1, :] = windows[x * 4, pl.ds(place_ref[0], 1), :]
    row = iota((SUB, LANES), 0)

    def group(start, steps):
        for part in range(steps // SUB):
            at = pl.ds(start + part * SUB, SUB)
            knots = knot_ref[at, :]
            first = (start + part * SUB) // rep
            left = resid_ref[at, :]
            for q in range(12):
                table = jnp.broadcast_to(windows[q, pl.ds(first, 1), :], (SUB, LANES))
                for k in range(1, SUB // rep):
                    later = jnp.broadcast_to(windows[q, pl.ds(first + k, 1), :], (SUB, LANES))
                    table = jnp.where(row >= k * rep, later, table)
                left = left - factor_ref[q, at, :] * jnp.take_along_axis(table, knots, axis=1)
            out_ref[at, :] = left

    over_steps(tiles, group)


BOTH = ("src", "ccd")
SMEM = pl.BlockSpec(memory_space=pltpu.SMEM)
VMEM = pl.BlockSpec(memory_space=pltpu.VMEM)
HBM = pl.BlockSpec(memory_space=pltpu.HBM)


def call(kernel, name, scalars, arrays, outs, scratch, space=VMEM):
    return pl.pallas_call(
        kernel,
        name=name,
        out_shape=outs,
        in_specs=[SMEM] * len(scalars) + [space] * len(arrays),
        out_specs=jax.tree.map(lambda _: VMEM, outs),
        scratch_shapes=scratch,
        compiler_params=pltpu.CompilerParams(vmem_limit_bytes=8 << 20),
    )(*scalars, *arrays)


def swapped(value, axis, bit):
    size = lax.axis_size(axis)
    return lax.ppermute(value, axis, [(i, i ^ bit) for i in range(size)])


def summed_over(value, axis):
    size = lax.axis_size(axis)
    if size & (size - 1):
        return lax.psum(value, axis)
    bit = 1
    while bit < size:
        value = value + swapped(value, axis, bit)
        bit *= 2
    return value


def halved(value, mask, keep):
    pair = value.reshape((2, value.shape[0] // 2) + value.shape[1:])
    kept = lax.dynamic_index_in_dim(pair, keep, 0, False)
    sent = lax.dynamic_index_in_dim(pair, 1 - keep, 0, False)
    return kept + swapped(sent, BOTH, mask)


def doubled(value, mask, keep):
    other = swapped(value, BOTH, mask)
    first = jnp.where(keep == 0, value, other)
    second = jnp.where(keep == 0, other, value)
    return jnp.concatenate([first, second], 0)


def on_device(design, observed, weight, phase_frac, axis_factors, source_index, knot_index, counts):
    row_count = observed.shape[0]
    tiles = row_count // LANES
    shards = lax.axis_size("src")
    obs, w, phase, index, knots = (
        a.reshape(tiles, LANES) for a in (observed, weight, phase_frac, source_index, knot_index)
    )
    tiled = pltpu.VMEM((tiles, SUB, LANES), f32)
    dense = pltpu.VMEM((tiles, LANES), f32)
    blocks = SRC_DEV // LANES
    moments, live = call(
        source_kernel, "source_sums", [],
        [pltpu.with_memory_space_constraint(a, pltpu.HBM) for a in (counts, design, obs, w, index)],
        (jax.ShapeDtypeStruct((SIGNALS, blocks, LANES), f32), jax.ShapeDtypeStruct((tiles, LANES), f32)),
        [
            pltpu.SMEM(counts.shape, jnp.int32), pltpu.VMEM(design.shape, f32), dense, dense,
            pltpu.VMEM((tiles, LANES), jnp.int32), pltpu.SemaphoreType.DMA((5,)), dense, dense,
            pltpu.VMEM((SRC_DEV // LOW * 64, LOW), f32),
        ],
        HBM,
    )
    band = call(
        band_kernel, "band_sums", [], [live, phase, axis_factors, w, knots],
        jax.ShapeDtypeStruct((24, shards, KNOT_DEV), f32),
        [dense, pltpu.VMEM((48, shards, KNOT_DEV), f32)],
    )
    if lax.axis_size("ccd") == 2:
        other = swapped(moments, "ccd", 1)
    else:
        moments = summed_over(moments, "ccd")
        other = jnp.zeros_like(moments)
    fast = lax.axis_size("ccd") == 2 and shards >= 4 and shards & (shards - 1) == 0
    parts = 4 if fast else 1
    owned = shards // parts
    message_rows = -(-(QUANTITIES * owned + halo_rows()) // SUB) * SUB
    params, resid, message = call(
        resid_kernel, "residuals", [],
        [moments, other, band, live, design, obs, w, index, phase, axis_factors, knots],
        (
            jax.ShapeDtypeStruct((5, SRC_DEV), f32),
            jax.ShapeDtypeStruct((tiles, LANES), f32),
            jax.ShapeDtypeStruct((parts, message_rows, LANES), f32),
        ),
        [tiled, dense, pltpu.VMEM((16, shards, KNOT_DEV), f32), pltpu.VMEM((5, blocks, LANES), f32),
         pltpu.VMEM((3, shards, KNOT_DEV), f32)],
    )
    factors = call(
        prepare_kernel, "prepare", [], [message, live, phase, axis_factors],
        jax.ShapeDtypeStruct((12, tiles, LANES), f32), [tiled],
    )
    place = lax.axis_index("src")
    if fast:
        upper = lax.axis_index("ccd")
        for shift in range(shards.bit_length() - 1):
            upper = upper ^ ((place >> shift) & 1)
        lower = place & 1
        sums = halved(halved(message, 1, upper), 3, lower)[0]
        bit = 2
        while bit < shards:
            sums = sums + swapped(sums, BOTH, 2 * bit + 1)
            bit *= 2
        part = 2 * upper + lower
    else:
        sums = summed_over(summed_over(message[0], "ccd"), "src")
        part = jnp.zeros_like(place)
    coefs = call(
        solve_kernel, "attitude", [jnp.stack([part, jnp.full_like(part, parts)])], [sums],
        jax.ShapeDtypeStruct((owned * 4, LANES), f32), [],
    )
    if fast:
        coefs = doubled(doubled(coefs, 3, lower), 1, upper)
    attitude, residual = call(
        predict_kernel, "predict", [place.reshape(1)], [coefs.reshape(shards, 4, LANES), factors, resid, knots],
        (jax.ShapeDtypeStruct((3, KNOT_DEV), f32), jax.ShapeDtypeStruct((tiles, LANES), f32)),
        [pltpu.VMEM((12, shards, KNOT_DEV), f32)],
    )
    return params, attitude, residual.reshape(row_count)


def solution(mesh):
    rows = P(("src", "ccd"))
    wide = P(None, ("src", "ccd"))
    in_specs = (wide, rows, rows, rows, wide, rows, rows, P("src", "ccd", None))
    out_specs = (P(None, "src"), P(None, "src"), rows)
    return jax.shard_map(on_device, mesh=mesh, in_specs=in_specs, out_specs=out_specs, check_vma=False)
```

```python
import math

import jax
import jax.numpy as jnp
from jax import lax
from jax.experimental import pallas as pl
from jax.experimental.pallas import tpu as pltpu
from jax.sharding import PartitionSpec as P

SRC_DEV = 1024
KNOT_DEV = 128
ITERS = 3
LANES = 128
SUB = 8
LOW = 256
QUANTITIES = 3 + 4 * 6
REACH = 3 * (ITERS - 1)
WINDOW = 2 * REACH
CUBICS = [(1.0, 0.0, 0.0, 0.0), (4.0, 12.0, 6.0, 1.0), (1.0, 6.0, 12.0, 4.0), (0.0, 0.0, 0.0, 1.0)]
SIGNALS = 15 + 5
PAIRS = [(x, y) for x in range(3) for y in range(x, 3)]

src_ridge = 1.0
att_ridge = 1.0
relax_step = 0.15

f32 = jnp.float32
bf16 = jnp.bfloat16


def bernstein_products():
    table = {}
    for i in range(4):
        for j in range(i, 4):
            coefs = [0.0] * 7
            for p in range(4):
                for q in range(4):
                    coefs[p + q] += CUBICS[i][p] * CUBICS[j][q] / 36.0
            table[i, j] = coefs
    return table


def split2(value):
    high = value.astype(bf16).astype(f32)
    return [high, value - high]


def split3(value):
    high = value.astype(bf16).astype(f32)
    rest = value - high
    middle = rest.astype(bf16).astype(f32)
    return [high, middle, rest - middle]


def spline_basis(phase_rows):
    remain = 1.0 - phase_rows
    square = phase_rows * phase_rows
    cube_term = square * phase_rows
    return [
        remain * remain * remain / 6.0,
        (3.0 * cube_term - 6.0 * square + 4.0) / 6.0,
        (-3.0 * cube_term + 3.0 * square + 3.0 * phase_rows + 1.0) / 6.0,
        cube_term / 6.0,
    ]


def solve_small(moments):
    matrix = {}
    position = 0
    for m in range(5):
        for n in range(m, 5):
            matrix[m, n] = moments[position] + (src_ridge if m == n else 0.0)
            position += 1
    factor = {}
    inverse = {}
    for j in range(5):
        for i in range(j, 5):
            running = matrix[j, i]
            for k in range(j):
                running = running - factor[i, k] * factor[j, k]
            if i == j:
                factor[j, j] = jnp.sqrt(running)
                inverse[j] = 1.0 / factor[j, j]
            else:
                factor[i, j] = running * inverse[j]
    forward = []
    for i in range(5):
        running = moments[15 + i]
        for k in range(i):
            running = running - factor[i, k] * forward[k]
        forward.append(running * inverse[i])
    solved = [None] * 5
    for i in reversed(range(5)):
        running = forward[i]
        for k in range(i + 1, 5):
            running = running - factor[k, i] * solved[k]
        solved[i] = running * inverse[i]
    return solved


def iota(shape, axis):
    return lax.broadcasted_iota(jnp.int32, shape, axis)


def over_steps(tiles, body):
    steps = math.gcd(tiles, 64)
    if steps == tiles:
        body(0, steps)
        return

    def one(g, _):
        body(pl.multiple_of(g * steps, steps), steps)
        return 0

    lax.fori_loop(0, tiles // steps, one, 0)


def spread_row(index_row, count):
    packed = jnp.broadcast_to(index_row, (2 * SUB, LANES)).astype(bf16)
    return jnp.concatenate([packed] * (count // (2 * SUB)), 0)


def is_equal(left, right):
    return jnp.where(left == right, jnp.ones((), bf16), jnp.zeros((), bf16))


def onehot(index_row, count):
    return is_equal(iota((count, LANES), 0).astype(f32).astype(bf16), spread_row(index_row, count))


def by_tile(wide_ref, tiled_ref):
    rows = wide_ref.shape[0]
    for t in range(tiled_ref.shape[0] // SUB):
        tiled_ref[t * SUB : t * SUB + rows, :] = wide_ref[:, t * LANES : (t + 1) * LANES]


def by_group(tiles):
    return range(0, tiles, SUB)


def across(start, row):
    return pl.ds(start * SUB + row, SUB, stride=SUB)


def tile_of(tiled_ref, t):
    return tiled_ref[pl.ds(t * SUB, SUB), :]


def low_bits(index, size):
    return index >> (size.bit_length() - 1), index & (size - 1)


def row_of(ref, t):
    return jnp.broadcast_to(ref[pl.ds(t, 1), :], (SUB, LANES))


def per_sublane(values, kind):
    row = iota((SUB, LANES), 0)
    out = jnp.full((SUB, LANES), values[0], kind)
    for s in range(1, SUB):
        if values[s] != values[0]:
            out = jnp.where(row == s, jnp.full((SUB, LANES), values[s], kind), out)
    return out


def pick_rows(value, pattern):
    return jnp.take_along_axis(value, pattern, axis=0)


def patterns(values):
    values = list(values) + [0] * (-len(values) % SUB)
    return [per_sublane(values[i : i + SUB], jnp.int32) for i in range(0, len(values), SUB)]


def stacked_parts(values, split):
    parts = split(jnp.concatenate(values, 0))
    if len(parts) * parts[0].shape[0] % (2 * SUB):
        parts.append(jnp.zeros((SUB, LANES), f32))
    return jnp.concatenate(parts, 0).astype(bf16)


def sum_parts(value, rows, count):
    return sum(value[i * rows : (i + 1) * rows] for i in range(count))


def add_blocks(moments_ref, start, steps, rep, rows, count, left_of, knot_ref):
    per_block = min(rep, steps)
    for b in range(steps // per_block):
        lefts, rights = [], []
        for i in range(b * per_block, (b + 1) * per_block):
            lefts.append(left_of(start + i))
            rights.append(onehot(knot_ref[pl.ds(start + i, 1), :].astype(f32), KNOT_DEV))
        got = contract(jnp.concatenate(lefts, 1), jnp.concatenate(rights, 1))
        summed = sum_parts(got, rows, count)
        where_to = (start + b * per_block) // rep
        where_to = pl.ds(where_to * rows, rows)
        if rep <= steps:
            moments_ref[where_to, :] = summed
        else:
            moments_ref[where_to, :] += summed


def contract(left, right):
    return lax.dot_general(left, right, (((1,), (1,)), ((), ())), preferred_element_type=f32)


def shift_up(value, n):
    turned = pltpu.roll(value, n, 1)
    before = pltpu.roll(turned, 1, 0)
    before = jnp.where(iota(value.shape, 0) == 0, 0.0, before)
    return jnp.where(iota(value.shape, 1) < n, before, turned)


def shift_down(value, n):
    turned = pltpu.roll(value, LANES - n, 1)
    after = pltpu.roll(turned, value.shape[0] - 1, 0)
    after = jnp.where(iota(value.shape, 0) == value.shape[0] - 1, 0.0, after)
    return jnp.where(iota(value.shape, 1) >= LANES - n, after, turned)


def source_kernel(
    counts_hbm, design_hbm, obs_hbm, weight_hbm, index_hbm, out_ref, live_ref,
    counts_ref, design_ref, obs_ref, weight_ref, index_ref, sems, low_ref, high_ref, total, tiled,
):
    tiles = obs_ref.shape[0]
    shards = counts_ref.shape[2]
    rep = tiles // shards
    copies = [
        pltpu.make_async_copy(src, dst, sems.at[i])
        for i, (src, dst) in enumerate(
            [(counts_hbm, counts_ref), (weight_hbm, weight_ref), (index_hbm, index_ref), (obs_hbm, obs_ref),
             (design_hbm, design_ref)]
        )
    ]
    for copy in copies:
        copy.start()
    if math.gcd(tiles, 64) != tiles:
        total[...] = jnp.zeros_like(total)
    highs = SRC_DEV // LOW
    pairs = [(m, n) for m in range(5) for n in range(m, 5)] + [(m, 5) for m in range(5)]
    pairs += pairs[2 * SUB :]
    lefts_of = patterns([m for m, _ in pairs])
    rights_of = patterns([n for _, n in pairs])
    first_half = iota((SUB, LANES), 0) < SUB // 2
    copies[0].wait()
    slots = iota((rep, LANES), 0) * LANES + iota((rep, LANES), 1)
    for d in range(shards):
        live_ref[pl.ds(d * rep, rep), :] = (slots < counts_ref[0, 0, d]).astype(f32)
    copies[1].wait()
    copies[2].wait()
    for start in by_group(tiles):
        at = pl.ds(start, SUB)
        weight_ref[at, :] = weight_ref[at, :] * live_ref[at, :]
        high, low = low_bits(index_ref[at, :], LOW)
        high_ref[at, :] = high.astype(f32)
        low_ref[at, :] = low.astype(f32)
    copies[3].wait()
    copies[4].wait()
    by_tile(design_ref, tiled)
    for start in by_group(tiles):
        tiled[across(start, 5), :] = obs_ref[pl.ds(start, SUB), :]

    def group(start, steps):
        lefts, rights = [], []
        for i in range(steps):
            t = start + i
            values = tile_of(tiled, t)
            scaled = values * row_of(weight_ref, t)
            products = [pick_rows(scaled, m) * pick_rows(values, n) for m, n in zip(lefts_of, rights_of)]
            high, middle, low = split3(products[2])
            parts = split3(jnp.concatenate(products[:2], 0)) + [jnp.where(first_half, high, middle), low]
            block = jnp.concatenate(parts, 0).astype(bf16)
            packed = spread_row(high_ref[pl.ds(t, 1), :], 2 * SUB)
            masks = [is_equal(packed, jnp.full((), h, bf16)) for h in range(highs)]
            repeats = block.shape[0] // (2 * SUB)
            lefts.append(jnp.concatenate([block * jnp.concatenate([mask] * repeats, 0) for mask in masks], 0))
            rights.append(onehot(low_ref[pl.ds(t, 1), :], LOW))
        got = contract(jnp.concatenate(lefts, 1), jnp.concatenate(rights, 1))
        if steps == tiles:
            total[...] = got
        else:
            total[...] += got

    over_steps(tiles, group)
    height = total.shape[0] // highs
    wide, half_tile = 2 * SUB, SUB // 2
    for h in range(highs):
        block = total[h * height : (h + 1) * height, :]
        tail = block[3 * wide :]
        summed = sum_parts(block, wide, 3)
        rest = tail[0:half_tile] + tail[half_tile : 2 * half_tile] + tail[2 * half_tile : 3 * half_tile]
        for half in range(LOW // LANES):
            cols = slice(half * LANES, (half + 1) * LANES)
            out_ref[0:wide, h * (LOW // LANES) + half, :] = summed[:, cols]
            out_ref[wide:SIGNALS, h * (LOW // LANES) + half, :] = rest[:, cols]


def band_kernel(live_ref, phase_ref, axis_ref, weight_ref, knot_ref, out_ref, tiled, powers_ref, moments):
    tiles, shards = phase_ref.shape[0], out_ref.shape[0] // 24
    rep = tiles // shards
    by_tile(axis_ref, tiled)
    rows = moments.shape[0] // shards
    lefts_of = patterns([PAIRS[q % 6][0] for q in range(24)])
    rights_of = patterns([PAIRS[q % 6][1] for q in range(24)])
    powers_of = patterns([q // 6 if q < 42 else 0 for q in range(rows)])
    for start in by_group(tiles):
        at = pl.ds(start, SUB)
        u = phase_ref[at, :]
        r = 1.0 - u
        u2, r2 = u * u, r * r
        u3, r3 = u2 * u, r2 * r
        w = weight_ref[at, :] * live_ref[at, :]
        u3w, r3w = u3 * w, r3 * w
        powers = [r3w * r3, r3w * (r2 * u), r3w * (r * u2), r3w * u3, u3w * (r2 * u), u3w * (r * u2), u3w * u3]
        for p in range(7):
            powers_ref[across(start, p), :] = powers[p]

    def left_of(t):
        axes = tile_of(tiled, t)
        powers = tile_of(powers_ref, t)
        products = [pick_rows(axes, x) * pick_rows(axes, y) for x, y in zip(lefts_of, rights_of)]
        return stacked_parts([products[i % 3] * pick_rows(powers, p) for i, p in enumerate(powers_of)], split2)

    def group(start, steps):
        add_blocks(moments, start, steps, rep, rows, 2, left_of, knot_ref)

    if rep > math.gcd(tiles, 64):
        moments[...] = jnp.zeros_like(moments)
    over_steps(tiles, group)
    table = bernstein_products()
    for n in range(6):
        parts = [moments[pl.ds(p * 6 + n, shards, stride=rows), :] for p in range(7)]

        def product(i, j):
            return sum(c * part for c, part in zip(table[i, j], parts) if c)

        for delta in range(4):
            running = product(3 - delta, 3)
            for j in reversed(range(3 - delta)):
                running = product(j, j + delta) + shift_up(running, 1)
            to = (delta * 6 + n) * shards
            out_ref[to : to + shards, :] = running


def halo_rows():
    return 1 + (QUANTITIES - 3) // SUB


def slots_of(value, shift):
    return pltpu.roll(value, shift, 1, stride=WINDOW, stride_axis=0)


def pack(source_ref, first, count, row, message_ref):
    parts, shards = message_ref.shape[0], source_ref.shape[0] // count
    owned = shards // parts
    lane, slot = iota((SUB, LANES), 1), iota((SUB, LANES), 0)
    mine = (lane >= WINDOW * slot) & (lane < WINDOW * (slot + 1)) & (slot < count)
    zero = jnp.zeros((SUB, LANES), f32)
    for base in range(0, count, SUB):
        for q in range(base, min(base + SUB, count)):
            for p in range(parts):
                at = q * shards + p * owned
                to = (first + q) * owned
                message_ref[p, to : to + owned, :] = source_ref[at : at + owned, :]
        for p in range(parts):
            taken = min(count, SUB)

            def edge(r):
                got = source_ref[pl.ds(base * shards + r, taken, stride=shards), :]
                return got if taken == SUB else jnp.concatenate([got, zero[taken:]], 0)

            after = edge((p + 1) * owned) if p < parts - 1 else zero
            before = edge(p * owned - 1) if p else zero
            packed = slots_of(jnp.where(lane < LANES // 2, after, before), REACH)
            to = QUANTITIES * owned + row + base // SUB
            message_ref[p, to : to + 1, :] = jnp.sum(jnp.where(mine, packed, 0.0), 0, keepdims=True)


def resid_kernel(
    mine_ref, other_ref, band_ref, live_ref, design_ref, obs_ref, weight_ref, index_ref, phase_ref, axis_ref, knot_ref,
    params_ref, resid_ref, message_ref, tiled, tiled_axis, splines_ref, moments, solved_ref, rhs_ref,
):
    tiles, shards = obs_ref.shape[0], rhs_ref.shape[0] // 3
    rep = tiles // shards
    by_tile(design_ref, tiled)
    by_tile(axis_ref, tiled_axis)
    solved = solve_small([mine_ref[q] + other_ref[q] for q in range(SIGNALS)])
    blocks = SRC_DEV // LANES
    for m in range(5):
        solved_ref[m] = solved[m]
        for b in range(blocks):
            params_ref[m : m + 1, b * LANES : (b + 1) * LANES] = solved[m][b : b + 1, :]
    rows = moments.shape[0] // shards
    axes_of = patterns([q % 3 for q in range(rows)])
    splines_of = patterns([min(q // 3, 3) for q in range(rows)])

    def left_of(t):
        axes = tile_of(tiled_axis, t)
        splines = tile_of(splines_ref, t)
        return stacked_parts([pick_rows(axes, x) * pick_rows(splines, j) for x, j in zip(axes_of, splines_of)], split3)

    def group(start, steps):
        for part in range(steps // SUB):
            at = pl.ds(start + part * SUB, SUB)
            live = live_ref[at, :]
            block_of, lane_of = low_bits(index_ref[at, :], LANES)
            hits = [block_of == b for b in range(blocks)]
            left = obs_ref[at, :]
            for m in range(5):
                for b in range(blocks):
                    table = jnp.broadcast_to(solved_ref[m, b : b + 1, :], (SUB, LANES))
                    found = jnp.take_along_axis(table, lane_of, axis=1)
                    picked = jnp.where(hits[b], found, picked) if b else found
                left = left - tiled[across(start + part * SUB, m), :] * picked
            resid = live * left
            resid_ref[at, :] = resid
            scaled = weight_ref[at, :] * resid
            for j, basis in enumerate(spline_basis(phase_ref[at, :])):
                splines_ref[across(start + part * SUB, j), :] = basis * scaled
        add_blocks(moments, start, steps, rep, rows, 3, left_of, knot_ref)

    if rep > math.gcd(tiles, 64):
        moments[...] = jnp.zeros_like(moments)
    over_steps(tiles, group)
    for x in range(3):
        running = moments[pl.ds(9 + x, shards, stride=rows), :]
        for j in reversed(range(3)):
            running = moments[pl.ds(j * 3 + x, shards, stride=rows), :] + shift_up(running, 1)
        rhs_ref[x * shards : (x + 1) * shards, :] = running
    pack(rhs_ref, 0, 3, 0, message_ref)
    pack(band_ref, 3, QUANTITIES - 3, 1, message_ref)


def solve_kernel(place_ref, sums_ref, out_ref, edges_ref):
    owned = out_ref.shape[0] // 4
    ring = -(-(owned + 2) // SUB) * SUB
    order = {pair: n for n, pair in enumerate(PAIRS)}
    row, lane = iota((ring, LANES), 0), iota((ring, LANES), 1)
    inside = row < owned
    after = (row == owned) & (lane < REACH)
    before = (row == ring - 1) & (lane >= LANES - REACH)
    edge = (place_ref[0] == place_ref[1] - 1).astype(jnp.int32)
    known = jnp.where(after & (jnp.full((ring, LANES), edge, jnp.int32) == 1), 0.0, 1.0)

    back = LANES - REACH - WINDOW * (SUB - 1)
    for i in range(halo_rows()):
        packed = sums_ref[QUANTITIES * owned + i : QUANTITIES * owned + i + 1, :]
        edges_ref[i * SUB : (i + 1) * SUB, :] = slots_of(jnp.broadcast_to(packed, (SUB, LANES)), back)

    def load(q):
        rows = sums_ref[q * owned : (q + 1) * owned, :]
        place = q if q < 3 else q + SUB - 3
        slot = place // SUB * SUB + SUB - 1 - place % SUB
        rest = jnp.broadcast_to(edges_ref[slot : slot + 1, :], (ring - owned, LANES))
        return jnp.where(inside | after | before, jnp.concatenate([rows, rest], 0), 0.0)

    def turn(value, n):
        turned = pltpu.roll(value, n % LANES, 1)
        if n > 0:
            return jnp.where(lane < n, pltpu.roll(turned, 1, 0), turned)
        return jnp.where(lane >= LANES + n, pltpu.roll(turned, ring - 1, 0), turned)

    loaded = [load(q) for q in range(QUANTITIES)]

    def band(delta, x, y):
        return loaded[3 + delta * 6 + order[min(x, y), max(x, y)]]

    rhs = loaded[:3]
    scale = [relax_step / (att_ridge + band(0, x, x)) * known for x in range(3)]
    coefs = [rhs[x] * scale[x] for x in range(3)]
    for _ in range(1, ITERS):
        ahead = {(y, delta): turn(coefs[y], -delta) for y in range(3) for delta in range(1, 4)}
        fresh = []
        for x in range(3):
            normal = att_ridge * coefs[x]
            for y in range(3):
                normal = normal + band(0, x, y) * coefs[y]
            for delta in range(1, 4):
                for y in range(3):
                    normal = normal + band(delta, x, y) * ahead[y, delta]
                normal = normal + turn(sum(band(delta, x, y) * coefs[y] for y in range(3)), delta)
            fresh.append(coefs[x] + scale[x] * (rhs[x] - normal))
        coefs = fresh
    for x in range(3):
        for r in range(owned):
            out_ref[pl.ds(r * 4 + x, 1), :] = coefs[x][r : r + 1]


def prepare_kernel(_, live_ref, phase_ref, axis_ref, out_ref, tiled):
    by_tile(axis_ref, tiled)

    def group(start, steps):
        for part in range(steps // SUB):
            at = pl.ds(start + part * SUB, SUB)
            basis = [b * live_ref[at, :] for b in spline_basis(phase_ref[at, :])]
            for x in range(3):
                along = tiled[across(start + part * SUB, x), :]
                for j in range(4):
                    out_ref[x * 4 + j, at, :] = along * basis[j]

    over_steps(phase_ref.shape[0], group)


def predict_kernel(place_ref, coef_ref, factor_ref, resid_ref, knot_ref, att_ref, out_ref, windows):
    tiles, shards = resid_ref.shape[0], coef_ref.shape[0]
    rep = tiles // shards
    for x in range(3):
        coefs = coef_ref[:, x, :]
        for j in range(4):
            windows[x * 4 + j] = coefs if j == 0 else shift_down(coefs, j)
        att_ref[x : x + 1, :] = windows[x * 4, pl.ds(place_ref[0], 1), :]
    row = iota((SUB, LANES), 0)

    def group(start, steps):
        for part in range(steps // SUB):
            at = pl.ds(start + part * SUB, SUB)
            knots = knot_ref[at, :]
            first = (start + part * SUB) // rep
            left = resid_ref[at, :]
            for q in range(12):
                table = jnp.broadcast_to(windows[q, pl.ds(first, 1), :], (SUB, LANES))
                for k in range(1, SUB // rep):
                    later = jnp.broadcast_to(windows[q, pl.ds(first + k, 1), :], (SUB, LANES))
                    table = jnp.where(row >= k * rep, later, table)
                left = left - factor_ref[q, at, :] * jnp.take_along_axis(table, knots, axis=1)
            out_ref[at, :] = left

    over_steps(tiles, group)


BOTH = ("src", "ccd")
SMEM = pl.BlockSpec(memory_space=pltpu.SMEM)
VMEM = pl.BlockSpec(memory_space=pltpu.VMEM)
HBM = pl.BlockSpec(memory_space=pltpu.HBM)


def call(kernel, name, scalars, arrays, outs, scratch, space=VMEM):
    return pl.pallas_call(
        kernel,
        name=name,
        out_shape=outs,
        in_specs=[SMEM] * len(scalars) + [space] * len(arrays),
        out_specs=jax.tree.map(lambda _: VMEM, outs),
        scratch_shapes=scratch,
        compiler_params=pltpu.CompilerParams(vmem_limit_bytes=8 << 20),
    )(*scalars, *arrays)


def swapped(value, axis, bit):
    size = lax.axis_size(axis)
    return lax.ppermute(value, axis, [(i, i ^ bit) for i in range(size)])


def summed_over(value, axis):
    size = lax.axis_size(axis)
    if size & (size - 1):
        return lax.psum(value, axis)
    bit = 1
    while bit < size:
        value = value + swapped(value, axis, bit)
        bit *= 2
    return value


def halved(value, mask, keep):
    pair = value.reshape((2, value.shape[0] // 2) + value.shape[1:])
    kept = lax.dynamic_index_in_dim(pair, keep, 0, False)
    sent = lax.dynamic_index_in_dim(pair, 1 - keep, 0, False)
    return kept + swapped(sent, BOTH, mask)


def doubled(value, mask, keep):
    other = swapped(value, BOTH, mask)
    first = jnp.where(keep == 0, value, other)
    second = jnp.where(keep == 0, other, value)
    return jnp.concatenate([first, second], 0)


def on_device(design, observed, weight, phase_frac, axis_factors, source_index, knot_index, counts):
    row_count = observed.shape[0]
    tiles = row_count // LANES
    shards = lax.axis_size("src")
    obs, w, phase, index, knots = (
        a.reshape(tiles, LANES) for a in (observed, weight, phase_frac, source_index, knot_index)
    )
    tiled = pltpu.VMEM((tiles * SUB, LANES), f32)
    dense = pltpu.VMEM((tiles, LANES), f32)
    blocks = SRC_DEV // LANES
    moments, live = call(
        source_kernel, "source_sums", [],
        [pltpu.with_memory_space_constraint(a, pltpu.HBM) for a in (counts, design, obs, w, index)],
        (jax.ShapeDtypeStruct((SIGNALS, blocks, LANES), f32), jax.ShapeDtypeStruct((tiles, LANES), f32)),
        [
            pltpu.SMEM(counts.shape, jnp.int32), pltpu.VMEM(design.shape, f32), dense, dense,
            pltpu.VMEM((tiles, LANES), jnp.int32), pltpu.SemaphoreType.DMA((5,)), dense, dense,
            pltpu.VMEM((SRC_DEV // LOW * 64, LOW), f32), tiled,
        ],
        HBM,
    )
    band = call(
        band_kernel, "band_sums", [], [live, phase, axis_factors, w, knots],
        jax.ShapeDtypeStruct((24 * shards, KNOT_DEV), f32),
        [tiled, tiled, pltpu.VMEM((shards * 48, KNOT_DEV), f32)],
    )
    if lax.axis_size("ccd") == 2:
        other = swapped(moments, "ccd", 1)
    else:
        moments = summed_over(moments, "ccd")
        other = jnp.zeros_like(moments)
    fast = lax.axis_size("ccd") == 2 and shards >= 4 and shards & (shards - 1) == 0
    parts = 4 if fast else 1
    owned = shards // parts
    message_rows = -(-(QUANTITIES * owned + halo_rows()) // SUB) * SUB
    params, resid, message = call(
        resid_kernel, "residuals", [],
        [moments, other, band, live, design, obs, w, index, phase, axis_factors, knots],
        (
            jax.ShapeDtypeStruct((5, SRC_DEV), f32),
            jax.ShapeDtypeStruct((tiles, LANES), f32),
            jax.ShapeDtypeStruct((parts, message_rows, LANES), f32),
        ),
        [tiled, tiled, tiled, pltpu.VMEM((shards * 16, KNOT_DEV), f32), pltpu.VMEM((5, blocks, LANES), f32),
         pltpu.VMEM((3 * shards, KNOT_DEV), f32)],
    )
    factors = call(
        prepare_kernel, "prepare", [], [message, live, phase, axis_factors],
        jax.ShapeDtypeStruct((12, tiles, LANES), f32), [tiled],
    )
    place = lax.axis_index("src")
    if fast:
        upper = lax.axis_index("ccd")
        for shift in range(shards.bit_length() - 1):
            upper = upper ^ ((place >> shift) & 1)
        lower = place & 1
        sums = halved(halved(message, 1, upper), 3, lower)[0]
        bit = 2
        while bit < shards:
            sums = sums + swapped(sums, BOTH, 2 * bit + 1)
            bit *= 2
        part = 2 * upper + lower
    else:
        sums = summed_over(summed_over(message[0], "ccd"), "src")
        part = jnp.zeros_like(place)
    coefs = call(
        solve_kernel, "attitude", [jnp.stack([part, jnp.full_like(part, parts)])], [sums],
        jax.ShapeDtypeStruct((owned * 4, LANES), f32), [pltpu.VMEM((halo_rows() * SUB, LANES), f32)],
    )
    if fast:
        coefs = doubled(doubled(coefs, 3, lower), 1, upper)
    attitude, residual = call(
        predict_kernel, "predict", [place.reshape(1)], [coefs.reshape(shards, 4, LANES), factors, resid, knots],
        (jax.ShapeDtypeStruct((3, KNOT_DEV), f32), jax.ShapeDtypeStruct((tiles, LANES), f32)),
        [pltpu.VMEM((12, shards, KNOT_DEV), f32)],
    )
    return params, attitude, residual.reshape(row_count)


def solution(mesh):
    rows = P(("src", "ccd"))
    wide = P(None, ("src", "ccd"))
    in_specs = (wide, rows, rows, rows, wide, rows, rows, P("src", "ccd", None))
    out_specs = (P(None, "src"), P(None, "src"), rows)
    return jax.shard_map(on_device, mesh=mesh, in_specs=in_specs, out_specs=out_specs, check_vma=False)
```

```python
import functools
import math

import jax
import jax.numpy as jnp
from jax import lax
from jax.experimental import pallas as pl
from jax.experimental.pallas import tpu as pltpu
from jax.sharding import PartitionSpec as P

SRC_DEV = 1024
KNOT_DEV = 128
ITERS = 3
LANES = 128
SUB = 8
LOW = 256
QUANTITIES = 3 + 4 * 6
REACH = 3 * (ITERS - 1)
WINDOW = 2 * REACH
CUBICS = [(1.0, 0.0, 0.0, 0.0), (4.0, 12.0, 6.0, 1.0), (1.0, 6.0, 12.0, 4.0), (0.0, 0.0, 0.0, 1.0)]
SIGNALS = 15 + 5
PAIRS = [(x, y) for x in range(3) for y in range(x, 3)]

src_ridge = 1.0
att_ridge = 1.0
relax_step = 0.15

f32 = jnp.float32
bf16 = jnp.bfloat16


def bernstein_products():
    table = {}
    for i in range(4):
        for j in range(i, 4):
            coefs = [0.0] * 7
            for p in range(4):
                for q in range(4):
                    coefs[p + q] += CUBICS[i][p] * CUBICS[j][q] / 36.0
            table[i, j] = coefs
    return table


def split2(value):
    high = value.astype(bf16).astype(f32)
    return [high, value - high]


def split3(value):
    high = value.astype(bf16).astype(f32)
    rest = value - high
    middle = rest.astype(bf16).astype(f32)
    return [high, middle, rest - middle]


def spline_basis(phase_rows):
    remain = 1.0 - phase_rows
    square = phase_rows * phase_rows
    cube_term = square * phase_rows
    return [
        remain * remain * remain / 6.0,
        (3.0 * cube_term - 6.0 * square + 4.0) / 6.0,
        (-3.0 * cube_term + 3.0 * square + 3.0 * phase_rows + 1.0) / 6.0,
        cube_term / 6.0,
    ]


def solve_small(moments):
    matrix = {}
    position = 0
    for m in range(5):
        for n in range(m, 5):
            matrix[m, n] = moments[position] + (src_ridge if m == n else 0.0)
            position += 1
    factor = {}
    inverse = {}
    for j in range(5):
        for i in range(j, 5):
            running = matrix[j, i]
            for k in range(j):
                running = running - factor[i, k] * factor[j, k]
            if i == j:
                factor[j, j] = jnp.sqrt(running)
                inverse[j] = 1.0 / factor[j, j]
            else:
                factor[i, j] = running * inverse[j]
    forward = []
    for i in range(5):
        running = moments[15 + i]
        for k in range(i):
            running = running - factor[i, k] * forward[k]
        forward.append(running * inverse[i])
    solved = [None] * 5
    for i in reversed(range(5)):
        running = forward[i]
        for k in range(i + 1, 5):
            running = running - factor[k, i] * solved[k]
        solved[i] = running * inverse[i]
    return solved


def iota(shape, axis):
    return lax.broadcasted_iota(jnp.int32, shape, axis)


def over_steps(tiles, body):
    steps = math.gcd(tiles, 64)
    if steps == tiles:
        body(0, steps)
        return

    def one(g, _):
        body(pl.multiple_of(g * steps, steps), steps)
        return 0

    lax.fori_loop(0, tiles // steps, one, 0)


def spread_row(index_row, count):
    packed = jnp.broadcast_to(index_row, (2 * SUB, LANES)).astype(bf16)
    return jnp.concatenate([packed] * (count // (2 * SUB)), 0)


def is_equal(left, right):
    return jnp.where(left == right, jnp.ones((), bf16), jnp.zeros((), bf16))


def onehot(index_row, count):
    return is_equal(iota((count, LANES), 0).astype(f32).astype(bf16), spread_row(index_row, count))


def by_tile(wide_ref, tiled_ref):
    rows = wide_ref.shape[0]
    for t in range(tiled_ref.shape[0] // SUB):
        tiled_ref[t * SUB : t * SUB + rows, :] = wide_ref[:, t * LANES : (t + 1) * LANES]


def by_group(tiles):
    return range(0, tiles, SUB)


def across(start, row):
    return pl.ds(start * SUB + row, SUB, stride=SUB)


def tile_of(tiled_ref, t):
    return tiled_ref[pl.ds(t * SUB, SUB), :]


def low_bits(index, size):
    return index >> (size.bit_length() - 1), index & (size - 1)


def row_of(ref, t):
    return jnp.broadcast_to(ref[pl.ds(t, 1), :], (SUB, LANES))


def per_sublane(values, kind):
    row = iota((SUB, LANES), 0)
    out = jnp.full((SUB, LANES), values[0], kind)
    for s in range(1, SUB):
        if values[s] != values[0]:
            out = jnp.where(row == s, jnp.full((SUB, LANES), values[s], kind), out)
    return out


def pick_rows(value, pattern):
    return jnp.take_along_axis(value, pattern, axis=0)


def patterns(values):
    values = list(values) + [0] * (-len(values) % SUB)
    return [per_sublane(values[i : i + SUB], jnp.int32) for i in range(0, len(values), SUB)]


def stacked_parts(values, split):
    parts = split(jnp.concatenate(values, 0))
    if len(parts) * parts[0].shape[0] % (2 * SUB):
        parts.append(jnp.zeros((SUB, LANES), f32))
    return jnp.concatenate(parts, 0).astype(bf16)


def sum_parts(value, rows, count):
    return sum(value[i * rows : (i + 1) * rows] for i in range(count))


def add_blocks(moments_ref, start, steps, rep, rows, count, left_of, knot_ref):
    per_block = min(rep, steps)
    for b in range(steps // per_block):
        lefts, rights = [], []
        for i in range(b * per_block, (b + 1) * per_block):
            lefts.append(left_of(start + i))
            rights.append(onehot(knot_ref[pl.ds(start + i, 1), :].astype(f32), KNOT_DEV))
        got = contract(jnp.concatenate(lefts, 1), jnp.concatenate(rights, 1))
        summed = sum_parts(got, rows, count)
        where_to = (start + b * per_block) // rep
        where_to = pl.ds(where_to * rows, rows)
        if rep <= steps:
            moments_ref[where_to, :] = summed
        else:
            moments_ref[where_to, :] += summed


def contract(left, right):
    return lax.dot_general(left, right, (((1,), (1,)), ((), ())), preferred_element_type=f32)


def shift_up(value, n):
    turned = pltpu.roll(value, n, 1)
    before = pltpu.roll(turned, 1, 0)
    before = jnp.where(iota(value.shape, 0) == 0, 0.0, before)
    return jnp.where(iota(value.shape, 1) < n, before, turned)


def shift_down(value, n):
    turned = pltpu.roll(value, LANES - n, 1)
    after = pltpu.roll(turned, value.shape[0] - 1, 0)
    after = jnp.where(iota(value.shape, 0) == value.shape[0] - 1, 0.0, after)
    return jnp.where(iota(value.shape, 1) >= LANES - n, after, turned)


def source_kernel(
    counts_hbm, design_hbm, obs_hbm, weight_hbm, index_hbm, out_ref, live_ref,
    counts_ref, design_ref, obs_ref, weight_ref, index_ref, sems, low_ref, high_ref, total, tiled,
):
    tiles = obs_ref.shape[0]
    shards = counts_ref.shape[2]
    rep = tiles // shards
    copies = [
        pltpu.make_async_copy(src, dst, sems.at[i])
        for i, (src, dst) in enumerate(
            [(counts_hbm, counts_ref), (weight_hbm, weight_ref), (index_hbm, index_ref), (obs_hbm, obs_ref),
             (design_hbm, design_ref)]
        )
    ]
    for copy in copies:
        copy.start()
    if math.gcd(tiles, 64) != tiles:
        total[...] = jnp.zeros_like(total)
    highs = SRC_DEV // LOW
    pairs = [(m, n) for m in range(5) for n in range(m, 5)] + [(m, 5) for m in range(5)]
    pairs += pairs[2 * SUB :]
    lefts_of = patterns([m for m, _ in pairs])
    rights_of = patterns([n for _, n in pairs])
    first_half = iota((SUB, LANES), 0) < SUB // 2
    copies[0].wait()
    slots = iota((rep, LANES), 0) * LANES + iota((rep, LANES), 1)
    for d in range(shards):
        live_ref[pl.ds(d * rep, rep), :] = (slots < counts_ref[0, 0, d]).astype(f32)
    copies[1].wait()
    copies[2].wait()
    for start in by_group(tiles):
        at = pl.ds(start, SUB)
        weight_ref[at, :] = weight_ref[at, :] * live_ref[at, :]
        high, low = low_bits(index_ref[at, :], LOW)
        high_ref[at, :] = high.astype(f32)
        low_ref[at, :] = low.astype(f32)
    copies[3].wait()
    copies[4].wait()
    by_tile(design_ref, tiled)
    for start in by_group(tiles):
        tiled[across(start, 5), :] = obs_ref[pl.ds(start, SUB), :]

    def group(start, steps):
        lefts, rights = [], []
        for i in range(steps):
            t = start + i
            values = tile_of(tiled, t)
            scaled = values * row_of(weight_ref, t)
            products = [pick_rows(scaled, m) * pick_rows(values, n) for m, n in zip(lefts_of, rights_of)]
            high, middle, low = split3(products[2])
            parts = split3(jnp.concatenate(products[:2], 0)) + [jnp.where(first_half, high, middle), low]
            block = jnp.concatenate(parts, 0).astype(bf16)
            packed = spread_row(high_ref[pl.ds(t, 1), :], 2 * SUB)
            masks = [is_equal(packed, jnp.full((), h, bf16)) for h in range(highs)]
            repeats = block.shape[0] // (2 * SUB)
            lefts.append(jnp.concatenate([block * jnp.concatenate([mask] * repeats, 0) for mask in masks], 0))
            rights.append(onehot(low_ref[pl.ds(t, 1), :], LOW))
        got = contract(jnp.concatenate(lefts, 1), jnp.concatenate(rights, 1))
        if steps == tiles:
            total[...] = got
        else:
            total[...] += got

    over_steps(tiles, group)
    height = total.shape[0] // highs
    wide, half_tile = 2 * SUB, SUB // 2
    for h in range(highs):
        block = total[h * height : (h + 1) * height, :]
        tail = block[3 * wide :]
        summed = sum_parts(block, wide, 3)
        rest = tail[0:half_tile] + tail[half_tile : 2 * half_tile] + tail[2 * half_tile : 3 * half_tile]
        for half in range(LOW // LANES):
            cols = slice(half * LANES, (half + 1) * LANES)
            out_ref[0:wide, h * (LOW // LANES) + half, :] = summed[:, cols]
            out_ref[wide:SIGNALS, h * (LOW // LANES) + half, :] = rest[:, cols]


def band_kernel(live_ref, phase_ref, axis_ref, weight_ref, knot_ref, out_ref, tiled, powers_ref, moments):
    tiles, shards = phase_ref.shape[0], out_ref.shape[0] // 24
    rep = tiles // shards
    by_tile(axis_ref, tiled)
    rows = moments.shape[0] // shards
    lefts_of = patterns([PAIRS[q % 6][0] for q in range(24)])
    rights_of = patterns([PAIRS[q % 6][1] for q in range(24)])
    powers_of = patterns([q // 6 if q < 42 else 0 for q in range(rows)])
    for start in by_group(tiles):
        at = pl.ds(start, SUB)
        u = phase_ref[at, :]
        r = 1.0 - u
        u2, r2 = u * u, r * r
        u3, r3 = u2 * u, r2 * r
        w = weight_ref[at, :] * live_ref[at, :]
        u3w, r3w = u3 * w, r3 * w
        powers = [r3w * r3, r3w * (r2 * u), r3w * (r * u2), r3w * u3, u3w * (r2 * u), u3w * (r * u2), u3w * u3]
        for p in range(7):
            powers_ref[across(start, p), :] = powers[p]

    def left_of(t):
        axes = tile_of(tiled, t)
        powers = tile_of(powers_ref, t)
        products = [pick_rows(axes, x) * pick_rows(axes, y) for x, y in zip(lefts_of, rights_of)]
        return stacked_parts([products[i % 3] * pick_rows(powers, p) for i, p in enumerate(powers_of)], split2)

    def group(start, steps):
        add_blocks(moments, start, steps, rep, rows, 2, left_of, knot_ref)

    if rep > math.gcd(tiles, 64):
        moments[...] = jnp.zeros_like(moments)
    over_steps(tiles, group)
    table = bernstein_products()
    for n in range(6):
        parts = [moments[pl.ds(p * 6 + n, shards, stride=rows), :] for p in range(7)]

        def product(i, j):
            return sum(c * part for c, part in zip(table[i, j], parts) if c)

        for delta in range(4):
            running = product(3 - delta, 3)
            for j in reversed(range(3 - delta)):
                running = product(j, j + delta) + shift_up(running, 1)
            to = (delta * 6 + n) * shards
            out_ref[to : to + shards, :] = running


def halo_rows():
    return 1 + (QUANTITIES - 3) // SUB


def slots_of(value, shift):
    return pltpu.roll(value, shift, 1, stride=WINDOW, stride_axis=0)


def pack(source_ref, first, count, row, message_ref):
    parts, shards = message_ref.shape[0], source_ref.shape[0] // count
    owned = shards // parts
    lane, slot = iota((SUB, LANES), 1), iota((SUB, LANES), 0)
    mine = (lane >= WINDOW * slot) & (lane < WINDOW * (slot + 1)) & (slot < count)
    zero = jnp.zeros((SUB, LANES), f32)
    for base in range(0, count, SUB):
        for q in range(base, min(base + SUB, count)):
            for p in range(parts):
                at = q * shards + p * owned
                to = (first + q) * owned
                message_ref[p, to : to + owned, :] = source_ref[at : at + owned, :]
        for p in range(parts):
            taken = min(count, SUB)

            def edge(r):
                got = source_ref[pl.ds(base * shards + r, taken, stride=shards), :]
                return got if taken == SUB else jnp.concatenate([got, zero[taken:]], 0)

            after = edge((p + 1) * owned) if p < parts - 1 else zero
            before = edge(p * owned - 1) if p else zero
            packed = slots_of(jnp.where(lane < LANES // 2, after, before), REACH)
            to = QUANTITIES * owned + row + base // SUB
            message_ref[p, to : to + 1, :] = jnp.sum(jnp.where(mine, packed, 0.0), 0, keepdims=True)


def resid_kernel(
    mine_ref, other_ref, band_ref, live_ref, design_ref, obs_ref, weight_ref, index_ref, phase_ref, axis_ref, knot_ref,
    params_ref, resid_ref, message_ref, tiled, tiled_axis, splines_ref, moments, solved_ref, rhs_ref,
):
    tiles, shards = obs_ref.shape[0], rhs_ref.shape[0] // 3
    rep = tiles // shards
    by_tile(design_ref, tiled)
    by_tile(axis_ref, tiled_axis)
    solved = solve_small([mine_ref[q] + other_ref[q] for q in range(SIGNALS)])
    blocks = SRC_DEV // LANES
    for m in range(5):
        solved_ref[m] = solved[m]
        for b in range(blocks):
            params_ref[m : m + 1, b * LANES : (b + 1) * LANES] = solved[m][b : b + 1, :]
    rows = moments.shape[0] // shards
    axes_of = patterns([q % 3 for q in range(rows)])
    splines_of = patterns([min(q // 3, 3) for q in range(rows)])

    def left_of(t):
        axes = tile_of(tiled_axis, t)
        splines = tile_of(splines_ref, t)
        return stacked_parts([pick_rows(axes, x) * pick_rows(splines, j) for x, j in zip(axes_of, splines_of)], split3)

    def group(start, steps):
        for part in range(steps // SUB):
            at = pl.ds(start + part * SUB, SUB)
            live = live_ref[at, :]
            block_of, lane_of = low_bits(index_ref[at, :], LANES)
            hits = [block_of == b for b in range(blocks)]
            left = obs_ref[at, :]
            for m in range(5):
                for b in range(blocks):
                    table = jnp.broadcast_to(solved_ref[m, b : b + 1, :], (SUB, LANES))
                    found = jnp.take_along_axis(table, lane_of, axis=1)
                    picked = jnp.where(hits[b], found, picked) if b else found
                left = left - tiled[across(start + part * SUB, m), :] * picked
            resid = live * left
            resid_ref[at, :] = resid
            scaled = weight_ref[at, :] * resid
            for j, basis in enumerate(spline_basis(phase_ref[at, :])):
                splines_ref[across(start + part * SUB, j), :] = basis * scaled
        add_blocks(moments, start, steps, rep, rows, 3, left_of, knot_ref)

    if rep > math.gcd(tiles, 64):
        moments[...] = jnp.zeros_like(moments)
    over_steps(tiles, group)
    for x in range(3):
        running = moments[pl.ds(9 + x, shards, stride=rows), :]
        for j in reversed(range(3)):
            running = moments[pl.ds(j * 3 + x, shards, stride=rows), :] + shift_up(running, 1)
        rhs_ref[x * shards : (x + 1) * shards, :] = running
    pack(rhs_ref, 0, 3, 0, message_ref)
    pack(band_ref, 3, QUANTITIES - 3, 1, message_ref)


def part_bits():
    place = lax.axis_index("src")
    upper = lax.axis_index("ccd")
    for shift in range(lax.axis_size("src").bit_length() - 1):
        upper = upper ^ ((place >> shift) & 1)
    return [upper, place & 1]


def solve_kernel(parts, sums_ref, out_ref, edges_ref):
    owned = out_ref.shape[0] // 4
    ring = -(-(owned + 2) // SUB) * SUB
    order = {pair: n for n, pair in enumerate(PAIRS)}
    row, lane = iota((ring, LANES), 0), iota((ring, LANES), 1)
    inside = row < owned
    after = (row == owned) & (lane < REACH)
    before = (row == ring - 1) & (lane >= LANES - REACH)
    part = 0 if parts == 1 else sum(bit << i for i, bit in enumerate(reversed(part_bits())))
    edge = (part == parts - 1) * jnp.ones((), jnp.int32)
    known = jnp.where(after & (jnp.full((ring, LANES), edge, jnp.int32) == 1), 0.0, 1.0)

    back = LANES - REACH - WINDOW * (SUB - 1)
    for i in range(halo_rows()):
        packed = sums_ref[QUANTITIES * owned + i : QUANTITIES * owned + i + 1, :]
        edges_ref[i * SUB : (i + 1) * SUB, :] = slots_of(jnp.broadcast_to(packed, (SUB, LANES)), back)

    def load(q):
        rows = sums_ref[q * owned : (q + 1) * owned, :]
        place = q if q < 3 else q + SUB - 3
        slot = place // SUB * SUB + SUB - 1 - place % SUB
        rest = jnp.broadcast_to(edges_ref[slot : slot + 1, :], (ring - owned, LANES))
        return jnp.where(inside | after | before, jnp.concatenate([rows, rest], 0), 0.0)

    def turn(value, n):
        turned = pltpu.roll(value, n % LANES, 1)
        if n > 0:
            return jnp.where(lane < n, pltpu.roll(turned, 1, 0), turned)
        return jnp.where(lane >= LANES + n, pltpu.roll(turned, ring - 1, 0), turned)

    loaded = [load(q) for q in range(QUANTITIES)]

    def band(delta, x, y):
        return loaded[3 + delta * 6 + order[min(x, y), max(x, y)]]

    rhs = loaded[:3]
    scale = [relax_step / (att_ridge + band(0, x, x)) * known for x in range(3)]
    coefs = [rhs[x] * scale[x] for x in range(3)]
    for _ in range(1, ITERS):
        ahead = {(y, delta): turn(coefs[y], -delta) for y in range(3) for delta in range(1, 4)}
        fresh = []
        for x in range(3):
            normal = att_ridge * coefs[x]
            for y in range(3):
                normal = normal + band(0, x, y) * coefs[y]
            for delta in range(1, 4):
                for y in range(3):
                    normal = normal + band(delta, x, y) * ahead[y, delta]
                normal = normal + turn(sum(band(delta, x, y) * coefs[y] for y in range(3)), delta)
            fresh.append(coefs[x] + scale[x] * (rhs[x] - normal))
        coefs = fresh
    for x in range(3):
        for r in range(owned):
            out_ref[pl.ds(r * 4 + x, 1), :] = coefs[x][r : r + 1]


def prepare_kernel(_, live_ref, phase_ref, axis_ref, out_ref, tiled):
    by_tile(axis_ref, tiled)

    def group(start, steps):
        for part in range(steps // SUB):
            at = pl.ds(start + part * SUB, SUB)
            basis = [b * live_ref[at, :] for b in spline_basis(phase_ref[at, :])]
            for x in range(3):
                along = tiled[across(start + part * SUB, x), :]
                for j in range(4):
                    out_ref[x * 4 + j, at, :] = along * basis[j]

    over_steps(phase_ref.shape[0], group)


def predict_kernel(coef_ref, factor_ref, resid_ref, knot_ref, att_ref, out_ref, windows):
    tiles, shards = resid_ref.shape[0], coef_ref.shape[0]
    rep = tiles // shards
    for x in range(3):
        coefs = coef_ref[:, x, :]
        for j in range(4):
            windows[x * 4 + j] = coefs if j == 0 else shift_down(coefs, j)
        att_ref[x : x + 1, :] = windows[x * 4, pl.ds(lax.axis_index("src"), 1), :]
    row = iota((SUB, LANES), 0)

    def group(start, steps):
        for part in range(steps // SUB):
            at = pl.ds(start + part * SUB, SUB)
            knots = knot_ref[at, :]
            first = (start + part * SUB) // rep
            left = resid_ref[at, :]
            for q in range(12):
                table = jnp.broadcast_to(windows[q, pl.ds(first, 1), :], (SUB, LANES))
                for k in range(1, SUB // rep):
                    later = jnp.broadcast_to(windows[q, pl.ds(first + k, 1), :], (SUB, LANES))
                    table = jnp.where(row >= k * rep, later, table)
                left = left - factor_ref[q, at, :] * jnp.take_along_axis(table, knots, axis=1)
            out_ref[at, :] = left

    over_steps(tiles, group)


BOTH = ("src", "ccd")
SMEM = pl.BlockSpec(memory_space=pltpu.SMEM)
VMEM = pl.BlockSpec(memory_space=pltpu.VMEM)
HBM = pl.BlockSpec(memory_space=pltpu.HBM)


def call(kernel, name, scalars, arrays, outs, scratch, space=VMEM):
    return pl.pallas_call(
        kernel,
        name=name,
        out_shape=outs,
        in_specs=[SMEM] * len(scalars) + [space] * len(arrays),
        out_specs=jax.tree.map(lambda _: VMEM, outs),
        scratch_shapes=scratch,
        compiler_params=pltpu.CompilerParams(vmem_limit_bytes=8 << 20),
    )(*scalars, *arrays)


def swapped(value, axis, bit):
    size = lax.axis_size(axis)
    return lax.ppermute(value, axis, [(i, i ^ bit) for i in range(size)])


def summed_over(value, axis):
    size = lax.axis_size(axis)
    if size & (size - 1):
        return lax.psum(value, axis)
    bit = 1
    while bit < size:
        value = value + swapped(value, axis, bit)
        bit *= 2
    return value


def halved(value, mask, keep):
    pair = value.reshape((2, value.shape[0] // 2) + value.shape[1:])
    kept = lax.dynamic_index_in_dim(pair, keep, 0, False)
    sent = lax.dynamic_index_in_dim(pair, 1 - keep, 0, False)
    return kept + swapped(sent, BOTH, mask)


def doubled(value, mask, keep):
    other = swapped(value, BOTH, mask)
    first = jnp.where(keep == 0, value, other)
    second = jnp.where(keep == 0, other, value)
    return jnp.concatenate([first, second], 0)


def on_device(design, observed, weight, phase_frac, axis_factors, source_index, knot_index, counts):
    row_count = observed.shape[0]
    tiles = row_count // LANES
    shards = lax.axis_size("src")
    obs, w, phase, index, knots = (
        a.reshape(tiles, LANES) for a in (observed, weight, phase_frac, source_index, knot_index)
    )
    tiled = pltpu.VMEM((tiles * SUB, LANES), f32)
    dense = pltpu.VMEM((tiles, LANES), f32)
    blocks = SRC_DEV // LANES
    moments, live = call(
        source_kernel, "source_sums", [],
        [pltpu.with_memory_space_constraint(a, pltpu.HBM) for a in (counts, design, obs, w, index)],
        (jax.ShapeDtypeStruct((SIGNALS, blocks, LANES), f32), jax.ShapeDtypeStruct((tiles, LANES), f32)),
        [
            pltpu.SMEM(counts.shape, jnp.int32), pltpu.VMEM(design.shape, f32), dense, dense,
            pltpu.VMEM((tiles, LANES), jnp.int32), pltpu.SemaphoreType.DMA((5,)), dense, dense,
            pltpu.VMEM((SRC_DEV // LOW * 64, LOW), f32), tiled,
        ],
        HBM,
    )
    band = call(
        band_kernel, "band_sums", [], [live, phase, axis_factors, w, knots],
        jax.ShapeDtypeStruct((24 * shards, KNOT_DEV), f32),
        [tiled, tiled, pltpu.VMEM((shards * 48, KNOT_DEV), f32)],
    )
    if lax.axis_size("ccd") == 2:
        other = swapped(moments, "ccd", 1)
    else:
        moments = summed_over(moments, "ccd")
        other = jnp.zeros_like(moments)
    fast = lax.axis_size("ccd") == 2 and shards >= 4 and shards & (shards - 1) == 0
    parts = 4 if fast else 1
    owned = shards // parts
    message_rows = -(-(QUANTITIES * owned + halo_rows()) // SUB) * SUB
    params, resid, message = call(
        resid_kernel, "residuals", [],
        [moments, other, band, live, design, obs, w, index, phase, axis_factors, knots],
        (
            jax.ShapeDtypeStruct((5, SRC_DEV), f32),
            jax.ShapeDtypeStruct((tiles, LANES), f32),
            jax.ShapeDtypeStruct((parts, message_rows, LANES), f32),
        ),
        [tiled, tiled, tiled, pltpu.VMEM((shards * 16, KNOT_DEV), f32), pltpu.VMEM((5, blocks, LANES), f32),
         pltpu.VMEM((3 * shards, KNOT_DEV), f32)],
    )
    factors = call(
        prepare_kernel, "prepare", [], [message, live, phase, axis_factors],
        jax.ShapeDtypeStruct((12, tiles, LANES), f32), [tiled],
    )
    if fast:
        upper, lower = part_bits()
        sums = halved(halved(message, 1, upper), 3, lower)[0]
        bit = 2
        while bit < shards:
            sums = sums + swapped(sums, BOTH, 2 * bit + 1)
            bit *= 2
    else:
        sums = summed_over(summed_over(message[0], "ccd"), "src")
    coefs = call(
        functools.partial(solve_kernel, parts), "attitude", [], [sums],
        jax.ShapeDtypeStruct((owned * 4, LANES), f32), [pltpu.VMEM((halo_rows() * SUB, LANES), f32)],
    )
    if fast:
        coefs = doubled(doubled(coefs, 3, lower), 1, upper)
    attitude, residual = call(
        predict_kernel, "predict", [], [coefs.reshape(shards, 4, LANES), factors, resid, knots],
        (jax.ShapeDtypeStruct((3, KNOT_DEV), f32), jax.ShapeDtypeStruct((tiles, LANES), f32)),
        [pltpu.VMEM((12, shards, KNOT_DEV), f32)],
    )
    return params, attitude, residual.reshape(row_count)


def solution(mesh):
    rows = P(("src", "ccd"))
    wide = P(None, ("src", "ccd"))
    in_specs = (wide, rows, rows, rows, wide, rows, rows, P("src", "ccd", None))
    out_specs = (P(None, "src"), P(None, "src"), rows)
    return jax.shard_map(on_device, mesh=mesh, in_specs=in_specs, out_specs=out_specs, check_vma=False)
```

```python
import functools
import math

import jax
import jax.numpy as jnp
from jax import lax
from jax.experimental import pallas as pl
from jax.experimental.pallas import tpu as pltpu
from jax.sharding import PartitionSpec as P

SRC_DEV = 1024
KNOT_DEV = 128
ITERS = 3
LANES = 128
SUB = 8
LOW = 256
QUANTITIES = 3 + 4 * 6
REACH = 3 * (ITERS - 1)
WINDOW = 2 * REACH
CUBICS = [(1.0, 0.0, 0.0, 0.0), (4.0, 12.0, 6.0, 1.0), (1.0, 6.0, 12.0, 4.0), (0.0, 0.0, 0.0, 1.0)]
SIGNALS = 15 + 5
PAIRS = [(x, y) for x in range(3) for y in range(x, 3)]

src_ridge = 1.0
att_ridge = 1.0
relax_step = 0.15

f32 = jnp.float32
bf16 = jnp.bfloat16


def bernstein_products():
    table = {}
    for i in range(4):
        for j in range(i, 4):
            coefs = [0.0] * 7
            for p in range(4):
                for q in range(4):
                    coefs[p + q] += CUBICS[i][p] * CUBICS[j][q] / 36.0
            table[i, j] = coefs
    return table


def split2(value):
    high = value.astype(bf16).astype(f32)
    return [high, value - high]


def split3(value):
    high = value.astype(bf16).astype(f32)
    rest = value - high
    middle = rest.astype(bf16).astype(f32)
    return [high, middle, rest - middle]


def spline_basis(phase_rows):
    remain = 1.0 - phase_rows
    square = phase_rows * phase_rows
    cube_term = square * phase_rows
    return [
        remain * remain * remain / 6.0,
        (3.0 * cube_term - 6.0 * square + 4.0) / 6.0,
        (-3.0 * cube_term + 3.0 * square + 3.0 * phase_rows + 1.0) / 6.0,
        cube_term / 6.0,
    ]


def solve_small(moments):
    matrix = {}
    position = 0
    for m in range(5):
        for n in range(m, 5):
            matrix[m, n] = moments[position] + (src_ridge if m == n else 0.0)
            position += 1
    scaled, factor, inverse = {}, {}, {}
    for j in range(5):
        for i in range(j, 5):
            running = matrix[j, i]
            for k in range(j):
                running = running - scaled[i, k] * factor[j, k]
            scaled[i, j] = running
        inverse[j] = 1.0 / scaled[j, j]
        for i in range(j + 1, 5):
            factor[i, j] = scaled[i, j] * inverse[j]
    forward = []
    for i in range(5):
        running = moments[15 + i]
        for k in range(i):
            running = running - factor[i, k] * forward[k]
        forward.append(running)
    solved = [None] * 5
    for i in reversed(range(5)):
        running = forward[i] * inverse[i]
        for k in range(i + 1, 5):
            running = running - factor[k, i] * solved[k]
        solved[i] = running
    return solved


def iota(shape, axis):
    return lax.broadcasted_iota(jnp.int32, shape, axis)


def over_steps(tiles, body):
    steps = math.gcd(tiles, 64)
    if steps == tiles:
        body(0, steps)
        return

    def one(g, _):
        body(pl.multiple_of(g * steps, steps), steps)
        return 0

    lax.fori_loop(0, tiles // steps, one, 0)


def spread_row(index_row, count):
    packed = jnp.broadcast_to(index_row, (2 * SUB, LANES)).astype(bf16)
    return jnp.concatenate([packed] * (count // (2 * SUB)), 0)


def is_equal(left, right):
    return jnp.where(left == right, jnp.ones((), bf16), jnp.zeros((), bf16))


def onehot(index_row, count):
    return is_equal(iota((count, LANES), 0).astype(f32).astype(bf16), spread_row(index_row, count))


def by_tile(wide_ref, tiled_ref):
    rows = wide_ref.shape[0]
    for t in range(tiled_ref.shape[0] // SUB):
        tiled_ref[t * SUB : t * SUB + rows, :] = wide_ref[:, t * LANES : (t + 1) * LANES]


def by_group(tiles):
    return range(0, tiles, SUB)


def across(start, row):
    return pl.ds(start * SUB + row, SUB, stride=SUB)


def tile_of(tiled_ref, t):
    return tiled_ref[pl.ds(t * SUB, SUB), :]


def low_bits(index, size):
    return index >> (size.bit_length() - 1), index & (size - 1)


def row_of(ref, t):
    return jnp.broadcast_to(ref[pl.ds(t, 1), :], (SUB, LANES))


def per_sublane(values, kind):
    row = iota((SUB, LANES), 0)
    out = jnp.full((SUB, LANES), values[0], kind)
    for s in range(1, SUB):
        if values[s] != values[0]:
            out = jnp.where(row == s, jnp.full((SUB, LANES), values[s], kind), out)
    return out


def pick_rows(value, pattern):
    return jnp.take_along_axis(value, pattern, axis=0)


def patterns(values):
    values = list(values) + [0] * (-len(values) % SUB)
    return [per_sublane(values[i : i + SUB], jnp.int32) for i in range(0, len(values), SUB)]


def stacked_parts(values, split):
    parts = split(jnp.concatenate(values, 0))
    if len(parts) * parts[0].shape[0] % (2 * SUB):
        parts.append(jnp.zeros((SUB, LANES), f32))
    return jnp.concatenate(parts, 0).astype(bf16)


def sum_parts(value, rows, count):
    return sum(value[i * rows : (i + 1) * rows] for i in range(count))


def add_blocks(moments_ref, start, steps, rep, rows, count, left_of, knot_ref):
    per_block = min(rep, steps)
    for b in range(steps // per_block):
        lefts, rights = [], []
        for i in range(b * per_block, (b + 1) * per_block):
            lefts.append(left_of(start + i))
            rights.append(onehot(knot_ref[pl.ds(start + i, 1), :].astype(f32), KNOT_DEV))
        got = contract(jnp.concatenate(lefts, 1), jnp.concatenate(rights, 1))
        summed = sum_parts(got, rows, count)
        where_to = (start + b * per_block) // rep
        where_to = pl.ds(where_to * rows, rows)
        if rep <= steps:
            moments_ref[where_to, :] = summed
        else:
            moments_ref[where_to, :] += summed


def contract(left, right):
    return lax.dot_general(left, right, (((1,), (1,)), ((), ())), preferred_element_type=f32)


def shift_up(value, n):
    turned = pltpu.roll(value, n, 1)
    before = pltpu.roll(turned, 1, 0)
    before = jnp.where(iota(value.shape, 0) == 0, 0.0, before)
    return jnp.where(iota(value.shape, 1) < n, before, turned)


def shift_down(value, n):
    turned = pltpu.roll(value, LANES - n, 1)
    after = pltpu.roll(turned, value.shape[0] - 1, 0)
    after = jnp.where(iota(value.shape, 0) == value.shape[0] - 1, 0.0, after)
    return jnp.where(iota(value.shape, 1) >= LANES - n, after, turned)


def source_kernel(
    counts_hbm, weight_hbm, index_hbm, obs_hbm, design_hbm, phase_hbm, axis_hbm, knot_hbm,
    out_ref, live_ref, weight_ref, index_ref, obs_ref, design_ref, phase_ref, axis_ref, knot_ref,
    counts_ref, sems, low_ref, high_ref, total, tiled,
):
    tiles = obs_ref.shape[0]
    shards = counts_ref.shape[2]
    rep = tiles // shards
    copies = [
        pltpu.make_async_copy(src, dst, sems.at[i])
        for i, (src, dst) in enumerate(
            [(counts_hbm, counts_ref), (weight_hbm, weight_ref), (index_hbm, index_ref), (obs_hbm, obs_ref),
             (design_hbm, design_ref), (phase_hbm, phase_ref), (axis_hbm, axis_ref), (knot_hbm, knot_ref)]
        )
    ]
    for copy in copies:
        copy.start()
    if math.gcd(tiles, 64) != tiles:
        total[...] = jnp.zeros_like(total)
    highs = SRC_DEV // LOW
    pairs = [(m, n) for m in range(5) for n in range(m, 5)] + [(m, 5) for m in range(5)]
    pairs += pairs[2 * SUB :]
    lefts_of = patterns([m for m, _ in pairs])
    rights_of = patterns([n for _, n in pairs])
    first_half = iota((SUB, LANES), 0) < SUB // 2
    copies[0].wait()
    slots = iota((rep, LANES), 0) * LANES + iota((rep, LANES), 1)
    for d in range(shards):
        live_ref[pl.ds(d * rep, rep), :] = (slots < counts_ref[0, 0, d]).astype(f32)
    copies[1].wait()
    copies[2].wait()
    for start in by_group(tiles):
        at = pl.ds(start, SUB)
        weight_ref[at, :] = weight_ref[at, :] * live_ref[at, :]
        high, low = low_bits(index_ref[at, :], LOW)
        high_ref[at, :] = high.astype(f32)
        low_ref[at, :] = low.astype(f32)
    copies[3].wait()
    copies[4].wait()
    by_tile(design_ref, tiled)
    for start in by_group(tiles):
        tiled[across(start, 5), :] = obs_ref[pl.ds(start, SUB), :]

    def group(start, steps):
        lefts, rights = [], []
        for i in range(steps):
            t = start + i
            values = tile_of(tiled, t)
            scaled = values * row_of(weight_ref, t)
            products = [pick_rows(scaled, m) * pick_rows(values, n) for m, n in zip(lefts_of, rights_of)]
            high, middle, low = split3(products[2])
            parts = split3(jnp.concatenate(products[:2], 0)) + [jnp.where(first_half, high, middle), low]
            block = jnp.concatenate(parts, 0).astype(bf16)
            packed = spread_row(high_ref[pl.ds(t, 1), :], 2 * SUB)
            masks = [is_equal(packed, jnp.full((), h, bf16)) for h in range(highs)]
            repeats = block.shape[0] // (2 * SUB)
            lefts.append(jnp.concatenate([block * jnp.concatenate([mask] * repeats, 0) for mask in masks], 0))
            rights.append(onehot(low_ref[pl.ds(t, 1), :], LOW))
        got = contract(jnp.concatenate(lefts, 1), jnp.concatenate(rights, 1))
        if steps == tiles:
            total[...] = got
        else:
            total[...] += got

    over_steps(tiles, group)
    for copy in copies[5:]:
        copy.wait()
    height = total.shape[0] // highs
    wide, half_tile = 2 * SUB, SUB // 2
    for h in range(highs):
        block = total[h * height : (h + 1) * height, :]
        tail = block[3 * wide :]
        summed = sum_parts(block, wide, 3)
        rest = tail[0:half_tile] + tail[half_tile : 2 * half_tile] + tail[2 * half_tile : 3 * half_tile]
        for half in range(LOW // LANES):
            cols = slice(half * LANES, (half + 1) * LANES)
            out_ref[0:wide, h * (LOW // LANES) + half, :] = summed[:, cols]
            out_ref[wide:SIGNALS, h * (LOW // LANES) + half, :] = rest[:, cols]


def band_kernel(phase_ref, axis_ref, weight_ref, knot_ref, out_ref, tiled, powers_ref, moments):
    tiles, shards = phase_ref.shape[0], out_ref.shape[0] // 24
    rep = tiles // shards
    by_tile(axis_ref, tiled)
    rows = moments.shape[0] // shards
    lefts_of = patterns([PAIRS[q % 6][0] for q in range(24)])
    rights_of = patterns([PAIRS[q % 6][1] for q in range(24)])
    powers_of = patterns([q // 6 if q < 42 else 0 for q in range(rows)])
    for start in by_group(tiles):
        at = pl.ds(start, SUB)
        u = phase_ref[at, :]
        r = 1.0 - u
        u2, r2 = u * u, r * r
        u3, r3 = u2 * u, r2 * r
        w = weight_ref[at, :]
        u3w, r3w = u3 * w, r3 * w
        powers = [r3w * r3, r3w * (r2 * u), r3w * (r * u2), r3w * u3, u3w * (r2 * u), u3w * (r * u2), u3w * u3]
        for p in range(7):
            powers_ref[across(start, p), :] = powers[p]

    def left_of(t):
        axes = tile_of(tiled, t)
        powers = tile_of(powers_ref, t)
        products = [pick_rows(axes, x) * pick_rows(axes, y) for x, y in zip(lefts_of, rights_of)]
        return stacked_parts([products[i % 3] * pick_rows(powers, p) for i, p in enumerate(powers_of)], split2)

    def group(start, steps):
        add_blocks(moments, start, steps, rep, rows, 2, left_of, knot_ref)

    if rep > math.gcd(tiles, 64):
        moments[...] = jnp.zeros_like(moments)
    over_steps(tiles, group)
    table = bernstein_products()
    for n in range(6):
        parts = [moments[pl.ds(p * 6 + n, shards, stride=rows), :] for p in range(7)]

        def product(i, j):
            return sum(c * part for c, part in zip(table[i, j], parts) if c)

        for delta in range(4):
            running = product(3 - delta, 3)
            for j in reversed(range(3 - delta)):
                running = product(j, j + delta) + shift_up(running, 1)
            to = (delta * 6 + n) * shards
            out_ref[to : to + shards, :] = running


def halo_rows():
    return 1 + (QUANTITIES - 3) // SUB


def slots_of(value, shift):
    return pltpu.roll(value, shift, 1, stride=WINDOW, stride_axis=0)


def pack(source_ref, first, count, row, message_ref):
    parts, shards = message_ref.shape[0], source_ref.shape[0] // count
    owned = shards // parts
    lane, slot = iota((SUB, LANES), 1), iota((SUB, LANES), 0)
    mine = (lane >= WINDOW * slot) & (lane < WINDOW * (slot + 1)) & (slot < count)
    zero = jnp.zeros((SUB, LANES), f32)
    for base in range(0, count, SUB):
        for q in range(base, min(base + SUB, count)):
            for p in range(parts):
                at = q * shards + p * owned
                to = (first + q) * owned
                message_ref[p, to : to + owned, :] = source_ref[at : at + owned, :]
        for p in range(parts):
            taken = min(count, SUB)

            def edge(r):
                got = source_ref[pl.ds(base * shards + r, taken, stride=shards), :]
                return got if taken == SUB else jnp.concatenate([got, zero[taken:]], 0)

            after = edge((p + 1) * owned) if p < parts - 1 else zero
            before = edge(p * owned - 1) if p else zero
            packed = slots_of(jnp.where(lane < LANES // 2, after, before), REACH)
            to = QUANTITIES * owned + row + base // SUB
            message_ref[p, to : to + 1, :] = jnp.sum(jnp.where(mine, packed, 0.0), 0, keepdims=True)


def resid_kernel(
    mine_ref, other_ref, band_ref, live_ref, design_ref, obs_ref, weight_ref, index_ref, phase_ref, axis_ref, knot_ref,
    params_ref, resid_ref, message_ref, tiled, tiled_axis, splines_ref, moments, solved_ref, rhs_ref,
):
    tiles, shards = obs_ref.shape[0], rhs_ref.shape[0] // 3
    rep = tiles // shards
    by_tile(design_ref, tiled)
    by_tile(axis_ref, tiled_axis)
    solved = solve_small([mine_ref[q] + other_ref[q] for q in range(SIGNALS)])
    blocks = SRC_DEV // LANES
    for m in range(5):
        solved_ref[m] = solved[m]
        for b in range(blocks):
            params_ref[m : m + 1, b * LANES : (b + 1) * LANES] = solved[m][b : b + 1, :]
    rows = moments.shape[0] // shards
    axes_of = patterns([q % 3 for q in range(rows)])
    splines_of = patterns([min(q // 3, 3) for q in range(rows)])

    def left_of(t):
        axes = tile_of(tiled_axis, t)
        splines = tile_of(splines_ref, t)
        return stacked_parts([pick_rows(axes, x) * pick_rows(splines, j) for x, j in zip(axes_of, splines_of)], split3)

    def group(start, steps):
        for part in range(steps // SUB):
            at = pl.ds(start + part * SUB, SUB)
            live = live_ref[at, :]
            block_of, lane_of = low_bits(index_ref[at, :], LANES)
            hits = [block_of == b for b in range(blocks)]
            left = obs_ref[at, :]
            for m in range(5):
                for b in range(blocks):
                    table = jnp.broadcast_to(solved_ref[m, b : b + 1, :], (SUB, LANES))
                    found = jnp.take_along_axis(table, lane_of, axis=1)
                    picked = jnp.where(hits[b], found, picked) if b else found
                left = left - tiled[across(start + part * SUB, m), :] * picked
            resid = live * left
            resid_ref[at, :] = resid
            scaled = weight_ref[at, :] * resid
            for j, basis in enumerate(spline_basis(phase_ref[at, :])):
                splines_ref[across(start + part * SUB, j), :] = basis * scaled
        add_blocks(moments, start, steps, rep, rows, 3, left_of, knot_ref)

    if rep > math.gcd(tiles, 64):
        moments[...] = jnp.zeros_like(moments)
    over_steps(tiles, group)
    for x in range(3):
        running = moments[pl.ds(9 + x, shards, stride=rows), :]
        for j in reversed(range(3)):
            running = moments[pl.ds(j * 3 + x, shards, stride=rows), :] + shift_up(running, 1)
        rhs_ref[x * shards : (x + 1) * shards, :] = running
    pack(rhs_ref, 0, 3, 0, message_ref)
    pack(band_ref, 3, QUANTITIES - 3, 1, message_ref)


def part_bits():
    place = lax.axis_index("src")
    upper = lax.axis_index("ccd")
    for shift in range(lax.axis_size("src").bit_length() - 1):
        upper = upper ^ ((place >> shift) & 1)
    return [upper, place & 1]


def solve_kernel(parts, sums_ref, out_ref, edges_ref):
    owned = out_ref.shape[0] // 4
    ring = -(-(owned + 2) // SUB) * SUB
    order = {pair: n for n, pair in enumerate(PAIRS)}
    row, lane = iota((ring, LANES), 0), iota((ring, LANES), 1)
    inside = row < owned
    after = (row == owned) & (lane < REACH)
    before = (row == ring - 1) & (lane >= LANES - REACH)
    part = 0 if parts == 1 else sum(bit << i for i, bit in enumerate(reversed(part_bits())))
    edge = (part == parts - 1) * jnp.ones((), jnp.int32)
    known = jnp.where(after & (jnp.full((ring, LANES), edge, jnp.int32) == 1), 0.0, 1.0)

    back = LANES - REACH - WINDOW * (SUB - 1)
    for i in range(halo_rows()):
        packed = sums_ref[QUANTITIES * owned + i : QUANTITIES * owned + i + 1, :]
        edges_ref[i * SUB : (i + 1) * SUB, :] = slots_of(jnp.broadcast_to(packed, (SUB, LANES)), back)

    def load(q):
        rows = sums_ref[q * owned : (q + 1) * owned, :]
        place = q if q < 3 else q + SUB - 3
        slot = place // SUB * SUB + SUB - 1 - place % SUB
        rest = jnp.broadcast_to(edges_ref[slot : slot + 1, :], (ring - owned, LANES))
        return jnp.where(inside | after | before, jnp.concatenate([rows, rest], 0), 0.0)

    def turn(value, n):
        turned = pltpu.roll(value, n % LANES, 1)
        if n > 0:
            return jnp.where(lane < n, pltpu.roll(turned, 1, 0), turned)
        return jnp.where(lane >= LANES + n, pltpu.roll(turned, ring - 1, 0), turned)

    loaded = [load(q) for q in range(QUANTITIES)]

    def band(delta, x, y):
        return loaded[3 + delta * 6 + order[min(x, y), max(x, y)]]

    rhs = loaded[:3]
    scale = [relax_step / (att_ridge + band(0, x, x)) * known for x in range(3)]
    coefs = [rhs[x] * scale[x] for x in range(3)]
    for _ in range(1, ITERS):
        ahead = {(y, delta): turn(coefs[y], -delta) for y in range(3) for delta in range(1, 4)}
        fresh = []
        for x in range(3):
            normal = att_ridge * coefs[x]
            for y in range(3):
                normal = normal + band(0, x, y) * coefs[y]
            for delta in range(1, 4):
                for y in range(3):
                    normal = normal + band(delta, x, y) * ahead[y, delta]
                normal = normal + turn(sum(band(delta, x, y) * coefs[y] for y in range(3)), delta)
            fresh.append(coefs[x] + scale[x] * (rhs[x] - normal))
        coefs = fresh
    for x in range(3):
        for r in range(owned):
            out_ref[pl.ds(r * 4 + x, 1), :] = coefs[x][r : r + 1]


def prepare_kernel(_, live_ref, phase_ref, axis_ref, out_ref, tiled):
    by_tile(axis_ref, tiled)

    def group(start, steps):
        for part in range(steps // SUB):
            at = pl.ds(start + part * SUB, SUB)
            basis = [b * live_ref[at, :] for b in spline_basis(phase_ref[at, :])]
            for x in range(3):
                along = tiled[across(start + part * SUB, x), :]
                for j in range(4):
                    out_ref[x * 4 + j, at, :] = along * basis[j]

    over_steps(phase_ref.shape[0], group)


def predict_kernel(coef_ref, factor_ref, resid_ref, knot_ref, att_ref, out_ref, windows):
    tiles, shards = resid_ref.shape[0], coef_ref.shape[0]
    rep = tiles // shards
    for x in range(3):
        coefs = coef_ref[:, x, :]
        for j in range(4):
            windows[x * 4 + j] = coefs if j == 0 else shift_down(coefs, j)
        att_ref[x : x + 1, :] = windows[x * 4, pl.ds(lax.axis_index("src"), 1), :]
    row = iota((SUB, LANES), 0)

    def group(start, steps):
        for part in range(steps // SUB):
            at = pl.ds(start + part * SUB, SUB)
            knots = knot_ref[at, :]
            first = (start + part * SUB) // rep
            left = resid_ref[at, :]
            for q in range(12):
                table = jnp.broadcast_to(windows[q, pl.ds(first, 1), :], (SUB, LANES))
                for k in range(1, SUB // rep):
                    later = jnp.broadcast_to(windows[q, pl.ds(first + k, 1), :], (SUB, LANES))
                    table = jnp.where(row >= k * rep, later, table)
                left = left - factor_ref[q, at, :] * jnp.take_along_axis(table, knots, axis=1)
            out_ref[at, :] = left

    over_steps(tiles, group)


BOTH = ("src", "ccd")
SMEM = pl.BlockSpec(memory_space=pltpu.SMEM)
VMEM = pl.BlockSpec(memory_space=pltpu.VMEM)
HBM = pl.BlockSpec(memory_space=pltpu.HBM)


def call(kernel, name, scalars, arrays, outs, scratch, space=VMEM):
    return pl.pallas_call(
        kernel,
        name=name,
        out_shape=outs,
        in_specs=[SMEM] * len(scalars) + [space] * len(arrays),
        out_specs=jax.tree.map(lambda _: VMEM, outs),
        scratch_shapes=scratch,
        compiler_params=pltpu.CompilerParams(vmem_limit_bytes=8 << 20),
    )(*scalars, *arrays)


def swapped(value, axis, bit):
    size = lax.axis_size(axis)
    return lax.ppermute(value, axis, [(i, i ^ bit) for i in range(size)])


def summed_over(value, axis):
    size = lax.axis_size(axis)
    if size & (size - 1):
        return lax.psum(value, axis)
    bit = 1
    while bit < size:
        value = value + swapped(value, axis, bit)
        bit *= 2
    return value


def halved(value, mask, keep):
    pair = value.reshape((2, value.shape[0] // 2) + value.shape[1:])
    kept = lax.dynamic_index_in_dim(pair, keep, 0, False)
    sent = lax.dynamic_index_in_dim(pair, 1 - keep, 0, False)
    return kept + swapped(sent, BOTH, mask)


def doubled(value, mask, keep):
    other = swapped(value, BOTH, mask)
    first = jnp.where(keep == 0, value, other)
    second = jnp.where(keep == 0, other, value)
    return jnp.concatenate([first, second], 0)


def on_device(design, observed, weight, phase_frac, axis_factors, source_index, knot_index, counts):
    row_count = observed.shape[0]
    tiles = row_count // LANES
    shards = lax.axis_size("src")
    obs, w, phase, index, knots = (
        a.reshape(tiles, LANES) for a in (observed, weight, phase_frac, source_index, knot_index)
    )
    tiled = pltpu.VMEM((tiles * SUB, LANES), f32)
    dense = pltpu.VMEM((tiles, LANES), f32)
    blocks = SRC_DEV // LANES
    inputs = (w, index, obs, design, phase, axis_factors, knots)
    moments, live, w, index, obs, design, phase, axis_factors, knots = call(
        source_kernel, "source_sums", [],
        [pltpu.with_memory_space_constraint(a, pltpu.HBM) for a in (counts,) + inputs],
        (jax.ShapeDtypeStruct((SIGNALS, blocks, LANES), f32), jax.ShapeDtypeStruct((tiles, LANES), f32))
        + tuple(jax.ShapeDtypeStruct(a.shape, a.dtype) for a in inputs),
        [
            pltpu.SMEM(counts.shape, jnp.int32), pltpu.SemaphoreType.DMA((8,)), dense, dense,
            pltpu.VMEM((SRC_DEV // LOW * 64, LOW), f32), tiled,
        ],
        HBM,
    )
    band = call(
        band_kernel, "band_sums", [], [phase, axis_factors, w, knots],
        jax.ShapeDtypeStruct((24 * shards, KNOT_DEV), f32),
        [tiled, tiled, pltpu.VMEM((shards * 48, KNOT_DEV), f32)],
    )
    if lax.axis_size("ccd") == 2:
        other = swapped(moments, "ccd", 1)
    else:
        moments = summed_over(moments, "ccd")
        other = jnp.zeros_like(moments)
    fast = lax.axis_size("ccd") == 2 and shards >= 4 and shards & (shards - 1) == 0
    parts = 4 if fast else 1
    owned = shards // parts
    message_rows = -(-(QUANTITIES * owned + halo_rows()) // SUB) * SUB
    params, resid, message = call(
        resid_kernel, "residuals", [],
        [moments, other, band, live, design, obs, w, index, phase, axis_factors, knots],
        (
            jax.ShapeDtypeStruct((5, SRC_DEV), f32),
            jax.ShapeDtypeStruct((tiles, LANES), f32),
            jax.ShapeDtypeStruct((parts, message_rows, LANES), f32),
        ),
        [tiled, tiled, tiled, pltpu.VMEM((shards * 16, KNOT_DEV), f32), pltpu.VMEM((5, blocks, LANES), f32),
         pltpu.VMEM((3 * shards, KNOT_DEV), f32)],
    )
    factors = call(
        prepare_kernel, "prepare", [], [message, live, phase, axis_factors],
        jax.ShapeDtypeStruct((12, tiles, LANES), f32), [tiled],
    )
    if fast:
        upper, lower = part_bits()
        sums = halved(halved(message, 1, upper), 3, lower)[0]
        bit = 2
        while bit < shards:
            sums = sums + swapped(sums, BOTH, 2 * bit + 1)
            bit *= 2
    else:
        sums = summed_over(summed_over(message[0], "ccd"), "src")
    coefs = call(
        functools.partial(solve_kernel, parts), "attitude", [], [sums],
        jax.ShapeDtypeStruct((owned * 4, LANES), f32), [pltpu.VMEM((halo_rows() * SUB, LANES), f32)],
    )
    if fast:
        coefs = doubled(doubled(coefs, 3, lower), 1, upper)
    attitude, residual = call(
        predict_kernel, "predict", [], [coefs.reshape(shards, 4, LANES), factors, resid, knots],
        (jax.ShapeDtypeStruct((3, KNOT_DEV), f32), jax.ShapeDtypeStruct((tiles, LANES), f32)),
        [pltpu.VMEM((12, shards, KNOT_DEV), f32)],
    )
    return params, attitude, residual.reshape(row_count)


def solution(mesh):
    rows = P(("src", "ccd"))
    wide = P(None, ("src", "ccd"))
    in_specs = (wide, rows, rows, rows, wide, rows, rows, P("src", "ccd", None))
    out_specs = (P(None, "src"), P(None, "src"), rows)
    return jax.shard_map(on_device, mesh=mesh, in_specs=in_specs, out_specs=out_specs, check_vma=False)
```

```python
import functools
import math

import jax
import jax.numpy as jnp
from jax import lax
from jax.experimental import pallas as pl
from jax.experimental.pallas import tpu as pltpu
from jax.sharding import PartitionSpec as P

SRC_DEV = 1024
KNOT_DEV = 128
ITERS = 3
LANES = 128
SUB = 8
LOW = 256
QUANTITIES = 3 + 4 * 6
REACH = 3 * (ITERS - 1)
WINDOW = 2 * REACH
CUBICS = [(1.0, 0.0, 0.0, 0.0), (4.0, 12.0, 6.0, 1.0), (1.0, 6.0, 12.0, 4.0), (0.0, 0.0, 0.0, 1.0)]
SIGNALS = 15 + 5
PAIRS = [(x, y) for x in range(3) for y in range(x, 3)]

src_ridge = 1.0
att_ridge = 1.0
relax_step = 0.15

f32 = jnp.float32
bf16 = jnp.bfloat16


def bernstein_products():
    table = {}
    for i in range(4):
        for j in range(i, 4):
            coefs = [0.0] * 7
            for p in range(4):
                for q in range(4):
                    coefs[p + q] += CUBICS[i][p] * CUBICS[j][q] / 36.0
            table[i, j] = coefs
    return table


def split2(value):
    high = value.astype(bf16).astype(f32)
    return [high, value - high]


def split3(value):
    high = value.astype(bf16).astype(f32)
    rest = value - high
    middle = rest.astype(bf16).astype(f32)
    return [high, middle, rest - middle]


def spline_basis(phase_rows):
    remain = 1.0 - phase_rows
    square = phase_rows * phase_rows
    cube_term = square * phase_rows
    return [
        remain * remain * remain / 6.0,
        (3.0 * cube_term - 6.0 * square + 4.0) / 6.0,
        (-3.0 * cube_term + 3.0 * square + 3.0 * phase_rows + 1.0) / 6.0,
        cube_term / 6.0,
    ]


def solve_small(moments):
    matrix = {}
    position = 0
    for m in range(5):
        for n in range(m, 5):
            matrix[m, n] = moments[position] + (src_ridge if m == n else 0.0)
            position += 1
    scaled, factor, inverse = {}, {}, {}
    for j in range(5):
        for i in range(j, 5):
            running = matrix[j, i]
            for k in range(j):
                running = running - scaled[i, k] * factor[j, k]
            scaled[i, j] = running
        inverse[j] = 1.0 / scaled[j, j]
        for i in range(j + 1, 5):
            factor[i, j] = scaled[i, j] * inverse[j]
    forward = []
    for i in range(5):
        running = moments[15 + i]
        for k in range(i):
            running = running - factor[i, k] * forward[k]
        forward.append(running)
    solved = [None] * 5
    for i in reversed(range(5)):
        running = forward[i] * inverse[i]
        for k in range(i + 1, 5):
            running = running - factor[k, i] * solved[k]
        solved[i] = running
    return solved


def iota(shape, axis):
    return lax.broadcasted_iota(jnp.int32, shape, axis)


def over_steps(tiles, body):
    steps = math.gcd(tiles, 64)
    if steps == tiles:
        body(0, steps)
        return

    def one(g, _):
        body(pl.multiple_of(g * steps, steps), steps)
        return 0

    lax.fori_loop(0, tiles // steps, one, 0)


def spread_row(index_row, count):
    packed = jnp.broadcast_to(index_row, (2 * SUB, LANES)).astype(bf16)
    return jnp.concatenate([packed] * (count // (2 * SUB)), 0)


def is_equal(left, right):
    return jnp.where(left == right, jnp.ones((), bf16), jnp.zeros((), bf16))


def onehot(index_row, count):
    return is_equal(iota((count, LANES), 0).astype(f32).astype(bf16), spread_row(index_row, count))


def by_tile(wide_ref, tiled_ref):
    rows = wide_ref.shape[0]
    for t in range(tiled_ref.shape[0] // SUB):
        tiled_ref[t * SUB : t * SUB + rows, :] = wide_ref[:, t * LANES : (t + 1) * LANES]


def by_group(tiles):
    return range(0, tiles, SUB)


def across(start, row):
    return pl.ds(start * SUB + row, SUB, stride=SUB)


def tile_of(tiled_ref, t):
    return tiled_ref[pl.ds(t * SUB, SUB), :]


def low_bits(index, size):
    return index >> (size.bit_length() - 1), index & (size - 1)


def row_of(ref, t):
    return jnp.broadcast_to(ref[pl.ds(t, 1), :], (SUB, LANES))


def per_sublane(values, kind):
    row = iota((SUB, LANES), 0)
    out = jnp.full((SUB, LANES), values[0], kind)
    for s in range(1, SUB):
        if values[s] != values[0]:
            out = jnp.where(row == s, jnp.full((SUB, LANES), values[s], kind), out)
    return out


def pick_rows(value, pattern):
    return jnp.take_along_axis(value, pattern, axis=0)


def patterns(values):
    values = list(values) + [0] * (-len(values) % SUB)
    return [per_sublane(values[i : i + SUB], jnp.int32) for i in range(0, len(values), SUB)]


def stacked_parts(values, split):
    parts = split(jnp.concatenate(values, 0))
    if len(parts) * parts[0].shape[0] % (2 * SUB):
        parts.append(jnp.zeros((SUB, LANES), f32))
    return jnp.concatenate(parts, 0).astype(bf16)


def sum_parts(value, rows, count):
    return sum(value[i * rows : (i + 1) * rows] for i in range(count))


def add_blocks(moments_ref, start, steps, rep, rows, count, left_of, knot_ref):
    per_block = min(rep, steps)
    for b in range(steps // per_block):
        lefts, rights = [], []
        for i in range(b * per_block, (b + 1) * per_block):
            lefts.append(left_of(start + i))
            rights.append(onehot(knot_ref[pl.ds(start + i, 1), :].astype(f32), KNOT_DEV))
        got = contract(jnp.concatenate(lefts, 1), jnp.concatenate(rights, 1))
        summed = sum_parts(got, rows, count)
        where_to = (start + b * per_block) // rep
        where_to = pl.ds(where_to * rows, rows)
        if rep <= steps:
            moments_ref[where_to, :] = summed
        else:
            moments_ref[where_to, :] += summed


def contract(left, right):
    return lax.dot_general(left, right, (((1,), (1,)), ((), ())), preferred_element_type=f32)


def shift_up(value, n):
    turned = pltpu.roll(value, n, 1)
    before = pltpu.roll(turned, 1, 0)
    before = jnp.where(iota(value.shape, 0) == 0, 0.0, before)
    return jnp.where(iota(value.shape, 1) < n, before, turned)


def shift_down(value, n):
    turned = pltpu.roll(value, LANES - n, 1)
    after = pltpu.roll(turned, value.shape[0] - 1, 0)
    after = jnp.where(iota(value.shape, 0) == value.shape[0] - 1, 0.0, after)
    return jnp.where(iota(value.shape, 1) >= LANES - n, after, turned)


def source_kernel(
    counts_hbm, weight_hbm, index_hbm, obs_hbm, design_hbm, phase_hbm, axis_hbm, knot_hbm,
    out_ref, live_ref, weight_ref, index_ref, obs_ref, design_ref, phase_ref, axis_ref, knot_ref,
    counts_ref, sems, low_ref, high_ref, total, tiled,
):
    tiles = obs_ref.shape[0]
    shards = counts_ref.shape[2]
    rep = tiles // shards
    copies = [
        pltpu.make_async_copy(src, dst, sems.at[i])
        for i, (src, dst) in enumerate(
            [(counts_hbm, counts_ref), (weight_hbm, weight_ref), (index_hbm, index_ref), (obs_hbm, obs_ref),
             (design_hbm, design_ref), (phase_hbm, phase_ref), (axis_hbm, axis_ref), (knot_hbm, knot_ref)]
        )
    ]
    for copy in copies:
        copy.start()
    if math.gcd(tiles, 64) != tiles:
        total[...] = jnp.zeros_like(total)
    highs = SRC_DEV // LOW
    pairs = [(m, n) for m in range(5) for n in range(m, 5)] + [(m, 5) for m in range(5)]
    pairs += pairs[2 * SUB :]
    lefts_of = patterns([m for m, _ in pairs])
    rights_of = patterns([n for _, n in pairs])
    first_half = iota((SUB, LANES), 0) < SUB // 2
    copies[0].wait()
    slots = iota((rep, LANES), 0) * LANES + iota((rep, LANES), 1)
    for d in range(shards):
        live_ref[pl.ds(d * rep, rep), :] = (slots < counts_ref[0, 0, d]).astype(f32)
    copies[1].wait()
    copies[2].wait()
    for start in by_group(tiles):
        at = pl.ds(start, SUB)
        weight_ref[at, :] = weight_ref[at, :] * live_ref[at, :]
        high, low = low_bits(index_ref[at, :], LOW)
        high_ref[at, :] = high.astype(f32)
        low_ref[at, :] = low.astype(f32)
    copies[3].wait()
    copies[4].wait()
    by_tile(design_ref, tiled)
    for start in by_group(tiles):
        tiled[across(start, 5), :] = obs_ref[pl.ds(start, SUB), :]

    def group(start, steps):
        lefts, rights = [], []
        for i in range(steps):
            t = start + i
            values = tile_of(tiled, t)
            scaled = values * row_of(weight_ref, t)
            products = [pick_rows(scaled, m) * pick_rows(values, n) for m, n in zip(lefts_of, rights_of)]
            high, middle, low = split3(products[2])
            parts = split3(jnp.concatenate(products[:2], 0)) + [jnp.where(first_half, high, middle), low]
            block = jnp.concatenate(parts, 0).astype(bf16)
            packed = spread_row(high_ref[pl.ds(t, 1), :], 2 * SUB)
            masks = [is_equal(packed, jnp.full((), h, bf16)) for h in range(highs)]
            repeats = block.shape[0] // (2 * SUB)
            lefts.append(jnp.concatenate([block * jnp.concatenate([mask] * repeats, 0) for mask in masks], 0))
            rights.append(onehot(low_ref[pl.ds(t, 1), :], LOW))
        got = contract(jnp.concatenate(lefts, 1), jnp.concatenate(rights, 1))
        if steps == tiles:
            total[...] = got
        else:
            total[...] += got

    over_steps(tiles, group)
    for copy in copies[5:]:
        copy.wait()
    height = total.shape[0] // highs
    wide, half_tile = 2 * SUB, SUB // 2
    for h in range(highs):
        block = total[h * height : (h + 1) * height, :]
        tail = block[3 * wide :]
        summed = sum_parts(block, wide, 3)
        rest = tail[0:half_tile] + tail[half_tile : 2 * half_tile] + tail[2 * half_tile : 3 * half_tile]
        for half in range(LOW // LANES):
            cols = slice(half * LANES, (half + 1) * LANES)
            out_ref[0:wide, h * (LOW // LANES) + half, :] = summed[:, cols]
            out_ref[wide:SIGNALS, h * (LOW // LANES) + half, :] = rest[:, cols]


def band_kernel(phase_ref, axis_ref, weight_ref, knot_ref, out_ref, tiled, powers_ref, moments):
    tiles, shards = phase_ref.shape[0], out_ref.shape[0] // 24
    rep = tiles // shards
    by_tile(axis_ref, tiled)
    rows = moments.shape[0] // shards
    lefts_of = patterns([PAIRS[q % 6][0] for q in range(24)])
    rights_of = patterns([PAIRS[q % 6][1] for q in range(24)])
    powers_of = patterns([q // 6 if q < 42 else 0 for q in range(rows)])
    for start in by_group(tiles):
        at = pl.ds(start, SUB)
        u = phase_ref[at, :]
        r = 1.0 - u
        u2, r2 = u * u, r * r
        u3, r3 = u2 * u, r2 * r
        w = weight_ref[at, :]
        u3w, r3w = u3 * w, r3 * w
        powers = [r3w * r3, r3w * (r2 * u), r3w * (r * u2), r3w * u3, u3w * (r2 * u), u3w * (r * u2), u3w * u3]
        for p in range(7):
            powers_ref[across(start, p), :] = powers[p]

    def left_of(t):
        axes = tile_of(tiled, t)
        powers = tile_of(powers_ref, t)
        products = [pick_rows(axes, x) * pick_rows(axes, y) for x, y in zip(lefts_of, rights_of)]
        return stacked_parts([products[i % 3] * pick_rows(powers, p) for i, p in enumerate(powers_of)], split2)

    def group(start, steps):
        add_blocks(moments, start, steps, rep, rows, 2, left_of, knot_ref)

    if rep > math.gcd(tiles, 64):
        moments[...] = jnp.zeros_like(moments)
    over_steps(tiles, group)
    table = bernstein_products()
    for n in range(6):
        parts = [moments[pl.ds(p * 6 + n, shards, stride=rows), :] for p in range(7)]

        def product(i, j):
            return sum(c * part for c, part in zip(table[i, j], parts) if c)

        for delta in range(4):
            running = product(3 - delta, 3)
            for j in reversed(range(3 - delta)):
                running = product(j, j + delta) + shift_up(running, 1)
            to = (delta * 6 + n) * shards
            out_ref[to : to + shards, :] = running


def halo_rows():
    return 1 + (QUANTITIES - 3) // SUB


def slots_of(value, shift):
    return pltpu.roll(value, shift, 1, stride=WINDOW, stride_axis=0)


def pack(source_ref, first, count, row, message_ref):
    parts, shards = message_ref.shape[0], source_ref.shape[0] // count
    owned = shards // parts
    lane, slot = iota((SUB, LANES), 1), iota((SUB, LANES), 0)
    mine = (lane >= WINDOW * slot) & (lane < WINDOW * (slot + 1)) & (slot < count)
    zero = jnp.zeros((SUB, LANES), f32)
    for base in range(0, count, SUB):
        for q in range(base, min(base + SUB, count)):
            for p in range(parts):
                at = q * shards + p * owned
                to = (first + q) * owned
                message_ref[p, to : to + owned, :] = source_ref[at : at + owned, :]
        for p in range(parts):
            taken = min(count, SUB)

            def edge(r):
                got = source_ref[pl.ds(base * shards + r, taken, stride=shards), :]
                return got if taken == SUB else jnp.concatenate([got, zero[taken:]], 0)

            after = edge((p + 1) * owned) if p < parts - 1 else zero
            before = edge(p * owned - 1) if p else zero
            packed = slots_of(jnp.where(lane < LANES // 2, after, before), REACH)
            to = QUANTITIES * owned + row + base // SUB
            message_ref[p, to : to + 1, :] = jnp.sum(jnp.where(mine, packed, 0.0), 0, keepdims=True)


def resid_kernel(
    mine_ref, other_ref, band_ref, live_ref, design_ref, obs_ref, weight_ref, index_ref, phase_ref, axis_ref, knot_ref,
    params_ref, resid_ref, message_ref, tiled, tiled_axis, splines_ref, moments, solved_ref, rhs_ref,
):
    tiles, shards = obs_ref.shape[0], rhs_ref.shape[0] // 3
    rep = tiles // shards
    by_tile(design_ref, tiled)
    by_tile(axis_ref, tiled_axis)
    solved = solve_small([mine_ref[q] + other_ref[q] for q in range(SIGNALS)])
    blocks = SRC_DEV // LANES
    for m in range(5):
        solved_ref[m] = solved[m]
        for b in range(blocks):
            params_ref[m : m + 1, b * LANES : (b + 1) * LANES] = solved[m][b : b + 1, :]
    rows = moments.shape[0] // shards
    axes_of = patterns([q % 3 for q in range(rows)])
    splines_of = patterns([min(q // 3, 3) for q in range(rows)])

    def left_of(t):
        axes = tile_of(tiled_axis, t)
        splines = tile_of(splines_ref, t)
        return stacked_parts([pick_rows(axes, x) * pick_rows(splines, j) for x, j in zip(axes_of, splines_of)], split3)

    def group(start, steps):
        for part in range(steps // SUB):
            at = pl.ds(start + part * SUB, SUB)
            live = live_ref[at, :]
            block_of, lane_of = low_bits(index_ref[at, :], LANES)
            hits = [block_of == b for b in range(blocks)]
            left = obs_ref[at, :]
            for m in range(5):
                for b in range(blocks):
                    table = jnp.broadcast_to(solved_ref[m, b : b + 1, :], (SUB, LANES))
                    found = jnp.take_along_axis(table, lane_of, axis=1)
                    picked = jnp.where(hits[b], found, picked) if b else found
                left = left - tiled[across(start + part * SUB, m), :] * picked
            resid = live * left
            resid_ref[at, :] = resid
            scaled = weight_ref[at, :] * resid
            for j, basis in enumerate(spline_basis(phase_ref[at, :])):
                splines_ref[across(start + part * SUB, j), :] = basis * scaled
        add_blocks(moments, start, steps, rep, rows, 3, left_of, knot_ref)

    if rep > math.gcd(tiles, 64):
        moments[...] = jnp.zeros_like(moments)
    over_steps(tiles, group)
    for x in range(3):
        running = moments[pl.ds(9 + x, shards, stride=rows), :]
        for j in reversed(range(3)):
            running = moments[pl.ds(j * 3 + x, shards, stride=rows), :] + shift_up(running, 1)
        rhs_ref[x * shards : (x + 1) * shards, :] = running
    pack(rhs_ref, 0, 3, 0, message_ref)
    pack(band_ref, 3, QUANTITIES - 3, 1, message_ref)


def part_bits():
    place = lax.axis_index("src")
    upper = lax.axis_index("ccd")
    for shift in range(lax.axis_size("src").bit_length() - 1):
        upper = upper ^ ((place >> shift) & 1)
    return [upper, place & 1]


def solve_kernel(parts, sums_ref, out_ref, edges_ref):
    owned = out_ref.shape[0] // 4
    ring = -(-(owned + 2) // SUB) * SUB
    order = {pair: n for n, pair in enumerate(PAIRS)}
    row, lane = iota((ring, LANES), 0), iota((ring, LANES), 1)
    inside = row < owned
    after = (row == owned) & (lane < REACH)
    before = (row == ring - 1) & (lane >= LANES - REACH)
    part = 0 if parts == 1 else sum(bit << i for i, bit in enumerate(reversed(part_bits())))
    edge = (part == parts - 1) * jnp.ones((), jnp.int32)
    known = jnp.where(after & (jnp.full((ring, LANES), edge, jnp.int32) == 1), 0.0, 1.0)

    back = LANES - REACH - WINDOW * (SUB - 1)
    for i in range(halo_rows()):
        packed = sums_ref[QUANTITIES * owned + i : QUANTITIES * owned + i + 1, :]
        edges_ref[i * SUB : (i + 1) * SUB, :] = slots_of(jnp.broadcast_to(packed, (SUB, LANES)), back)

    def load(q):
        rows = sums_ref[q * owned : (q + 1) * owned, :]
        place = q if q < 3 else q + SUB - 3
        slot = place // SUB * SUB + SUB - 1 - place % SUB
        rest = jnp.broadcast_to(edges_ref[slot : slot + 1, :], (ring - owned, LANES))
        return jnp.where(inside | after | before, jnp.concatenate([rows, rest], 0), 0.0)

    def turn(value, n):
        turned = pltpu.roll(value, n % LANES, 1)
        if n > 0:
            return jnp.where(lane < n, pltpu.roll(turned, 1, 0), turned)
        return jnp.where(lane >= LANES + n, pltpu.roll(turned, ring - 1, 0), turned)

    loaded = [load(q) for q in range(QUANTITIES)]

    def band(delta, x, y):
        return loaded[3 + delta * 6 + order[min(x, y), max(x, y)]]

    rhs = loaded[:3]
    scale = [relax_step / (att_ridge + band(0, x, x)) * known for x in range(3)]
    coefs = [rhs[x] * scale[x] for x in range(3)]
    for _ in range(1, ITERS):
        ahead = {(y, delta): turn(coefs[y], -delta) for y in range(3) for delta in range(1, 4)}
        fresh = []
        for x in range(3):
            normal = att_ridge * coefs[x]
            for y in range(3):
                normal = normal + band(0, x, y) * coefs[y]
            for delta in range(1, 4):
                for y in range(3):
                    normal = normal + band(delta, x, y) * ahead[y, delta]
                normal = normal + turn(sum(band(delta, x, y) * coefs[y] for y in range(3)), delta)
            fresh.append(coefs[x] + scale[x] * (rhs[x] - normal))
        coefs = fresh
    for x in range(3):
        for r in range(owned):
            out_ref[pl.ds(r * 4 + x, 1), :] = coefs[x][r : r + 1]


def prepare_kernel(_, live_ref, phase_ref, axis_ref, out_ref, tiled):
    by_tile(axis_ref, tiled)

    def group(start, steps):
        for part in range(steps // SUB):
            at = pl.ds(start + part * SUB, SUB)
            basis = [b * live_ref[at, :] for b in spline_basis(phase_ref[at, :])]
            for x in range(3):
                along = tiled[across(start + part * SUB, x), :]
                for j in range(4):
                    out_ref[x * 4 + j, at, :] = along * basis[j]

    over_steps(phase_ref.shape[0], group)


def predict_kernel(coef_ref, factor_ref, resid_ref, knot_ref, att_ref, out_ref, windows):
    tiles, shards = resid_ref.shape[0], coef_ref.shape[0]
    rep = tiles // shards
    for x in range(3):
        coefs = coef_ref[:, x, :]
        for j in range(4):
            windows[x * 4 + j] = coefs if j == 0 else shift_down(coefs, j)
        att_ref[x : x + 1, :] = windows[x * 4, pl.ds(lax.axis_index("src"), 1), :]
    row = iota((SUB, LANES), 0)

    def group(start, steps):
        for part in range(steps // SUB):
            at = pl.ds(start + part * SUB, SUB)
            knots = knot_ref[at, :]
            first = (start + part * SUB) // rep
            left = resid_ref[at, :]
            for q in range(12):
                table = jnp.broadcast_to(windows[q, pl.ds(first, 1), :], (SUB, LANES))
                for k in range(1, SUB // rep):
                    later = jnp.broadcast_to(windows[q, pl.ds(first + k, 1), :], (SUB, LANES))
                    table = jnp.where(row >= k * rep, later, table)
                left = left - factor_ref[q, at, :] * jnp.take_along_axis(table, knots, axis=1)
            out_ref[at, :] = left

    over_steps(tiles, group)


BOTH = ("src", "ccd")
SMEM = pl.BlockSpec(memory_space=pltpu.SMEM)
VMEM = pl.BlockSpec(memory_space=pltpu.VMEM)
HBM = pl.BlockSpec(memory_space=pltpu.HBM)


def call(kernel, name, scalars, arrays, outs, scratch, space=VMEM):
    return pl.pallas_call(
        kernel,
        name=name,
        out_shape=outs,
        in_specs=[SMEM] * len(scalars) + [space] * len(arrays),
        out_specs=jax.tree.map(lambda _: VMEM, outs),
        scratch_shapes=scratch,
        compiler_params=pltpu.CompilerParams(vmem_limit_bytes=8 << 20),
    )(*scalars, *arrays)


def swapped(value, axis, bit):
    size = lax.axis_size(axis)
    return lax.ppermute(value, axis, [(i, i ^ bit) for i in range(size)])


def summed_over(value, axis):
    size = lax.axis_size(axis)
    if size & (size - 1):
        return lax.psum(value, axis)
    bit = 1
    while bit < size:
        value = value + swapped(value, axis, bit)
        bit *= 2
    return value


def halved(value, mask, keep):
    pair = value.reshape((2, value.shape[0] // 2) + value.shape[1:])
    kept = lax.dynamic_index_in_dim(pair, keep, 0, False)
    sent = lax.dynamic_index_in_dim(pair, 1 - keep, 0, False)
    return kept + swapped(sent, BOTH, mask)


def doubled(value, mask, keep):
    other = swapped(value, BOTH, mask)
    first = jnp.where(keep == 0, value, other)
    second = jnp.where(keep == 0, other, value)
    return jnp.concatenate([first, second], 0)


def on_device(design, observed, weight, phase_frac, axis_factors, source_index, knot_index, counts):
    row_count = observed.shape[0]
    tiles = row_count // LANES
    shards = lax.axis_size("src")
    obs, w, phase, index, knots = (
        a.reshape(tiles, LANES) for a in (observed, weight, phase_frac, source_index, knot_index)
    )
    tiled = pltpu.VMEM((tiles * SUB, LANES), f32)
    dense = pltpu.VMEM((tiles, LANES), f32)
    blocks = SRC_DEV // LANES
    inputs = (w, index, obs, design, phase, axis_factors, knots)
    moments, live, w, index, obs, design, phase, axis_factors, knots = call(
        source_kernel, "source_sums", [],
        [pltpu.with_memory_space_constraint(a, pltpu.HBM) for a in (counts,) + inputs],
        (jax.ShapeDtypeStruct((SIGNALS, blocks, LANES), f32), jax.ShapeDtypeStruct((tiles, LANES), f32))
        + tuple(jax.ShapeDtypeStruct(a.shape, a.dtype) for a in inputs),
        [
            pltpu.SMEM(counts.shape, jnp.int32), pltpu.SemaphoreType.DMA((8,)), dense, dense,
            pltpu.VMEM((SRC_DEV // LOW * 64, LOW), f32), tiled,
        ],
        HBM,
    )
    band = call(
        band_kernel, "band_sums", [], [phase, axis_factors, w, knots],
        jax.ShapeDtypeStruct((24 * shards, KNOT_DEV), f32),
        [tiled, tiled, pltpu.VMEM((shards * 48, KNOT_DEV), f32)],
    )
    if lax.axis_size("ccd") == 2:
        other = swapped(moments, "ccd", 1)
    else:
        moments = summed_over(moments, "ccd")
        other = jnp.zeros_like(moments)
    fast = lax.axis_size("ccd") == 2 and shards >= 4 and shards & (shards - 1) == 0
    parts = 4 if fast else 1
    owned = shards // parts
    message_rows = -(-(QUANTITIES * owned + halo_rows()) // SUB) * SUB
    params, resid, message = call(
        resid_kernel, "residuals", [],
        [moments, other, band, live, design, obs, w, index, phase, axis_factors, knots],
        (
            jax.ShapeDtypeStruct((5, SRC_DEV), f32),
            jax.ShapeDtypeStruct((tiles, LANES), f32),
            jax.ShapeDtypeStruct((parts, message_rows, LANES), f32),
        ),
        [tiled, tiled, tiled, pltpu.VMEM((shards * 16, KNOT_DEV), f32), pltpu.VMEM((5, blocks, LANES), f32),
         pltpu.VMEM((3 * shards, KNOT_DEV), f32)],
    )
    factors = call(
        prepare_kernel, "prepare", [], [message, live, phase, axis_factors],
        jax.ShapeDtypeStruct((12, tiles, LANES), f32), [tiled],
    )
    if fast:
        upper, lower = part_bits()
        sums = halved(halved(message, 1, upper), 3, lower)[0]
        bit = shards // 2
        while bit > 1:
            sums = sums + swapped(sums, BOTH, 2 * bit + 1)
            bit //= 2
    else:
        sums = summed_over(summed_over(message[0], "ccd"), "src")
    coefs = call(
        functools.partial(solve_kernel, parts), "attitude", [], [sums],
        jax.ShapeDtypeStruct((owned * 4, LANES), f32), [pltpu.VMEM((halo_rows() * SUB, LANES), f32)],
    )
    if fast:
        coefs = doubled(doubled(coefs, 3, lower), 1, upper)
    attitude, residual = call(
        predict_kernel, "predict", [], [coefs.reshape(shards, 4, LANES), factors, resid, knots],
        (jax.ShapeDtypeStruct((3, KNOT_DEV), f32), jax.ShapeDtypeStruct((tiles, LANES), f32)),
        [pltpu.VMEM((12, shards, KNOT_DEV), f32)],
    )
    return params, attitude, residual.reshape(row_count)


def solution(mesh):
    rows = P(("src", "ccd"))
    wide = P(None, ("src", "ccd"))
    in_specs = (wide, rows, rows, rows, wide, rows, rows, P("src", "ccd", None))
    out_specs = (P(None, "src"), P(None, "src"), rows)
    return jax.shard_map(on_device, mesh=mesh, in_specs=in_specs, out_specs=out_specs, check_vma=False)
```

```python
import functools
import math

import jax
import jax.numpy as jnp
from jax import lax
from jax.experimental import pallas as pl
from jax.experimental.pallas import tpu as pltpu
from jax.sharding import PartitionSpec as P

SRC_DEV = 1024
KNOT_DEV = 128
ITERS = 3
LANES = 128
SUB = 8
LOW = 256
QUANTITIES = 3 + 4 * 6
REACH = 3 * (ITERS - 1)
WINDOW = 2 * REACH
CUBICS = [(1.0, 0.0, 0.0, 0.0), (4.0, 12.0, 6.0, 1.0), (1.0, 6.0, 12.0, 4.0), (0.0, 0.0, 0.0, 1.0)]
SIGNALS = 15 + 5
PAIRS = [(x, y) for x in range(3) for y in range(x, 3)]

src_ridge = 1.0
att_ridge = 1.0
relax_step = 0.15

f32 = jnp.float32
bf16 = jnp.bfloat16


def bernstein_products():
    table = {}
    for i in range(4):
        for j in range(i, 4):
            coefs = [0.0] * 7
            for p in range(4):
                for q in range(4):
                    coefs[p + q] += CUBICS[i][p] * CUBICS[j][q] / 36.0
            table[i, j] = coefs
    return table


def split2(value):
    high = value.astype(bf16)
    return [high, (value - high.astype(f32)).astype(bf16)]


def split3(value):
    high = value.astype(bf16).astype(f32)
    rest = value - high
    middle = rest.astype(bf16).astype(f32)
    return [high, middle, rest - middle]


def spline_basis(phase_rows):
    remain = 1.0 - phase_rows
    square = phase_rows * phase_rows
    cube_term = square * phase_rows
    return [
        remain * remain * remain / 6.0,
        (3.0 * cube_term - 6.0 * square + 4.0) / 6.0,
        (-3.0 * cube_term + 3.0 * square + 3.0 * phase_rows + 1.0) / 6.0,
        cube_term / 6.0,
    ]


def solve_small(moments):
    matrix = {}
    position = 0
    for m in range(5):
        for n in range(m, 5):
            matrix[m, n] = moments[position] + (src_ridge if m == n else 0.0)
            position += 1
    scaled, factor, inverse = {}, {}, {}
    for j in range(5):
        for i in range(j, 5):
            running = matrix[j, i]
            for k in range(j):
                running = running - scaled[i, k] * factor[j, k]
            scaled[i, j] = running
        inverse[j] = 1.0 / scaled[j, j]
        for i in range(j + 1, 5):
            factor[i, j] = scaled[i, j] * inverse[j]
    forward = []
    for i in range(5):
        running = moments[15 + i]
        for k in range(i):
            running = running - factor[i, k] * forward[k]
        forward.append(running)
    solved = [None] * 5
    for i in reversed(range(5)):
        running = forward[i] * inverse[i]
        for k in range(i + 1, 5):
            running = running - factor[k, i] * solved[k]
        solved[i] = running
    return solved


def iota(shape, axis):
    return lax.broadcasted_iota(jnp.int32, shape, axis)


def over_steps(tiles, body):
    steps = math.gcd(tiles, 64)
    if steps == tiles:
        body(0, steps)
        return

    def one(g, _):
        body(pl.multiple_of(g * steps, steps), steps)
        return 0

    lax.fori_loop(0, tiles // steps, one, 0)


def spread_row(index_row, count):
    packed = jnp.broadcast_to(index_row, (2 * SUB, LANES)).astype(bf16)
    return jnp.concatenate([packed] * (count // (2 * SUB)), 0)


def is_equal(left, right):
    return jnp.where(left == right, jnp.ones((), bf16), jnp.zeros((), bf16))


def onehot(index_row, count):
    return is_equal(iota((count, LANES), 0).astype(f32).astype(bf16), spread_row(index_row, count))


def by_tile(wide_ref, tiled_ref):
    rows = wide_ref.shape[0]
    for t in range(tiled_ref.shape[0] // SUB):
        tiled_ref[t * SUB : t * SUB + rows, :] = wide_ref[:, t * LANES : (t + 1) * LANES]


def by_group(tiles):
    return range(0, tiles, SUB)


def across(start, row):
    return pl.ds(start * SUB + row, SUB, stride=SUB)


def tile_of(tiled_ref, t):
    return tiled_ref[pl.ds(t * SUB, SUB), :]


def low_bits(index, size):
    return index >> (size.bit_length() - 1), index & (size - 1)


def row_of(ref, t):
    return jnp.broadcast_to(ref[pl.ds(t, 1), :], (SUB, LANES))


def per_sublane(values, kind):
    row = iota((SUB, LANES), 0)
    out = jnp.full((SUB, LANES), values[0], kind)
    for s in range(1, SUB):
        if values[s] != values[0]:
            out = jnp.where(row == s, jnp.full((SUB, LANES), values[s], kind), out)
    return out


def pick_rows(value, pattern):
    return jnp.take_along_axis(value, pattern, axis=0)


def patterns(values):
    values = list(values) + [0] * (-len(values) % SUB)
    return [per_sublane(values[i : i + SUB], jnp.int32) for i in range(0, len(values), SUB)]


def stacked_parts(values, split):
    parts = split(jnp.concatenate(values, 0))
    if split is split2:
        return jnp.concatenate(parts, 0)
    if len(parts) * parts[0].shape[0] % (2 * SUB):
        parts.append(jnp.zeros((SUB, LANES), f32))
    return jnp.concatenate(parts, 0).astype(bf16)


def sum_parts(value, rows, count):
    return sum(value[i * rows : (i + 1) * rows] for i in range(count))


def add_blocks(moments_ref, start, steps, rep, rows, count, left_of, knot_ref):
    per_block = min(rep, steps)
    for b in range(steps // per_block):
        lefts, rights = [], []
        for i in range(b * per_block, (b + 1) * per_block):
            lefts.append(left_of(start + i))
            rights.append(onehot(knot_ref[pl.ds(start + i, 1), :].astype(f32), KNOT_DEV))
        got = contract(jnp.concatenate(lefts, 1), jnp.concatenate(rights, 1))
        summed = sum_parts(got, rows, count)
        where_to = (start + b * per_block) // rep
        where_to = pl.ds(where_to * rows, rows)
        if rep <= steps:
            moments_ref[where_to, :] = summed
        else:
            moments_ref[where_to, :] += summed


def contract(left, right):
    return lax.dot_general(left, right, (((1,), (1,)), ((), ())), preferred_element_type=f32)


def shift_up(value, n):
    turned = pltpu.roll(value, n, 1)
    before = pltpu.roll(turned, 1, 0)
    before = jnp.where(iota(value.shape, 0) == 0, 0.0, before)
    return jnp.where(iota(value.shape, 1) < n, before, turned)


def shift_down(value, n):
    turned = pltpu.roll(value, LANES - n, 1)
    after = pltpu.roll(turned, value.shape[0] - 1, 0)
    after = jnp.where(iota(value.shape, 0) == value.shape[0] - 1, 0.0, after)
    return jnp.where(iota(value.shape, 1) >= LANES - n, after, turned)


def source_kernel(
    counts_hbm, weight_hbm, index_hbm, obs_hbm, design_hbm, phase_hbm, axis_hbm, knot_hbm,
    out_ref, live_ref, weight_ref, index_ref, obs_ref, design_ref, phase_ref, axis_ref, knot_ref,
    counts_ref, sems, low_ref, high_ref, total, tiled,
):
    tiles = obs_ref.shape[0]
    shards = counts_ref.shape[2]
    rep = tiles // shards
    copies = [
        pltpu.make_async_copy(src, dst, sems.at[i])
        for i, (src, dst) in enumerate(
            [(counts_hbm, counts_ref), (weight_hbm, weight_ref), (index_hbm, index_ref), (obs_hbm, obs_ref),
             (design_hbm, design_ref), (phase_hbm, phase_ref), (axis_hbm, axis_ref), (knot_hbm, knot_ref)]
        )
    ]
    for copy in copies:
        copy.start()
    if math.gcd(tiles, 64) != tiles:
        total[...] = jnp.zeros_like(total)
    highs = SRC_DEV // LOW
    pairs = [(m, n) for m in range(5) for n in range(m, 5)] + [(m, 5) for m in range(5)]
    pairs += pairs[2 * SUB :]
    lefts_of = patterns([m for m, _ in pairs])
    rights_of = patterns([n for _, n in pairs])
    first_half = iota((SUB, LANES), 0) < SUB // 2
    copies[0].wait()
    slots = iota((rep, LANES), 0) * LANES + iota((rep, LANES), 1)
    for d in range(shards):
        live_ref[pl.ds(d * rep, rep), :] = (slots < counts_ref[0, 0, d]).astype(f32)
    copies[1].wait()
    copies[2].wait()
    for start in by_group(tiles):
        at = pl.ds(start, SUB)
        weight_ref[at, :] = weight_ref[at, :] * live_ref[at, :]
        high, low = low_bits(index_ref[at, :], LOW)
        high_ref[at, :] = high.astype(f32)
        low_ref[at, :] = low.astype(f32)
    copies[3].wait()
    copies[4].wait()
    by_tile(design_ref, tiled)
    for start in by_group(tiles):
        tiled[across(start, 5), :] = obs_ref[pl.ds(start, SUB), :]

    def group(start, steps):
        lefts, rights = [], []
        for i in range(steps):
            t = start + i
            values = tile_of(tiled, t)
            scaled = values * row_of(weight_ref, t)
            products = [pick_rows(scaled, m) * pick_rows(values, n) for m, n in zip(lefts_of, rights_of)]
            high, middle, low = split3(products[2])
            parts = split3(jnp.concatenate(products[:2], 0)) + [jnp.where(first_half, high, middle), low]
            block = jnp.concatenate(parts, 0).astype(bf16)
            packed = spread_row(high_ref[pl.ds(t, 1), :], 2 * SUB)
            masks = [is_equal(packed, jnp.full((), h, bf16)) for h in range(highs)]
            repeats = block.shape[0] // (2 * SUB)
            lefts.append(jnp.concatenate([block * jnp.concatenate([mask] * repeats, 0) for mask in masks], 0))
            rights.append(onehot(low_ref[pl.ds(t, 1), :], LOW))
        got = contract(jnp.concatenate(lefts, 1), jnp.concatenate(rights, 1))
        if steps == tiles:
            total[...] = got
        else:
            total[...] += got

    over_steps(tiles, group)
    for copy in copies[5:]:
        copy.wait()
    height = total.shape[0] // highs
    wide, half_tile, blocks = 2 * SUB, SUB // 2, SRC_DEV // LANES
    for h in range(highs):
        sums = total[h * height : (h + 1) * height, :]
        tail = sums[3 * wide :]
        summed = sum_parts(sums, wide, 3)
        rest = tail[0:half_tile] + tail[half_tile : 2 * half_tile] + tail[2 * half_tile : 3 * half_tile]
        for half in range(LOW // LANES):
            cols = slice(half * LANES, (half + 1) * LANES)
            block = h * (LOW // LANES) + half
            out_ref[pl.ds(block, wide, stride=blocks), :] = summed[:, cols]
            out_ref[pl.ds(wide * blocks + block, SIGNALS - wide, stride=blocks), :] = rest[:, cols]


def band_kernel(phase_ref, axis_ref, weight_ref, knot_ref, out_ref, tiled, powers_ref, moments):
    tiles, shards = phase_ref.shape[0], out_ref.shape[0] // 24
    rep = tiles // shards
    by_tile(axis_ref, tiled)
    rows = moments.shape[0] // shards
    lefts_of = patterns([PAIRS[q % 6][0] for q in range(24)])
    rights_of = patterns([PAIRS[q % 6][1] for q in range(24)])
    powers_of = patterns([q // 6 if q < 42 else 0 for q in range(rows)])
    def dense(start):
        at = pl.ds(start, SUB)
        u = phase_ref[at, :]
        r = 1.0 - u
        u2, r2 = u * u, r * r
        u3, r3 = u2 * u, r2 * r
        w = weight_ref[at, :]
        u3w, r3w = u3 * w, r3 * w
        powers = [r3w * r3, r3w * (r2 * u), r3w * (r * u2), r3w * u3, u3w * (r2 * u), u3w * (r * u2), u3w * u3]
        for p in range(7):
            powers_ref[across(start, p), :] = powers[p]

    def left_of(t):
        axes = tile_of(tiled, t)
        powers = tile_of(powers_ref, t)
        products = [pick_rows(axes, x) * pick_rows(axes, y) for x, y in zip(lefts_of, rights_of)]
        return stacked_parts([products[i % 3] * pick_rows(powers, p) for i, p in enumerate(powers_of)], split2)

    def group(start, steps):
        for part in range(steps // SUB):
            dense(start + part * SUB)
            add_blocks(moments, start + part * SUB, SUB, rep, rows, 2, left_of, knot_ref)

    if rep > SUB:
        moments[...] = jnp.zeros_like(moments)
    over_steps(tiles, group)
    table = bernstein_products()
    for n in range(6):
        parts = [moments[pl.ds(p * 6 + n, shards, stride=rows), :] for p in range(7)]

        def product(i, j):
            return sum(c * part for c, part in zip(table[i, j], parts) if c)

        for delta in range(4):
            running = product(3 - delta, 3)
            for j in reversed(range(3 - delta)):
                running = product(j, j + delta) + shift_up(running, 1)
            to = (delta * 6 + n) * shards
            out_ref[to : to + shards, :] = running


def halo_rows():
    return 1 + (QUANTITIES - 3) // SUB


def slots_of(value, shift):
    return pltpu.roll(value, shift, 1, stride=WINDOW, stride_axis=0)


def pack(source_ref, first, count, row, message_ref):
    parts, shards = message_ref.shape[0], source_ref.shape[0] // count
    owned = shards // parts
    lane, slot = iota((SUB, LANES), 1), iota((SUB, LANES), 0)
    mine = (lane >= WINDOW * slot) & (lane < WINDOW * (slot + 1)) & (slot < count)
    zero = jnp.zeros((SUB, LANES), f32)
    for base in range(0, count, SUB):
        for q in range(base, min(base + SUB, count)):
            for p in range(parts):
                at = q * shards + p * owned
                to = (first + q) * owned
                message_ref[p, to : to + owned, :] = source_ref[at : at + owned, :]
        for p in range(parts):
            taken = min(count, SUB)

            def edge(r):
                got = source_ref[pl.ds(base * shards + r, taken, stride=shards), :]
                return got if taken == SUB else jnp.concatenate([got, zero[taken:]], 0)

            after = edge((p + 1) * owned) if p < parts - 1 else zero
            before = edge(p * owned - 1) if p else zero
            packed = slots_of(jnp.where(lane < LANES // 2, after, before), REACH)
            to = QUANTITIES * owned + row + base // SUB
            message_ref[p, to : to + 1, :] = jnp.sum(jnp.where(mine, packed, 0.0), 0, keepdims=True)


def resid_kernel(
    mine_ref, other_ref, band_ref, live_ref, design_ref, obs_ref, weight_ref, index_ref, phase_ref, axis_ref, knot_ref,
    params_ref, resid_ref, message_ref, tiled, tiled_axis, splines_ref, moments, solved_ref, rhs_ref,
):
    tiles, shards = obs_ref.shape[0], rhs_ref.shape[0] // 3
    rep = tiles // shards
    by_tile(design_ref, tiled)
    by_tile(axis_ref, tiled_axis)
    blocks = SRC_DEV // LANES
    at = [slice(q * blocks, (q + 1) * blocks) for q in range(SIGNALS)]
    solved = solve_small([mine_ref[rows, :] + other_ref[rows, :] for rows in at])
    for m in range(5):
        solved_ref[m] = solved[m]
        for b in range(blocks):
            params_ref[m : m + 1, b * LANES : (b + 1) * LANES] = solved[m][b : b + 1, :]
    rows = moments.shape[0] // shards
    axes_of = patterns([q % 3 for q in range(rows)])
    splines_of = patterns([min(q // 3, 3) for q in range(rows)])

    def left_of(t):
        axes = tile_of(tiled_axis, t)
        splines = tile_of(splines_ref, t)
        return stacked_parts([pick_rows(axes, x) * pick_rows(splines, j) for x, j in zip(axes_of, splines_of)], split3)

    def group(start, steps):
        for part in range(steps // SUB):
            at = pl.ds(start + part * SUB, SUB)
            live = live_ref[at, :]
            block_of, lane_of = low_bits(index_ref[at, :], LANES)
            hits = [block_of == b for b in range(blocks)]
            left = obs_ref[at, :]
            for m in range(5):
                for b in range(blocks):
                    table = jnp.broadcast_to(solved_ref[m, b : b + 1, :], (SUB, LANES))
                    found = jnp.take_along_axis(table, lane_of, axis=1)
                    picked = jnp.where(hits[b], found, picked) if b else found
                left = left - tiled[across(start + part * SUB, m), :] * picked
            resid = live * left
            resid_ref[at, :] = resid
            scaled = weight_ref[at, :] * resid
            for j, basis in enumerate(spline_basis(phase_ref[at, :])):
                splines_ref[across(start + part * SUB, j), :] = basis * scaled
            add_blocks(moments, start + part * SUB, SUB, rep, rows, 3, left_of, knot_ref)

    if rep > SUB:
        moments[...] = jnp.zeros_like(moments)
    over_steps(tiles, group)
    for x in range(3):
        running = moments[pl.ds(9 + x, shards, stride=rows), :]
        for j in reversed(range(3)):
            running = moments[pl.ds(j * 3 + x, shards, stride=rows), :] + shift_up(running, 1)
        rhs_ref[x * shards : (x + 1) * shards, :] = running
    pack(rhs_ref, 0, 3, 0, message_ref)
    pack(band_ref, 3, QUANTITIES - 3, 1, message_ref)


def part_bits():
    place = lax.axis_index("src")
    upper = lax.axis_index("ccd")
    for shift in range(lax.axis_size("src").bit_length() - 1):
        upper = upper ^ ((place >> shift) & 1)
    return [upper, place & 1]


def solve_kernel(parts, sums_ref, out_ref, edges_ref):
    owned = out_ref.shape[0] // 4
    ring = -(-(owned + 2) // SUB) * SUB
    order = {pair: n for n, pair in enumerate(PAIRS)}
    row, lane = iota((ring, LANES), 0), iota((ring, LANES), 1)
    inside = row < owned
    after = (row == owned) & (lane < REACH)
    before = (row == ring - 1) & (lane >= LANES - REACH)
    part = 0 if parts == 1 else sum(bit << i for i, bit in enumerate(reversed(part_bits())))
    edge = (part == parts - 1) * jnp.ones((), jnp.int32)
    known = jnp.where(after & (jnp.full((ring, LANES), edge, jnp.int32) == 1), 0.0, 1.0)

    back = LANES - REACH - WINDOW * (SUB - 1)
    for i in range(halo_rows()):
        packed = sums_ref[QUANTITIES * owned + i : QUANTITIES * owned + i + 1, :]
        edges_ref[i * SUB : (i + 1) * SUB, :] = slots_of(jnp.broadcast_to(packed, (SUB, LANES)), back)

    def load(q):
        rows = sums_ref[q * owned : (q + 1) * owned, :]
        place = q if q < 3 else q + SUB - 3
        slot = place // SUB * SUB + SUB - 1 - place % SUB
        rest = jnp.broadcast_to(edges_ref[slot : slot + 1, :], (ring - owned, LANES))
        return jnp.where(inside | after | before, jnp.concatenate([rows, rest], 0), 0.0)

    def turn(value, n):
        turned = pltpu.roll(value, n % LANES, 1)
        if n > 0:
            return jnp.where(lane < n, pltpu.roll(turned, 1, 0), turned)
        return jnp.where(lane >= LANES + n, pltpu.roll(turned, ring - 1, 0), turned)

    loaded = [load(q) for q in range(QUANTITIES)]

    def band(delta, x, y):
        return loaded[3 + delta * 6 + order[min(x, y), max(x, y)]]

    rhs = loaded[:3]
    scale = [relax_step / (att_ridge + band(0, x, x)) * known for x in range(3)]
    coefs = [rhs[x] * scale[x] for x in range(3)]
    for _ in range(1, ITERS):
        ahead = {(y, delta): turn(coefs[y], -delta) for y in range(3) for delta in range(1, 4)}
        fresh = []
        for x in range(3):
            normal = att_ridge * coefs[x]
            for y in range(3):
                normal = normal + band(0, x, y) * coefs[y]
            for delta in range(1, 4):
                for y in range(3):
                    normal = normal + band(delta, x, y) * ahead[y, delta]
                normal = normal + turn(sum(band(delta, x, y) * coefs[y] for y in range(3)), delta)
            fresh.append(coefs[x] + scale[x] * (rhs[x] - normal))
        coefs = fresh
    for x in range(3):
        for r in range(owned):
            out_ref[pl.ds(r * 4 + x, 1), :] = coefs[x][r : r + 1]


def prepare_kernel(_, live_ref, phase_ref, axis_ref, out_ref, tiled):
    by_tile(axis_ref, tiled)

    def group(start, steps):
        for part in range(steps // SUB):
            at = pl.ds(start + part * SUB, SUB)
            basis = [b * live_ref[at, :] for b in spline_basis(phase_ref[at, :])]
            for x in range(3):
                along = tiled[across(start + part * SUB, x), :]
                for j in range(4):
                    out_ref[x * 4 + j, at, :] = along * basis[j]

    over_steps(phase_ref.shape[0], group)


def predict_kernel(coef_ref, factor_ref, resid_ref, knot_ref, att_ref, out_ref, windows):
    tiles, shards = resid_ref.shape[0], coef_ref.shape[0] // 4
    rep = tiles // shards
    for x in range(3):
        coefs = coef_ref[pl.ds(x, shards, stride=4), :]
        for j in range(4):
            windows[x * 4 + j] = coefs if j == 0 else shift_down(coefs, j)
        att_ref[x : x + 1, :] = windows[x * 4, pl.ds(lax.axis_index("src"), 1), :]
    row = iota((SUB, LANES), 0)

    def group(start, steps):
        for part in range(steps // SUB):
            at = pl.ds(start + part * SUB, SUB)
            knots = knot_ref[at, :]
            first = (start + part * SUB) // rep
            left = resid_ref[at, :]
            for q in range(12):
                table = jnp.broadcast_to(windows[q, pl.ds(first, 1), :], (SUB, LANES))
                for k in range(1, SUB // rep):
                    later = jnp.broadcast_to(windows[q, pl.ds(first + k, 1), :], (SUB, LANES))
                    table = jnp.where(row >= k * rep, later, table)
                left = left - factor_ref[q, at, :] * jnp.take_along_axis(table, knots, axis=1)
            out_ref[at, :] = left

    over_steps(tiles, group)


BOTH = ("src", "ccd")
SMEM = pl.BlockSpec(memory_space=pltpu.SMEM)
VMEM = pl.BlockSpec(memory_space=pltpu.VMEM)
HBM = pl.BlockSpec(memory_space=pltpu.HBM)


def call(kernel, name, scalars, arrays, outs, scratch, space=VMEM):
    return pl.pallas_call(
        kernel,
        name=name,
        out_shape=outs,
        in_specs=[SMEM] * len(scalars) + [space] * len(arrays),
        out_specs=jax.tree.map(lambda _: VMEM, outs),
        scratch_shapes=scratch,
        compiler_params=pltpu.CompilerParams(vmem_limit_bytes=8 << 20),
    )(*scalars, *arrays)


def swapped(value, axis, bit):
    size = lax.axis_size(axis)
    return lax.ppermute(value, axis, [(i, i ^ bit) for i in range(size)])


def summed_over(value, axis):
    size = lax.axis_size(axis)
    if size & (size - 1):
        return lax.psum(value, axis)
    bit = 1
    while bit < size:
        value = value + swapped(value, axis, bit)
        bit *= 2
    return value


def halved(value, mask, keep):
    pair = value.reshape((2, value.shape[0] // 2) + value.shape[1:])
    kept = lax.dynamic_index_in_dim(pair, keep, 0, False)
    sent = lax.dynamic_index_in_dim(pair, 1 - keep, 0, False)
    return kept + swapped(sent, BOTH, mask)


def doubled(value, mask, keep):
    other = swapped(value, BOTH, mask)
    first = jnp.where(keep == 0, value, other)
    second = jnp.where(keep == 0, other, value)
    return jnp.concatenate([first, second], 0)


def on_device(design, observed, weight, phase_frac, axis_factors, source_index, knot_index, counts):
    row_count = observed.shape[0]
    tiles = row_count // LANES
    shards = lax.axis_size("src")
    obs, w, phase, index, knots = (
        a.reshape(tiles, LANES) for a in (observed, weight, phase_frac, source_index, knot_index)
    )
    tiled = pltpu.VMEM((tiles * SUB, LANES), f32)
    dense = pltpu.VMEM((tiles, LANES), f32)
    blocks = SRC_DEV // LANES
    inputs = (w, index, obs, design, phase, axis_factors, knots)
    moments, live, w, index, obs, design, phase, axis_factors, knots = call(
        source_kernel, "source_sums", [],
        [pltpu.with_memory_space_constraint(a, pltpu.HBM) for a in (counts,) + inputs],
        (jax.ShapeDtypeStruct((SIGNALS * blocks, LANES), f32), jax.ShapeDtypeStruct((tiles, LANES), f32))
        + tuple(jax.ShapeDtypeStruct(a.shape, a.dtype) for a in inputs),
        [
            pltpu.SMEM(counts.shape, jnp.int32), pltpu.SemaphoreType.DMA((8,)), dense, dense,
            pltpu.VMEM((SRC_DEV // LOW * 64, LOW), f32), tiled,
        ],
        HBM,
    )
    band = call(
        band_kernel, "band_sums", [], [phase, axis_factors, w, knots],
        jax.ShapeDtypeStruct((24 * shards, KNOT_DEV), f32),
        [tiled, tiled, pltpu.VMEM((shards * 48, KNOT_DEV), f32)],
    )
    if lax.axis_size("ccd") == 2:
        other = swapped(moments, "ccd", 1)
    else:
        moments = summed_over(moments, "ccd")
        other = jnp.zeros_like(moments)
    fast = lax.axis_size("ccd") == 2 and shards >= 4 and shards & (shards - 1) == 0
    parts = 4 if fast else 1
    owned = shards // parts
    message_rows = -(-(QUANTITIES * owned + halo_rows()) // SUB) * SUB
    params, resid, message = call(
        resid_kernel, "residuals", [],
        [moments, other, band, live, design, obs, w, index, phase, axis_factors, knots],
        (
            jax.ShapeDtypeStruct((5, SRC_DEV), f32),
            jax.ShapeDtypeStruct((tiles, LANES), f32),
            jax.ShapeDtypeStruct((parts, message_rows, LANES), f32),
        ),
        [tiled, tiled, tiled, pltpu.VMEM((shards * 16, KNOT_DEV), f32), pltpu.VMEM((5, blocks, LANES), f32),
         pltpu.VMEM((3 * shards, KNOT_DEV), f32)],
    )
    factors = call(
        prepare_kernel, "prepare", [], [message, live, phase, axis_factors],
        jax.ShapeDtypeStruct((12, tiles, LANES), f32), [tiled],
    )
    if fast:
        upper, lower = part_bits()
        sums = halved(halved(message, 1, upper), 3, lower)[0]
        bit = shards // 2
        while bit > 1:
            sums = sums + swapped(sums, BOTH, 2 * bit + 1)
            bit //= 2
    else:
        sums = summed_over(summed_over(message[0], "ccd"), "src")
    coefs = call(
        functools.partial(solve_kernel, parts), "attitude", [], [sums],
        jax.ShapeDtypeStruct((owned * 4, LANES), f32), [pltpu.VMEM((halo_rows() * SUB, LANES), f32)],
    )
    if fast:
        coefs = doubled(doubled(coefs, 3, lower), 1, upper)
    attitude, residual = call(
        predict_kernel, "predict", [], [coefs, factors, resid, knots],
        (jax.ShapeDtypeStruct((3, KNOT_DEV), f32), jax.ShapeDtypeStruct((tiles, LANES), f32)),
        [pltpu.VMEM((12, shards, KNOT_DEV), f32)],
    )
    return params, attitude, residual.reshape(row_count)


def solution(mesh):
    rows = P(("src", "ccd"))
    wide = P(None, ("src", "ccd"))
    in_specs = (wide, rows, rows, rows, wide, rows, rows, P("src", "ccd", None))
    out_specs = (P(None, "src"), P(None, "src"), rows)
    return jax.shard_map(on_device, mesh=mesh, in_specs=in_specs, out_specs=out_specs, check_vma=False)
```

```python
import functools
import math

import jax
import jax.numpy as jnp
from jax import lax
from jax.experimental import pallas as pl
from jax.experimental.pallas import tpu as pltpu
from jax.sharding import PartitionSpec as P

SRC_DEV = 1024
KNOT_DEV = 128
ITERS = 3
LANES = 128
SUB = 8
LOW = 256
QUANTITIES = 3 + 4 * 6
REACH = 3 * (ITERS - 1)
WINDOW = 2 * REACH
CUBICS = [(1.0, 0.0, 0.0, 0.0), (4.0, 12.0, 6.0, 1.0), (1.0, 6.0, 12.0, 4.0), (0.0, 0.0, 0.0, 1.0)]
SIGNALS = 15 + 5
PAIRS = [(x, y) for x in range(3) for y in range(x, 3)]

src_ridge = 1.0
att_ridge = 1.0
relax_step = 0.15

f32 = jnp.float32
bf16 = jnp.bfloat16


def bernstein_products():
    table = {}
    for i in range(4):
        for j in range(i, 4):
            coefs = [0.0] * 7
            for p in range(4):
                for q in range(4):
                    coefs[p + q] += CUBICS[i][p] * CUBICS[j][q] / 36.0
            table[i, j] = coefs
    return table


def split2(value):
    high = value.astype(bf16).astype(f32)
    return [high, value - high]


def split3(value):
    high = value.astype(bf16).astype(f32)
    rest = value - high
    middle = rest.astype(bf16).astype(f32)
    return [high, middle, rest - middle]


def spline_basis(phase_rows):
    remain = 1.0 - phase_rows
    square = phase_rows * phase_rows
    cube_term = square * phase_rows
    return [
        remain * remain * remain / 6.0,
        (3.0 * cube_term - 6.0 * square + 4.0) / 6.0,
        (-3.0 * cube_term + 3.0 * square + 3.0 * phase_rows + 1.0) / 6.0,
        cube_term / 6.0,
    ]


def solve_small(moments):
    matrix = {}
    position = 0
    for m in range(5):
        for n in range(m, 5):
            matrix[m, n] = moments[position] + (src_ridge if m == n else 0.0)
            position += 1
    scaled, factor, inverse = {}, {}, {}
    for j in range(5):
        for i in range(j, 5):
            running = matrix[j, i]
            for k in range(j):
                running = running - scaled[i, k] * factor[j, k]
            scaled[i, j] = running
        inverse[j] = 1.0 / scaled[j, j]
        for i in range(j + 1, 5):
            factor[i, j] = scaled[i, j] * inverse[j]
    forward = []
    for i in range(5):
        running = moments[15 + i]
        for k in range(i):
            running = running - factor[i, k] * forward[k]
        forward.append(running)
    solved = [None] * 5
    for i in reversed(range(5)):
        running = forward[i] * inverse[i]
        for k in range(i + 1, 5):
            running = running - factor[k, i] * solved[k]
        solved[i] = running
    return solved


def iota(shape, axis):
    return lax.broadcasted_iota(jnp.int32, shape, axis)


def over_steps(tiles, body):
    steps = math.gcd(tiles, 64)
    if steps == tiles:
        body(0, steps)
        return

    def one(g, _):
        body(pl.multiple_of(g * steps, steps), steps)
        return 0

    lax.fori_loop(0, tiles // steps, one, 0)


def spread_row(index_row, count):
    packed = jnp.broadcast_to(index_row, (2 * SUB, LANES)).astype(bf16)
    return jnp.concatenate([packed] * (count // (2 * SUB)), 0)


def is_equal(left, right):
    return jnp.where(left == right, jnp.ones((), bf16), jnp.zeros((), bf16))


def onehot(index_row, count):
    return is_equal(iota((count, LANES), 0).astype(f32).astype(bf16), spread_row(index_row, count))


def by_tile(wide_ref, tiled_ref):
    rows = wide_ref.shape[0]
    for t in range(tiled_ref.shape[0] // SUB):
        tiled_ref[t * SUB : t * SUB + rows, :] = wide_ref[:, t * LANES : (t + 1) * LANES]


def by_group(tiles):
    return range(0, tiles, SUB)


def across(start, row):
    return pl.ds(start * SUB + row, SUB, stride=SUB)


def tile_of(tiled_ref, t):
    return tiled_ref[pl.ds(t * SUB, SUB), :]


def low_bits(index, size):
    return index >> (size.bit_length() - 1), index & (size - 1)


def row_of(ref, t):
    return jnp.broadcast_to(ref[pl.ds(t, 1), :], (SUB, LANES))


def per_sublane(values, kind):
    row = iota((SUB, LANES), 0)
    out = jnp.full((SUB, LANES), values[0], kind)
    for s in range(1, SUB):
        if values[s] != values[0]:
            out = jnp.where(row == s, jnp.full((SUB, LANES), values[s], kind), out)
    return out


def pick_rows(value, pattern):
    return jnp.take_along_axis(value, pattern, axis=0)


def patterns(values):
    values = list(values) + [0] * (-len(values) % SUB)
    return [per_sublane(values[i : i + SUB], jnp.int32) for i in range(0, len(values), SUB)]


def stacked_parts(values, split):
    parts = split(jnp.concatenate(values, 0))
    if len(parts) * parts[0].shape[0] % (2 * SUB):
        parts.append(jnp.zeros((SUB, LANES), f32))
    return jnp.concatenate(parts, 0).astype(bf16)


def sum_parts(value, rows, count):
    return sum(value[i * rows : (i + 1) * rows] for i in range(count))


def add_blocks(moments_ref, start, steps, rep, rows, count, left_of, knot_ref):
    per_block = min(rep, steps)
    for b in range(steps // per_block):
        lefts, rights = [], []
        for i in range(b * per_block, (b + 1) * per_block):
            lefts.append(left_of(start + i))
            rights.append(onehot(knot_ref[pl.ds(start + i, 1), :].astype(f32), KNOT_DEV))
        got = contract(jnp.concatenate(lefts, 1), jnp.concatenate(rights, 1))
        summed = sum_parts(got, rows, count)
        where_to = (start + b * per_block) // rep
        where_to = pl.ds(where_to * rows, rows)
        if rep <= steps:
            moments_ref[where_to, :] = summed
        else:
            moments_ref[where_to, :] += summed


def contract(left, right):
    return lax.dot_general(left, right, (((1,), (1,)), ((), ())), preferred_element_type=f32)


def shift_up(value, n):
    turned = pltpu.roll(value, n, 1)
    before = pltpu.roll(turned, 1, 0)
    before = jnp.where(iota(value.shape, 0) == 0, 0.0, before)
    return jnp.where(iota(value.shape, 1) < n, before, turned)


def shift_down(value, n):
    turned = pltpu.roll(value, LANES - n, 1)
    after = pltpu.roll(turned, value.shape[0] - 1, 0)
    after = jnp.where(iota(value.shape, 0) == value.shape[0] - 1, 0.0, after)
    return jnp.where(iota(value.shape, 1) >= LANES - n, after, turned)


def source_kernel(
    counts_hbm, weight_hbm, index_hbm, obs_hbm, design_hbm, phase_hbm, axis_hbm, knot_hbm,
    out_ref, live_ref, weight_ref, index_ref, obs_ref, design_ref, phase_ref, axis_ref, knot_ref,
    counts_ref, sems, low_ref, high_ref, total, tiled,
):
    tiles = obs_ref.shape[0]
    shards = counts_ref.shape[2]
    rep = tiles // shards
    copies = [
        pltpu.make_async_copy(src, dst, sems.at[i])
        for i, (src, dst) in enumerate(
            [(counts_hbm, counts_ref), (weight_hbm, weight_ref), (index_hbm, index_ref), (obs_hbm, obs_ref),
             (design_hbm, design_ref), (phase_hbm, phase_ref), (axis_hbm, axis_ref), (knot_hbm, knot_ref)]
        )
    ]
    for copy in copies:
        copy.start()
    if math.gcd(tiles, 64) != tiles:
        total[...] = jnp.zeros_like(total)
    highs = SRC_DEV // LOW
    pairs = [(m, n) for m in range(5) for n in range(m, 5)] + [(m, 5) for m in range(5)]
    pairs += pairs[2 * SUB :]
    lefts_of = patterns([m for m, _ in pairs])
    rights_of = patterns([n for _, n in pairs])
    first_half = iota((SUB, LANES), 0) < SUB // 2
    copies[0].wait()
    slots = iota((rep, LANES), 0) * LANES + iota((rep, LANES), 1)
    for d in range(shards):
        live_ref[pl.ds(d * rep, rep), :] = (slots < counts_ref[0, 0, d]).astype(f32)
    copies[1].wait()
    copies[2].wait()
    for start in by_group(tiles):
        at = pl.ds(start, SUB)
        weight_ref[at, :] = weight_ref[at, :] * live_ref[at, :]
        high, low = low_bits(index_ref[at, :], LOW)
        high_ref[at, :] = high.astype(f32)
        low_ref[at, :] = low.astype(f32)
    copies[3].wait()
    copies[4].wait()
    by_tile(design_ref, tiled)
    for start in by_group(tiles):
        tiled[across(start, 5), :] = obs_ref[pl.ds(start, SUB), :]

    def group(start, steps):
        lefts, rights = [], []
        for i in range(steps):
            t = start + i
            values = tile_of(tiled, t)
            scaled = values * row_of(weight_ref, t)
            products = [pick_rows(scaled, m) * pick_rows(values, n) for m, n in zip(lefts_of, rights_of)]
            high, middle, low = split3(products[2])
            parts = split3(jnp.concatenate(products[:2], 0)) + [jnp.where(first_half, high, middle), low]
            block = jnp.concatenate(parts, 0).astype(bf16)
            packed = spread_row(high_ref[pl.ds(t, 1), :], 2 * SUB)
            masks = [is_equal(packed, jnp.full((), h, bf16)) for h in range(highs)]
            repeats = block.shape[0] // (2 * SUB)
            lefts.append(jnp.concatenate([block * jnp.concatenate([mask] * repeats, 0) for mask in masks], 0))
            rights.append(onehot(low_ref[pl.ds(t, 1), :], LOW))
        got = contract(jnp.concatenate(lefts, 1), jnp.concatenate(rights, 1))
        if steps == tiles:
            total[...] = got
        else:
            total[...] += got

    over_steps(tiles, group)
    for copy in copies[5:]:
        copy.wait()
    height = total.shape[0] // highs
    wide, half_tile = 2 * SUB, SUB // 2
    for h in range(highs):
        block = total[h * height : (h + 1) * height, :]
        tail = block[3 * wide :]
        summed = sum_parts(block, wide, 3)
        rest = tail[0:half_tile] + tail[half_tile : 2 * half_tile] + tail[2 * half_tile : 3 * half_tile]
        for half in range(LOW // LANES):
            cols = slice(half * LANES, (half + 1) * LANES)
            out_ref[0:wide, h * (LOW // LANES) + half, :] = summed[:, cols]
            out_ref[wide:SIGNALS, h * (LOW // LANES) + half, :] = rest[:, cols]


def band_kernel(phase_ref, axis_ref, weight_ref, knot_ref, out_ref, tiled, powers_ref, moments):
    tiles, shards = phase_ref.shape[0], out_ref.shape[0] // 24
    rep = tiles // shards
    by_tile(axis_ref, tiled)
    rows = moments.shape[0] // shards
    lefts_of = patterns([PAIRS[q % 6][0] for q in range(24)])
    rights_of = patterns([PAIRS[q % 6][1] for q in range(24)])
    powers_of = patterns([q // 6 if q < 42 else 0 for q in range(rows)])
    for start in by_group(tiles):
        at = pl.ds(start, SUB)
        u = phase_ref[at, :]
        r = 1.0 - u
        u2, r2 = u * u, r * r
        u3, r3 = u2 * u, r2 * r
        w = weight_ref[at, :]
        u3w, r3w = u3 * w, r3 * w
        powers = [r3w * r3, r3w * (r2 * u), r3w * (r * u2), r3w * u3, u3w * (r2 * u), u3w * (r * u2), u3w * u3]
        for p in range(7):
            powers_ref[across(start, p), :] = powers[p]

    def left_of(t):
        axes = tile_of(tiled, t)
        powers = tile_of(powers_ref, t)
        products = [pick_rows(axes, x) * pick_rows(axes, y) for x, y in zip(lefts_of, rights_of)]
        return stacked_parts([products[i % 3] * pick_rows(powers, p) for i, p in enumerate(powers_of)], split2)

    def group(start, steps):
        add_blocks(moments, start, steps, rep, rows, 2, left_of, knot_ref)

    if rep > math.gcd(tiles, 64):
        moments[...] = jnp.zeros_like(moments)
    over_steps(tiles, group)
    table = bernstein_products()
    for n in range(6):
        parts = [moments[pl.ds(p * 6 + n, shards, stride=rows), :] for p in range(7)]

        def product(i, j):
            return sum(c * part for c, part in zip(table[i, j], parts) if c)

        for delta in range(4):
            running = product(3 - delta, 3)
            for j in reversed(range(3 - delta)):
                running = product(j, j + delta) + shift_up(running, 1)
            to = (delta * 6 + n) * shards
            out_ref[to : to + shards, :] = running


def halo_rows():
    return 1 + (QUANTITIES - 3) // SUB


def slots_of(value, shift):
    return pltpu.roll(value, shift, 1, stride=WINDOW, stride_axis=0)


def pack(source_ref, first, count, row, message_ref):
    parts, shards = message_ref.shape[0], source_ref.shape[0] // count
    owned = shards // parts
    lane, slot = iota((SUB, LANES), 1), iota((SUB, LANES), 0)
    mine = (lane >= WINDOW * slot) & (lane < WINDOW * (slot + 1)) & (slot < count)
    zero = jnp.zeros((SUB, LANES), f32)
    for base in range(0, count, SUB):
        for q in range(base, min(base + SUB, count)):
            for p in range(parts):
                at = q * shards + p * owned
                to = (first + q) * owned
                message_ref[p, to : to + owned, :] = source_ref[at : at + owned, :]
        for p in range(parts):
            taken = min(count, SUB)

            def edge(r):
                got = source_ref[pl.ds(base * shards + r, taken, stride=shards), :]
                return got if taken == SUB else jnp.concatenate([got, zero[taken:]], 0)

            after = edge((p + 1) * owned) if p < parts - 1 else zero
            before = edge(p * owned - 1) if p else zero
            packed = slots_of(jnp.where(lane < LANES // 2, after, before), REACH)
            to = QUANTITIES * owned + row + base // SUB
            message_ref[p, to : to + 1, :] = jnp.sum(jnp.where(mine, packed, 0.0), 0, keepdims=True)


def resid_kernel(
    mine_ref, other_ref, band_ref, live_ref, design_ref, obs_ref, weight_ref, index_ref, phase_ref, axis_ref, knot_ref,
    params_ref, resid_ref, message_ref, tiled, tiled_axis, splines_ref, moments, solved_ref, rhs_ref,
):
    tiles, shards = obs_ref.shape[0], rhs_ref.shape[0] // 3
    rep = tiles // shards
    by_tile(design_ref, tiled)
    by_tile(axis_ref, tiled_axis)
    solved = solve_small([mine_ref[q] + other_ref[q] for q in range(SIGNALS)])
    blocks = SRC_DEV // LANES
    for m in range(5):
        solved_ref[m] = solved[m]
        for b in range(blocks):
            params_ref[m : m + 1, b * LANES : (b + 1) * LANES] = solved[m][b : b + 1, :]
    rows = moments.shape[0] // shards
    axes_of = patterns([q % 3 for q in range(rows)])
    splines_of = patterns([min(q // 3, 3) for q in range(rows)])

    def left_of(t):
        axes = tile_of(tiled_axis, t)
        splines = tile_of(splines_ref, t)
        return stacked_parts([pick_rows(axes, x) * pick_rows(splines, j) for x, j in zip(axes_of, splines_of)], split2)

    def group(start, steps):
        for part in range(steps // SUB):
            at = pl.ds(start + part * SUB, SUB)
            live = live_ref[at, :]
            block_of, lane_of = low_bits(index_ref[at, :], LANES)
            hits = [block_of == b for b in range(blocks)]
            left = obs_ref[at, :]
            for m in range(5):
                for b in range(blocks):
                    table = jnp.broadcast_to(solved_ref[m, b : b + 1, :], (SUB, LANES))
                    found = jnp.take_along_axis(table, lane_of, axis=1)
                    picked = jnp.where(hits[b], found, picked) if b else found
                left = left - tiled[across(start + part * SUB, m), :] * picked
            resid = live * left
            resid_ref[at, :] = resid
            scaled = weight_ref[at, :] * resid
            for j, basis in enumerate(spline_basis(phase_ref[at, :])):
                splines_ref[across(start + part * SUB, j), :] = basis * scaled
        add_blocks(moments, start, steps, rep, rows, 2, left_of, knot_ref)

    if rep > math.gcd(tiles, 64):
        moments[...] = jnp.zeros_like(moments)
    over_steps(tiles, group)
    for x in range(3):
        running = moments[pl.ds(9 + x, shards, stride=rows), :]
        for j in reversed(range(3)):
            running = moments[pl.ds(j * 3 + x, shards, stride=rows), :] + shift_up(running, 1)
        rhs_ref[x * shards : (x + 1) * shards, :] = running
    pack(rhs_ref, 0, 3, 0, message_ref)
    pack(band_ref, 3, QUANTITIES - 3, 1, message_ref)


def part_bits():
    place = lax.axis_index("src")
    upper = lax.axis_index("ccd")
    for shift in range(lax.axis_size("src").bit_length() - 1):
        upper = upper ^ ((place >> shift) & 1)
    return [upper, place & 1]


def solve_kernel(parts, sums_ref, out_ref, edges_ref):
    owned = out_ref.shape[0] // 4
    ring = -(-(owned + 2) // SUB) * SUB
    order = {pair: n for n, pair in enumerate(PAIRS)}
    row, lane = iota((ring, LANES), 0), iota((ring, LANES), 1)
    inside = row < owned
    after = (row == owned) & (lane < REACH)
    before = (row == ring - 1) & (lane >= LANES - REACH)
    part = 0 if parts == 1 else sum(bit << i for i, bit in enumerate(reversed(part_bits())))
    edge = (part == parts - 1) * jnp.ones((), jnp.int32)
    known = jnp.where(after & (jnp.full((ring, LANES), edge, jnp.int32) == 1), 0.0, 1.0)

    back = LANES - REACH - WINDOW * (SUB - 1)
    for i in range(halo_rows()):
        packed = sums_ref[QUANTITIES * owned + i : QUANTITIES * owned + i + 1, :]
        edges_ref[i * SUB : (i + 1) * SUB, :] = slots_of(jnp.broadcast_to(packed, (SUB, LANES)), back)

    def load(q):
        rows = sums_ref[q * owned : (q + 1) * owned, :]
        place = q if q < 3 else q + SUB - 3
        slot = place // SUB * SUB + SUB - 1 - place % SUB
        rest = jnp.broadcast_to(edges_ref[slot : slot + 1, :], (ring - owned, LANES))
        return jnp.where(inside | after | before, jnp.concatenate([rows, rest], 0), 0.0)

    def turn(value, n):
        turned = pltpu.roll(value, n % LANES, 1)
        if n > 0:
            return jnp.where(lane < n, pltpu.roll(turned, 1, 0), turned)
        return jnp.where(lane >= LANES + n, pltpu.roll(turned, ring - 1, 0), turned)

    loaded = [load(q) for q in range(QUANTITIES)]

    def band(delta, x, y):
        return loaded[3 + delta * 6 + order[min(x, y), max(x, y)]]

    rhs = loaded[:3]
    scale = [relax_step / (att_ridge + band(0, x, x)) * known for x in range(3)]
    coefs = [rhs[x] * scale[x] for x in range(3)]
    for _ in range(1, ITERS):
        ahead = {(y, delta): turn(coefs[y], -delta) for y in range(3) for delta in range(1, 4)}
        fresh = []
        for x in range(3):
            normal = att_ridge * coefs[x]
            for y in range(3):
                normal = normal + band(0, x, y) * coefs[y]
            for delta in range(1, 4):
                for y in range(3):
                    normal = normal + band(delta, x, y) * ahead[y, delta]
                normal = normal + turn(sum(band(delta, x, y) * coefs[y] for y in range(3)), delta)
            fresh.append(coefs[x] + scale[x] * (rhs[x] - normal))
        coefs = fresh
    for x in range(3):
        for r in range(owned):
            out_ref[pl.ds(r * 4 + x, 1), :] = coefs[x][r : r + 1]


def prepare_kernel(_, live_ref, phase_ref, axis_ref, out_ref, tiled):
    by_tile(axis_ref, tiled)

    def group(start, steps):
        for part in range(steps // SUB):
            at = pl.ds(start + part * SUB, SUB)
            basis = [b * live_ref[at, :] for b in spline_basis(phase_ref[at, :])]
            for x in range(3):
                along = tiled[across(start + part * SUB, x), :]
                for j in range(4):
                    out_ref[x * 4 + j, at, :] = along * basis[j]

    over_steps(phase_ref.shape[0], group)


def predict_kernel(coef_ref, factor_ref, resid_ref, knot_ref, att_ref, out_ref, windows):
    tiles, shards = resid_ref.shape[0], coef_ref.shape[0]
    rep = tiles // shards
    for x in range(3):
        coefs = coef_ref[:, x, :]
        for j in range(4):
            windows[x * 4 + j] = coefs if j == 0 else shift_down(coefs, j)
        att_ref[x : x + 1, :] = windows[x * 4, pl.ds(lax.axis_index("src"), 1), :]
    row = iota((SUB, LANES), 0)

    def group(start, steps):
        for part in range(steps // SUB):
            at = pl.ds(start + part * SUB, SUB)
            knots = knot_ref[at, :]
            first = (start + part * SUB) // rep
            left = resid_ref[at, :]
            for q in range(12):
                table = jnp.broadcast_to(windows[q, pl.ds(first, 1), :], (SUB, LANES))
                for k in range(1, SUB // rep):
                    later = jnp.broadcast_to(windows[q, pl.ds(first + k, 1), :], (SUB, LANES))
                    table = jnp.where(row >= k * rep, later, table)
                left = left - factor_ref[q, at, :] * jnp.take_along_axis(table, knots, axis=1)
            out_ref[at, :] = left

    over_steps(tiles, group)


BOTH = ("src", "ccd")
SMEM = pl.BlockSpec(memory_space=pltpu.SMEM)
VMEM = pl.BlockSpec(memory_space=pltpu.VMEM)
HBM = pl.BlockSpec(memory_space=pltpu.HBM)


def call(kernel, name, scalars, arrays, outs, scratch, space=VMEM):
    return pl.pallas_call(
        kernel,
        name=name,
        out_shape=outs,
        in_specs=[SMEM] * len(scalars) + [space] * len(arrays),
        out_specs=jax.tree.map(lambda _: VMEM, outs),
        scratch_shapes=scratch,
        compiler_params=pltpu.CompilerParams(vmem_limit_bytes=8 << 20),
    )(*scalars, *arrays)


def swapped(value, axis, bit):
    size = lax.axis_size(axis)
    return lax.ppermute(value, axis, [(i, i ^ bit) for i in range(size)])


def summed_over(value, axis):
    size = lax.axis_size(axis)
    if size & (size - 1):
        return lax.psum(value, axis)
    bit = 1
    while bit < size:
        value = value + swapped(value, axis, bit)
        bit *= 2
    return value


def halved(value, mask, keep):
    pair = value.reshape((2, value.shape[0] // 2) + value.shape[1:])
    kept = lax.dynamic_index_in_dim(pair, keep, 0, False)
    sent = lax.dynamic_index_in_dim(pair, 1 - keep, 0, False)
    return kept + swapped(sent, BOTH, mask)


def doubled(value, mask, keep):
    other = swapped(value, BOTH, mask)
    first = jnp.where(keep == 0, value, other)
    second = jnp.where(keep == 0, other, value)
    return jnp.concatenate([first, second], 0)


def on_device(design, observed, weight, phase_frac, axis_factors, source_index, knot_index, counts):
    row_count = observed.shape[0]
    tiles = row_count // LANES
    shards = lax.axis_size("src")
    obs, w, phase, index, knots = (
        a.reshape(tiles, LANES) for a in (observed, weight, phase_frac, source_index, knot_index)
    )
    tiled = pltpu.VMEM((tiles * SUB, LANES), f32)
    dense = pltpu.VMEM((tiles, LANES), f32)
    blocks = SRC_DEV // LANES
    inputs = (w, index, obs, design, phase, axis_factors, knots)
    moments, live, w, index, obs, design, phase, axis_factors, knots = call(
        source_kernel, "source_sums", [],
        [pltpu.with_memory_space_constraint(a, pltpu.HBM) for a in (counts,) + inputs],
        (jax.ShapeDtypeStruct((SIGNALS, blocks, LANES), f32), jax.ShapeDtypeStruct((tiles, LANES), f32))
        + tuple(jax.ShapeDtypeStruct(a.shape, a.dtype) for a in inputs),
        [
            pltpu.SMEM(counts.shape, jnp.int32), pltpu.SemaphoreType.DMA((8,)), dense, dense,
            pltpu.VMEM((SRC_DEV // LOW * 64, LOW), f32), tiled,
        ],
        HBM,
    )
    band = call(
        band_kernel, "band_sums", [], [phase, axis_factors, w, knots],
        jax.ShapeDtypeStruct((24 * shards, KNOT_DEV), f32),
        [tiled, tiled, pltpu.VMEM((shards * 48, KNOT_DEV), f32)],
    )
    if lax.axis_size("ccd") == 2:
        other = swapped(moments, "ccd", 1)
    else:
        moments = summed_over(moments, "ccd")
        other = jnp.zeros_like(moments)
    fast = lax.axis_size("ccd") == 2 and shards >= 4 and shards & (shards - 1) == 0
    parts = 4 if fast else 1
    owned = shards // parts
    message_rows = -(-(QUANTITIES * owned + halo_rows()) // SUB) * SUB
    params, resid, message = call(
        resid_kernel, "residuals", [],
        [moments, other, band, live, design, obs, w, index, phase, axis_factors, knots],
        (
            jax.ShapeDtypeStruct((5, SRC_DEV), f32),
            jax.ShapeDtypeStruct((tiles, LANES), f32),
            jax.ShapeDtypeStruct((parts, message_rows, LANES), f32),
        ),
        [tiled, tiled, tiled, pltpu.VMEM((shards * 16, KNOT_DEV), f32), pltpu.VMEM((5, blocks, LANES), f32),
         pltpu.VMEM((3 * shards, KNOT_DEV), f32)],
    )
    factors = call(
        prepare_kernel, "prepare", [], [message, live, phase, axis_factors],
        jax.ShapeDtypeStruct((12, tiles, LANES), f32), [tiled],
    )
    if fast:
        upper, lower = part_bits()
        sums = halved(halved(message, 1, upper), 3, lower)[0]
        bit = shards // 2
        while bit > 1:
            sums = sums + swapped(sums, BOTH, 2 * bit + 1)
            bit //= 2
    else:
        sums = summed_over(summed_over(message[0], "ccd"), "src")
    coefs = call(
        functools.partial(solve_kernel, parts), "attitude", [], [sums],
        jax.ShapeDtypeStruct((owned * 4, LANES), f32), [pltpu.VMEM((halo_rows() * SUB, LANES), f32)],
    )
    if fast:
        coefs = doubled(doubled(coefs, 3, lower), 1, upper)
    attitude, residual = call(
        predict_kernel, "predict", [], [coefs.reshape(shards, 4, LANES), factors, resid, knots],
        (jax.ShapeDtypeStruct((3, KNOT_DEV), f32), jax.ShapeDtypeStruct((tiles, LANES), f32)),
        [pltpu.VMEM((12, shards, KNOT_DEV), f32)],
    )
    return params, attitude, residual.reshape(row_count)


def solution(mesh):
    rows = P(("src", "ccd"))
    wide = P(None, ("src", "ccd"))
    in_specs = (wide, rows, rows, rows, wide, rows, rows, P("src", "ccd", None))
    out_specs = (P(None, "src"), P(None, "src"), rows)
    return jax.shard_map(on_device, mesh=mesh, in_specs=in_specs, out_specs=out_specs, check_vma=False)
```
